32 devices in a mesh: groups: 2 (over y), seq: 4 (over x, core), tensor: 4 (over z).
Axes of the slice: x: 2, y: 2, z: 4, core: 2. Of those that a mesh axis runs over, the one named last changes fastest.
Arguments:
- patches: bfloat16 [2056, 1280], P(('groups', 'seq')), parts along dimension 0, may hold values from -6 to 6
- latents: bfloat16 [64, 1280], replicated, may hold values from -160 to 160
- wq_res: bfloat16 [1280, 1536], P(None, 'tensor'), may hold values from -0.15625 to 0.15625
- wk_res: bfloat16 [1280, 1536], P(None, 'tensor'), may hold values from -0.3125 to 0.3125
- wv_res: bfloat16 [1280, 1536], P(None, 'tensor'), may hold values from -0.15625 to 0.15625
- wo_res: bfloat16 [1536, 1280], P('tensor'), may hold values from -0.625 to 0.625
- text: bfloat16 [3072, 8192], P('groups', 'seq'), parts along dimension 0, may hold values from -240 to 240
- norm_gain: bfloat16 [8192], P('seq'), may hold values from 0.25 to 1.75
- wq_x: bfloat16 [8192, 8192], P('seq', 'tensor'), may hold values from -0.0625 to 0.0625
- wk_x: bfloat16 [1280, 8192], P(None, 'tensor'), may hold values from -0.15625 to 0.15625
- wv_x: bfloat16 [1280, 8192], P(None, 'tensor'), may hold values from -0.15625 to 0.15625
- wo_x: bfloat16 [8192, 8192], P('tensor', 'seq'), may hold values from -0.25 to 0.25
- gate_x: float32 [8192], P('seq'), may hold values from -1.5 to 1.5
- text_image: int32 [3072], P('groups'), parts along dimension 0, may hold values from -1 to 3, as said below
Outputs:
- text_out: float32 [3072, 8192], P('groups', 'seq'), parts along dimension 0
- page_latents: bfloat16 [512, 1280], P(('groups', 'seq')), parts along dimension 0
The draws below stay inside these ranges and needn't reach their ends.
There are 2 independent parts, one for each index of `groups`. The reference program is written for one: setup_inputs(seed, part) draws one part's arguments, and reference() takes and returns one part's arrays. A program takes and returns all parts, laid end to end along the dimension named above; an argument that names none is the same for every part. Nothing has to cross between parts.
Inputs may be any that keep to these rules, and one draw needn't show every extreme that they name: text_image[t] is the index of the last image placed at or before token t, -1 before the first image; it never falls along the tokens, and every one of the 4 images is the value of some tokens.
All inputs are finite; a program needn't handle non-finite values.
Results may differ from the reference program's by a relative error of at most 0.015.
The reference program's roundings to bfloat16 on the way count: a program that leaves them out, or rounds other values in their place, can miss the bound.
Values may be sent and summed in bfloat16 or wider, within the bound.
A program may use at most 192 MiB of HBM per device.

```python
import math
import jax
import jax.numpy as jnp
from jax import lax

WIDTH = 8192
HEAD = 128
LATENTS = 64
VIS_WIDTH = 1280
RES_HEADS = 16
RES_HEAD = 96
PATCH_IMG = 257
TEXT = 1536
IMAGES = 4
RES_INNER = 1536
N_TENSOR = 4


def draw_latents(key, part):
    first_key = jax.random.fold_in(key, 0)
    drawn = jnp.clip(jax.random.normal(first_key, (LATENTS, VIS_WIDTH), jnp.float32), -6.0, 6.0)
    return drawn.astype(jnp.bfloat16)


def draw_text(key, part):
    first_key, second_key = jax.random.split(key, 2)
    column = jnp.arange(WIDTH, dtype=jnp.float32) / WIDTH
    ramp = jnp.exp(math.log(3.0) * column)
    rough = jax.random.uniform(second_key, (WIDTH,), jnp.float32, 0.6, 1.5)
    drawn = jnp.clip(jax.random.normal(first_key, (TEXT, WIDTH), jnp.float32), -6.0, 6.0)
    return (drawn * ramp * rough).astype(jnp.bfloat16)


def draw_text_image(key, part):
    lower = max(1, TEXT // (2 * (IMAGES + 1)))
    upper = TEXT // (IMAGES + 1) + 1
    spacing = jax.random.randint(key, (IMAGES,), lower, upper, jnp.int32)
    starts = jnp.cumsum(spacing).astype(jnp.int32)
    positions = jnp.arange(TEXT, dtype=jnp.int32)
    placed = (starts[None, :] <= positions[:, None]).astype(jnp.int32)
    return (jnp.sum(placed, axis=1) - 1).astype(jnp.int32)


def shard_levels(rng, dims, cuts, low, top_value):
    def one(position, blocks):
        heights = jax.random.uniform(jax.random.fold_in(jax.random.fold_in(rng, 6), position), (blocks,), jnp.float32, low / len(cuts), top_value / len(cuts))
        return jnp.repeat(jnp.exp(heights), dims[position] // blocks).reshape((-1,) + (1,) * (len(dims) - position - 1))

    gain = one(*cuts[0])
    for cut in cuts[1:]:
        gain = gain * one(*cut)
    return gain


def bell_draw(rng, dims, deviation, most, cuts=(), kind=jnp.bfloat16):
    values = deviation * jax.random.normal(rng, dims, jnp.float32)
    if cuts:
        values = values * shard_levels(rng, dims, cuts, -0.22, 0.18)
    return jnp.clip(values, -most, most).astype(kind)


def setup_inputs(seed: int = 0, part: int = 0) -> dict:
    keys = jax.random.split(jax.random.key(seed), 15)
    own_keys = jax.random.split(jax.random.fold_in(keys[14], part), 15)
    patches = bell_draw(own_keys[0], (IMAGES * PATCH_IMG, VIS_WIDTH), 1.0, 6.0, ((0, 4),))
    latents = draw_latents(jax.random.fold_in(keys[14], 71), part)
    wq_res = bell_draw(keys[2], (VIS_WIDTH, RES_INNER), VIS_WIDTH ** -0.5, 0.15625, ((1, 4),))
    wk_res = bell_draw(keys[3], (VIS_WIDTH, RES_INNER), (VIS_WIDTH // 4) ** -0.5, 0.3125, ((1, 4),))
    wv_res = bell_draw(keys[4], (VIS_WIDTH, RES_INNER), VIS_WIDTH ** -0.5, 0.15625, ((1, 4),))
    wo_res = bell_draw(keys[5], (RES_INNER, VIS_WIDTH), RES_HEAD ** -0.5, 0.625, ((0, 4),))
    text = draw_text(jax.random.fold_in(jax.random.fold_in(keys[14], part), 71), part)
    norm_gain = jnp.clip(1.0 + 0.15 * jax.random.normal(keys[7], (WIDTH,), jnp.float32), 0.25, 1.75).astype(jnp.bfloat16)
    wq_x = bell_draw(keys[8], (WIDTH, WIDTH), WIDTH ** -0.5, 0.0625, ((0, 4), (1, 4)))
    wk_x = bell_draw(keys[9], (VIS_WIDTH, WIDTH), VIS_WIDTH ** -0.5, 0.15625, ((1, 4),))
    wv_x = bell_draw(keys[10], (VIS_WIDTH, WIDTH), VIS_WIDTH ** -0.5, 0.15625, ((1, 4),))
    wo_x = bell_draw(keys[11], (WIDTH, WIDTH), (WIDTH // 16) ** -0.5, 0.25, ((0, 4), (1, 4)))
    gate_x = jnp.clip(jax.random.uniform(keys[12], (WIDTH,), jnp.float32, -1.5, 1.5) * shard_levels(keys[12], (WIDTH,), ((0, 4),), -0.4, 0.0), -1.5, 1.5)
    text_image = draw_text_image(jax.random.fold_in(jax.random.fold_in(keys[14], part), 71), part)
    return dict(patches=patches, latents=latents, wq_res=wq_res, wk_res=wk_res, wv_res=wv_res, wo_res=wo_res, text=text, norm_gain=norm_gain, wq_x=wq_x, wk_x=wk_x, wv_x=wv_x, wo_x=wo_x, gate_x=gate_x, text_image=text_image)


def reference(patches, latents, wq_res, wk_res, wv_res, wo_res, text, norm_gain, wq_x, wk_x, wv_x, wo_x, gate_x, text_image):
    inv_res = 1.0 / math.sqrt(RES_HEAD)
    inv_root = 1.0 / math.sqrt(HEAD)
    queries = jnp.dot(latents, wq_res, preferred_element_type=jnp.float32).astype(jnp.bfloat16).reshape(LATENTS, RES_HEADS, RES_HEAD)
    page_keys = jnp.dot(patches, wk_res, preferred_element_type=jnp.float32).astype(jnp.bfloat16).reshape(IMAGES, PATCH_IMG, RES_HEADS, RES_HEAD)
    page_values = jnp.dot(patches, wv_res, preferred_element_type=jnp.float32).astype(jnp.bfloat16).reshape(IMAGES, PATCH_IMG, RES_HEADS, RES_HEAD)
    scores = jnp.einsum('lhd,iphd->ihlp', queries.astype(jnp.float32), page_keys.astype(jnp.float32)) * inv_res
    summit = lax.optimization_barrier(jnp.max(scores, axis=3, keepdims=True))
    rounded = jnp.exp(scores - summit).astype(jnp.bfloat16)
    weights = lax.optimization_barrier(rounded).astype(jnp.float32)
    totals = lax.optimization_barrier(jnp.sum(weights, axis=3))
    blended = jnp.einsum('ihlp,iphd->ihld', weights, page_values.astype(jnp.float32))
    pooled = (blended / totals[:, :, :, None]).transpose(0, 2, 1, 3).reshape(IMAGES * LATENTS, RES_INNER).astype(jnp.bfloat16)
    repeated = jnp.tile(latents.astype(jnp.float32), (IMAGES, 1))
    page_latents = (repeated + jnp.dot(pooled, wo_res, preferred_element_type=jnp.float32)).astype(jnp.bfloat16)
    hidden = text.astype(jnp.float32)
    inverse = lax.rsqrt(lax.optimization_barrier(jnp.mean(hidden * hidden, axis=1)) + 1e-05)
    scaled = (hidden * norm_gain.astype(jnp.float32)).astype(jnp.bfloat16)
    heads_x = WIDTH // HEAD
    text_queries = (jnp.dot(scaled, wq_x, preferred_element_type=jnp.float32) * inverse[:, None]).astype(jnp.bfloat16).reshape(TEXT, heads_x, HEAD)
    cross_keys = jnp.dot(page_latents, wk_x, preferred_element_type=jnp.float32).astype(jnp.bfloat16).reshape(IMAGES * LATENTS, heads_x, HEAD)
    cross_values = jnp.dot(page_latents, wv_x, preferred_element_type=jnp.float32).astype(jnp.bfloat16).reshape(IMAGES * LATENTS, heads_x, HEAD)
    latent_owner = jnp.arange(IMAGES * LATENTS, dtype=jnp.int32) // LATENTS
    allowed = text_image[:, None] == latent_owner[None, :]

    def one_head(operands):
        head_q, head_k, head_v = operands
        logits = jnp.dot(head_q.astype(jnp.float32), head_k.astype(jnp.float32).T) * inv_root
        logits = jnp.where(allowed, logits, -1e+30)
        row_peak = lax.optimization_barrier(jnp.max(logits, axis=1, keepdims=True))
        head_round = jnp.exp(logits - row_peak).astype(jnp.bfloat16)
        head_weights = lax.optimization_barrier(head_round).astype(jnp.float32)
        row_total = lax.optimization_barrier(jnp.sum(head_weights, axis=1))
        mixture = jnp.dot(head_weights, head_v.astype(jnp.float32))
        return mixture / row_total[:, None]
    per_head = lax.map(one_head, (text_queries.transpose(1, 0, 2), cross_keys.transpose(1, 0, 2), cross_values.transpose(1, 0, 2)))
    visible = (text_image >= 0).astype(jnp.float32)
    attended = (per_head.transpose(1, 0, 2) * visible[:, None, None]).astype(jnp.bfloat16).reshape(TEXT, WIDTH)
    col_group = WIDTH // N_TENSOR
    att_groups = attended.reshape(TEXT, N_TENSOR, col_group).transpose(1, 0, 2)
    wo_groups = wo_x.reshape(N_TENSOR, col_group, WIDTH)

    def add_group(running, inputs):
        term = lax.optimization_barrier(jnp.dot(inputs[0], inputs[1], preferred_element_type=jnp.float32).astype(jnp.bfloat16)).astype(jnp.float32)
        return (running + term, None)
    branch, unused = lax.scan(add_group, jnp.zeros((TEXT, WIDTH), jnp.float32), (att_groups, wo_groups))
    text_out = hidden + jnp.tanh(gate_x.astype(jnp.float32)) * branch
    return (text_out, page_latents)
```

```python
import functools
import math

import jax
import jax.numpy as jnp
from jax import lax
from jax.experimental import pallas as pl
from jax.experimental.pallas import tpu as pltpu
from jax.sharding import PartitionSpec as P

HEAD = 128
RES_HEAD = 96
PATCH_IMG = 257
SUB = 32
LEAD = 9
SUM_STEP, PAGE_STEP, PASS_STEP = 3, 6, 8
EARLY, LATER = 3, 7
RING = 4
BF = jnp.bfloat16
F32 = jnp.float32


def resample(patches, latents, wq_res, wk_res, wv_res, wo_res):
    inv_res = 1.0 / math.sqrt(RES_HEAD)
    lat_count = latents.shape[0]
    img_count = patches.shape[0] // PATCH_IMG
    heads_res = wq_res.shape[1] // RES_HEAD
    queries = (
        jnp.dot(latents, wq_res, preferred_element_type=F32)
        .astype(BF)
        .reshape(lat_count, heads_res, RES_HEAD)
    )
    page_keys = (
        jnp.dot(patches, wk_res, preferred_element_type=F32)
        .astype(BF)
        .reshape(img_count, PATCH_IMG, heads_res, RES_HEAD)
    )
    page_values = (
        jnp.dot(patches, wv_res, preferred_element_type=F32)
        .astype(BF)
        .reshape(img_count, PATCH_IMG, heads_res, RES_HEAD)
    )
    scores = jnp.einsum("lhd,iphd->ihlp", queries, page_keys, preferred_element_type=F32) * inv_res
    summit = jnp.max(scores, axis=3, keepdims=True)
    weights = jnp.exp(scores - summit).astype(BF)
    totals = jnp.sum(weights, axis=3, dtype=F32)
    blended = jnp.einsum("ihlp,iphd->ihld", weights, page_values, preferred_element_type=F32)
    pooled = (
        (blended / totals[:, :, :, None])
        .transpose(0, 2, 1, 3)
        .reshape(img_count * lat_count, heads_res * RES_HEAD)
        .astype(BF)
    )
    return jnp.dot(pooled, wo_res, preferred_element_type=F32)


def flow_kernel(dims, *refs):
    n_x, n, count, sub, owners, shared = dims
    (part_ref, lat_ref, gain_ref, img_ref, own_ref, text_ref, wq_ref, wk_ref, wv_ref, wo_ref) = refs[:10]
    out_ref, page_ref = refs[10:12]
    (wq, wkv, late, text, own_half, away_out, away_in, x_out, x_in, sq_half, sq_away_out, sq_away_in,
     sq_x_out, sq_x_in, query, keys, values, pages, lat_in, att, part, came) = refs[12:34]
    (load_sem, text_sem, qc_send, qc_recv, qx_send, qx_recv, lat_send, lat_recv, pz_send, pz_recv,
     pg_send, pg_x, pg_core, side_sem, core_sem, block_sem, in_sem, back_sem, inward_sem,
     outward_sem) = refs[34:]
    n_seq, half = 2 * n_x, n // 2
    total = count * n_seq
    rows_all, rows_half = n_seq * sub, n_x * sub
    seq_me, me = lax.axis_index("seq"), lax.axis_index("tensor")
    core, x_me = seq_me % 2, seq_me // 2
    partner = 2 * x_me + 1 - core
    own = core * n_x + x_me
    side = me // half
    depth = me * (1 - side) + (n - 1 - me) * side
    inner, outer = me + 1 - 2 * side, me - 1 + 2 * side
    lag = 2 + 4 * (half - 1 - depth)
    feat, qwidth = wq.shape
    width = wo_ref.shape[1]
    heads = qwidth // HEAD
    scale = 1.0 / math.sqrt(HEAD)
    lat_rows = part_ref.shape[0]
    vis = part_ref.shape[1]
    part_rows = lat_rows // owners
    stride = n // owners
    wo = wkv if shared else late

    def remote(src, dst, sent, got, **where):
        return pltpu.make_async_remote_copy(
            src_ref=src, dst_ref=dst, send_sem=sent, recv_sem=got,
            device_id=where, device_id_type=pl.DeviceIdType.MESH,
        )

    def other_x(j):
        return (x_me + j) % n_x

    def other_z(j):
        return (me + j) % n

    def load_text(c):
        rows = pl.ds(pl.multiple_of(c * rows_all, rows_all), rows_all)
        return pltpu.make_async_copy(text_ref.at[rows], text.at[c % RING], text_sem.at[c % RING])

    load_q = pltpu.make_async_copy(wq_ref, wq, load_sem.at[0])
    load_k = pltpu.make_async_copy(wk_ref, wkv.at[pl.ds(0, vis)], load_sem.at[1])
    load_v = pltpu.make_async_copy(wv_ref, wkv.at[pl.ds(vis, vis)], load_sem.at[2])
    load_o = pltpu.make_async_copy(wo_ref, wo.at[pl.ds(0, qwidth)], load_sem.at[3])

    def lat_piece(j):
        rows = pl.ds(j * part_rows, part_rows)
        return remote(
            part_ref.at[rows], lat_in.at[me], lat_send.at[j], lat_recv.at[me], tensor=j * stride
        )

    def page_rows(j):
        return pl.ds(pl.multiple_of(j * part_rows, part_rows), part_rows)

    def page_piece(j, z, k):
        ref = pages.at[seq_me, page_rows(j)]
        return remote(ref, ref, pz_send.at[k], pz_recv.at[j], tensor=z)

    def page_core(x, j):
        ref = pages.at[2 * x + core]
        return remote(ref, ref, pg_send.at[j], pg_core.at[x], seq=partner)

    def page_from_core(x):
        ref = pages.at[2 * x + 1 - core]
        return remote(ref, ref, pg_send.at[0], pg_core.at[x], seq=partner)

    def page_x(j):
        ref = pages.at[seq_me]
        return remote(
            ref, ref, pg_send.at[n_x + j - 1], pg_x.at[x_me], seq=2 * other_x(j) + core
        )

    def page_from_x(j):
        x = other_x(j)
        ref = pages.at[2 * x + core]
        return remote(ref, ref, pg_send.at[n_x + j - 1], pg_x.at[x], seq=2 * x + core)

    def away(c, which):
        src, dst = (away_out, away_in) if which == 0 else (sq_away_out, sq_away_in)
        return remote(
            src.at[c % RING], dst.at[c], qc_send.at[which, c % RING], qc_recv.at[which, c], seq=partner
        )

    def aside(c, j, which):
        src, dst = (x_out, x_in) if which == 0 else (sq_x_out, sq_x_in)
        return remote(
            src.at[c % RING, j - 1], dst.at[c, j - 1], qx_send.at[which, c % RING, j - 1],
            qx_recv.at[which, c, j - 1], seq=2 * other_x(j) + core,
        )

    def to_core(c, x, j):
        ref = att.at[c, core * n_x + x]
        return remote(ref, ref, block_sem.at[c, j], core_sem.at[c, x], seq=partner)

    def from_core(c, x):
        ref = att.at[c, (1 - core) * n_x + x]
        return remote(ref, ref, block_sem.at[c, 0], core_sem.at[c, x], seq=partner)

    def to_x(c, j):
        ref = att.at[c, own]
        return remote(
            ref, ref, block_sem.at[c, n_x + j - 1], side_sem.at[c, x_me], seq=2 * other_x(j) + core
        )

    def from_x(c, j):
        x = other_x(j)
        ref = att.at[c, core * n_x + x]
        return remote(ref, ref, block_sem.at[c, n_x + j - 1], side_sem.at[c, x], seq=2 * x + core)

    def rows_of(p):
        return pl.ds(pl.multiple_of(p * sub, sub), sub)

    def inward(p):
        return remote(part.at[p], came.at[p], inward_sem.at[p], in_sem.at[p], tensor=inner)

    def across(p):
        return remote(
            part.at[p], out_ref.at[rows_of(p)], inward_sem.at[p], back_sem.at[p], tensor=inner
        )

    def outward(p):
        ref = out_ref.at[rows_of(p)]
        return remote(ref, ref, outward_sem.at[p], back_sem.at[p], tensor=outer)

    def half_rows(which):
        return pl.ds(pl.multiple_of(which * rows_half, rows_half), rows_half)

    def strip(x):
        return pl.ds(pl.multiple_of(x * sub, sub), sub)

    def project(c):
        slot = c % RING
        load_text(c).wait()

        @pl.when(c >= RING)
        def _():
            for which in (0, 1):
                away(c - RING, which).wait_send()

        rows = jnp.concatenate(
            [text[slot, half_rows(1 - core)], text[slot, half_rows(core)]], axis=0
        ).astype(F32)
        squares = rows * rows
        sums = squares[:, :128]
        for g in range(1, feat // 128):
            sums = sums + squares[:, g * 128 : (g + 1) * 128]
        sq_away_out[slot] = sums[:rows_half]
        sq_half[c] = sums[rows_half:]
        scaled = (rows * gain_ref[...].astype(F32)).astype(BF)
        tile = math.gcd(qwidth, 1024)
        for t in range(0, qwidth, tile):
            value = jnp.dot(scaled, wq[:, t : t + tile], preferred_element_type=F32)
            away_out[slot, :, t : t + tile] = value[:rows_half].astype(BF)
            own_half[c, :, t : t + tile] = value[rows_half:]
        for which in (0, 1):
            away(c, which).start()

        @pl.when(c + RING < count)
        def _():
            load_text(c + RING).start()

    def scatter(c):
        slot = c % RING
        for which in (0, 1):
            away(c, which).wait_recv()

        @pl.when(c >= RING)
        def _():
            for j in range(1, n_x):
                for which in (0, 1):
                    aside(c - RING, j, which).wait_send()

        for j in range(1, n_x):
            rows = strip(other_x(j))
            x_out[slot, j - 1] = (own_half[c, rows] + away_in[c, rows].astype(F32)).astype(BF)
            sq_x_out[slot, j - 1] = sq_half[c, rows] + sq_away_in[c, rows]
            for which in (0, 1):
                aside(c, j, which).start()

    def finish(c):
        rows = strip(x_me)
        value = own_half[c, rows] + away_in[c, rows].astype(F32)
        square = sq_half[c, rows] + sq_away_in[c, rows]
        for j in range(1, n_x):
            for which in (0, 1):
                aside(c, j, which).wait_recv()
            value = value + x_in[c, j - 1].astype(F32)
            square = square + sq_x_in[c, j - 1]
        mean = jnp.sum(square, axis=1, keepdims=True) / (feat * n_seq)
        query[...] = (value * lax.rsqrt(mean + 1e-05)).astype(BF)

    def attend(c):
        img = img_ref[strip(c)]
        allowed = img == own_ref[...]
        visible = (img >= 0).astype(F32)
        cuts = [slice(h * HEAD, (h + 1) * HEAD) for h in range(heads)]
        logits = [
            lax.dot_general(
                query[:, cut], keys[:, cut], (((1,), (1,)), ((), ())), preferred_element_type=F32
            )
            for cut in cuts
        ]
        logits = [jnp.where(allowed, value * scale, -1e30) for value in logits]
        peaks = [jnp.max(value, axis=1, keepdims=True) for value in logits]
        probs = [jnp.exp(value - peak).astype(BF) for value, peak in zip(logits, peaks)]
        weights = [jnp.sum(p.astype(F32), axis=1, keepdims=True) for p in probs]
        mixed = [
            jnp.dot(p, values[:, cut], preferred_element_type=F32) for p, cut in zip(probs, cuts)
        ]
        for value, weight, cut in zip(mixed, weights, cuts):
            att[c, own, :, cut] = (value / weight * visible).astype(BF)
        for j in range(1, n_x):
            to_x(c, j).start()
        to_core(c, x_me, 0).start()

    def product(c):
        tile = math.gcd(width, 1024)

        @pl.loop(0, width // tile)
        def _(t):
            cols = pl.ds(pl.multiple_of(t * tile, tile), tile)
            rows = att[c].reshape(rows_all, qwidth)
            value = jnp.dot(rows, wo[:qwidth, cols], preferred_element_type=F32).astype(BF)
            for b in range(n_seq):
                part[c * n_seq + b, :, cols] = value[b * sub : (b + 1) * sub]

    def gather(p):
        @pl.when(depth > 0)
        def _():
            inward(p).wait_recv()
            part[p] = (part[p].astype(F32) + came[p].astype(F32)).astype(BF)

        @pl.when(depth < half - 1)
        def _():
            inward(p).start()

        @pl.when(depth == half - 1)
        def _():
            across(p).start()

    def spread(p):
        outward(p).wait_recv()

        @pl.when(depth == half - 1)
        def _():
            rows = rows_of(p)
            out_ref[rows] = (part[p].astype(F32) + out_ref[rows].astype(F32)).astype(BF)

        @pl.when(depth > 0)
        def _():
            outward(p).start()

    def sum_latents():
        @pl.when(me % stride == 0)
        def _():
            j = me // stride
            rows = page_rows(j)
            value = part_ref[rows]
            for k in range(1, n):
                z = other_z(k)
                remote(
                    part_ref.at[rows], lat_in.at[z], lat_send.at[0], lat_recv.at[z], tensor=z
                ).wait_recv()
                value = value + lat_in[z]
            base = (j * part_rows) % lat_ref.shape[0]
            mine = lat_ref[pl.ds(pl.multiple_of(base, part_rows), part_rows)].astype(F32)
            pages[seq_me, rows] = (mine + value).astype(BF)
            for k in range(1, n):
                page_piece(j, other_z(k), k - 1).start()

    def share_page():
        for j in range(owners):
            @pl.when(me != j * stride)
            def _(j=j):
                page_piece(j, j * stride, 0).wait_recv()

        for j in range(1, n_x):
            page_x(j).start()
        page_core(x_me, 0).start()
        page_ref[...] = pages[seq_me]

    def pass_pages():
        for j in range(1, n_x):
            page_from_x(j).wait_recv()
            page_core(other_x(j), j).start()

    def keys_values():
        load_k.wait()
        load_v.wait()
        for x in range(n_x):
            page_from_core(x).wait_recv()
        rows = pages[...].reshape(n_seq * lat_rows, vis)
        tile = math.gcd(qwidth, 1024)
        for base, target in ((0, keys), (vis, values)):
            @pl.loop(0, qwidth // tile)
            def _(t, base=base, target=target):
                cols = pl.ds(pl.multiple_of(t * tile, tile), tile)
                target[:, cols] = jnp.dot(
                    rows, wkv[base : base + vis, cols], preferred_element_type=F32
                ).astype(BF)
        if shared:
            load_o.start()

    load_text(0).start()
    load_q.start()
    for c in range(1, min(RING, count)):
        load_text(c).start()
    load_k.start()
    load_v.start()
    if not shared:
        load_o.start()

    barrier = pltpu.get_barrier_semaphore()

    def greet(**where):
        pl.semaphore_signal(barrier, inc=1, device_id=where, device_id_type=pl.DeviceIdType.MESH)

    greet(seq=partner)
    for j in range(1, n_x):
        greet(seq=2 * other_x(j) + core)
    for j in range(1, n):
        greet(tensor=other_z(j))
    pl.semaphore_wait(barrier, 1 + (n_x - 1) + (n - 1))

    for j in range(owners):
        @pl.when(me != j * stride)
        def _(j=j):
            lat_piece(j).start()

    load_q.wait()

    @pl.loop(0, count + LEAD + 1)
    def _(s):
        pl.when(s == SUM_STEP)(sum_latents)
        pl.when(s == PAGE_STEP)(share_page)
        pl.when(s == PASS_STEP)(pass_pages)

        @pl.when(s < count)
        def _():
            project(s)

        later = jnp.maximum(s - LATER, 0)

        @pl.when(jnp.logical_or(s == EARLY, jnp.logical_and(later >= 1, later < count)))
        def _():
            scatter(later)

        c = s - LEAD - 1

        @pl.when(c >= 0)
        def _():
            for j in range(1, n_x):
                from_x(c, j).wait_recv()
                to_core(c, other_x(j), j).start()

        pl.when(s == LEAD)(keys_values)

        @pl.when(jnp.logical_and(s >= LEAD, s < LEAD + count))
        def _():
            finish(s - LEAD)
            attend(s - LEAD)

        pl.when(c == 0)(load_o.wait)

        @pl.when(c >= 0)
        def _():
            for x in range(n_x):
                from_core(c, x).wait_recv()
            product(c)

            @pl.loop(0, n_seq)
            def _(b):
                p = c * n_seq + b
                gather(p)

                @pl.when(jnp.logical_and(depth > 0, p >= lag))
                def _():
                    spread(p - lag)

    @pl.loop(0, total)
    def _(p):
        @pl.when(jnp.logical_or(depth == 0, p >= total - lag))
        def _():
            spread(p)

    @pl.loop(0, total)
    def _(p):
        inward(p).wait_send()

        @pl.when(depth > 0)
        def _():
            outward(p).wait_send()

    @pl.loop(0, count)
    def _(c):
        for j in range(n_x):
            to_core(c, x_me, j).wait_send()
        for j in range(1, n_x):
            to_x(c, j).wait_send()

    for c in range(max(count - RING, 0), count):
        for which in (0, 1):
            away(c, which).wait_send()
            for j in range(1, n_x):
                aside(c, j, which).wait_send()
    for j in range(n_x):
        page_core(x_me, j).wait_send()
    for j in range(1, n_x):
        page_x(j).wait_send()
    for j in range(owners):
        @pl.when(me != j * stride)
        def _(j=j):
            lat_piece(j).wait_send()

    @pl.when(me % stride == 0)
    def _():
        for k in range(1, n):
            page_piece(me // stride, other_z(k), k - 1).wait_send()


def flow(partial_value, latents, gain, img, owner, text, wq, wk, wv, wo, n_x, n):
    n_seq = 2 * n_x
    tokens, feat = text.shape
    qwidth, width = wo.shape
    lat_rows, vis = partial_value.shape
    sub = math.gcd(tokens // n_seq, SUB)
    count = tokens // (n_seq * sub)
    pieces = count * n_seq
    owners = math.gcd(n, lat_rows // 16)
    shared = qwidth == width and qwidth <= 2 * vis
    dma = pltpu.SemaphoreType.DMA
    vmem, anywhere = pl.BlockSpec(memory_space=pltpu.VMEM), pl.BlockSpec(memory_space=pl.ANY)
    others = max(n_x - 1, 1)
    half_rows = n_x * sub
    scratch = [
        ((feat, qwidth), BF),
        ((2 * vis, qwidth), BF),
        ((16, 128) if shared else (qwidth, width), BF),
        ((RING, n_seq * sub, feat), BF),
        ((count, half_rows, qwidth), F32),
        ((RING, half_rows, qwidth), BF),
        ((count, half_rows, qwidth), BF),
        ((RING, others, sub, qwidth), BF),
        ((count, others, sub, qwidth), BF),
        ((count, half_rows, 128), F32),
        ((RING, half_rows, 128), F32),
        ((count, half_rows, 128), F32),
        ((RING, others, sub, 128), F32),
        ((count, others, sub, 128), F32),
        ((sub, qwidth), BF),
        ((n_seq * lat_rows, qwidth), BF),
        ((n_seq * lat_rows, qwidth), BF),
        ((n_seq, lat_rows, vis), BF),
        ((n, lat_rows // owners, vis), F32),
        ((count, n_seq, sub, qwidth), BF),
        ((pieces, sub, width), BF),
        ((pieces, sub, width), BF),
    ]
    return pl.pallas_call(
        functools.partial(flow_kernel, (n_x, n, count, sub, owners, shared)),
        out_shape=(
            jax.ShapeDtypeStruct((tokens, width), BF),
            jax.ShapeDtypeStruct((lat_rows, vis), BF),
        ),
        in_specs=[vmem] * 5 + [anywhere] * 5,
        out_specs=(vmem, vmem),
        scratch_shapes=[pltpu.VMEM(shape, kind) for shape, kind in scratch]
        + [
            dma((4,)),
            dma((RING,)),
            dma((2, RING)),
            dma((2, count)),
            dma((2, RING, others)),
            dma((2, count, others)),
            dma((owners,)),
            dma((n,)),
            dma((n,)),
            dma((owners,)),
            dma((2 * n_x,)),
            dma((n_x,)),
            dma((n_x,)),
            dma((count, n_x)),
            dma((count, n_x)),
            dma((count, 2 * n_x - 1)),
        ]
        + [dma((pieces,))] * 4,
        compiler_params=pltpu.CompilerParams(
            collective_id=0, has_side_effects=True, vmem_limit_bytes=63 << 20
        ),
        name="flow",
    )(partial_value, latents, gain, img, owner, text, wq, wk, wv, wo)


def close_kernel(rows, text_ref, gate_ref, branch_ref, out_ref):
    at = pl.multiple_of(pl.program_id(0) * rows, rows)
    branch = branch_ref[pl.ds(at, rows)].astype(F32)
    out_ref[...] = text_ref[...].astype(F32) + jnp.tanh(gate_ref[...]) * branch


def close(text, gate, branch):
    tokens, width = text.shape
    rows = math.gcd(tokens, 128)
    block = pl.BlockSpec((rows, width), lambda i: (i, 0))
    whole = pl.BlockSpec(memory_space=pltpu.VMEM)
    return pl.pallas_call(
        functools.partial(close_kernel, rows),
        out_shape=jax.ShapeDtypeStruct((tokens, width), F32),
        grid=(tokens // rows,),
        in_specs=[block, whole, whole],
        out_specs=block,
        compiler_params=pltpu.CompilerParams(vmem_limit_bytes=16 << 20),
        name="close",
    )(text, gate, branch)


def make_shards(n_seq, n_tensor):
    n_x = n_seq // 2

    def shards(
        patches,
        latents,
        wq_res,
        wk_res,
        wv_res,
        wo_res,
        text,
        norm_gain,
        wq_x,
        wk_x,
        wv_x,
        wo_x,
        gate_x,
        text_image,
    ):
        seq_me = lax.axis_index("seq")
        block = (seq_me % 2) * n_x + seq_me // 2
        lat_count = latents.shape[0]
        tokens = text.shape[0]
        sub = math.gcd(tokens // n_seq, SUB)
        img = lax.dynamic_index_in_dim(
            text_image.reshape(-1, n_seq, sub), block, 1, keepdims=False
        ).reshape(-1, 1)
        partial_value = resample(patches, latents, wq_res, wk_res, wv_res, wo_res)
        owner = jnp.arange(n_seq * partial_value.shape[0], dtype=jnp.int32) // lat_count
        branch, page_latents = flow(
            partial_value, latents, norm_gain[None, :], img, owner[None, :], text,
            wq_x, wk_x, wv_x, wo_x, n_x, n_tensor,
        )
        return close(text, gate_x[None, :], branch), page_latents

    return shards


def solution(mesh):
    in_specs = (
        P(("groups", "seq"), None),
        P(),
        P(None, "tensor"),
        P(None, "tensor"),
        P(None, "tensor"),
        P("tensor", None),
        P("groups", "seq"),
        P("seq"),
        P("seq", "tensor"),
        P(None, "tensor"),
        P(None, "tensor"),
        P("tensor", "seq"),
        P("seq"),
        P("groups"),
    )
    out_specs = (P("groups", "seq"), P(("groups", "seq"), None))
    body = make_shards(mesh.shape["seq"], mesh.shape["tensor"])
    return jax.shard_map(body, mesh=mesh, in_specs=in_specs, out_specs=out_specs, check_vma=False)
```

```python
import functools
import math

import jax
import jax.numpy as jnp
from jax import lax
from jax.experimental import pallas as pl
from jax.experimental.pallas import tpu as pltpu
from jax.sharding import PartitionSpec as P

HEAD = 128
RES_HEAD = 96
PATCH_IMG = 257
SUB = 32
LEAD = 9
SUM_STEP, PAGE_STEP, PASS_STEP = 3, 6, 8
EARLY, LATER = 3, 7
RING = 2
BF = jnp.bfloat16
F32 = jnp.float32


def resample(patches, latents, wq_res, wk_res, wv_res, wo_res):
    inv_res = 1.0 / math.sqrt(RES_HEAD)
    lat_count = latents.shape[0]
    img_count = patches.shape[0] // PATCH_IMG
    heads_res = wq_res.shape[1] // RES_HEAD
    queries = (
        jnp.dot(latents, wq_res, preferred_element_type=F32)
        .astype(BF)
        .reshape(lat_count, heads_res, RES_HEAD)
    )
    page_keys = (
        jnp.dot(patches, wk_res, preferred_element_type=F32)
        .astype(BF)
        .reshape(img_count, PATCH_IMG, heads_res, RES_HEAD)
    )
    page_values = (
        jnp.dot(patches, wv_res, preferred_element_type=F32)
        .astype(BF)
        .reshape(img_count, PATCH_IMG, heads_res, RES_HEAD)
    )
    scores = jnp.einsum("lhd,iphd->ihlp", queries, page_keys, preferred_element_type=F32) * inv_res
    summit = jnp.max(scores, axis=3, keepdims=True)
    weights = jnp.exp(scores - summit).astype(BF)
    totals = jnp.sum(weights, axis=3, dtype=F32)
    blended = jnp.einsum("ihlp,iphd->ihld", weights, page_values, preferred_element_type=F32)
    pooled = (
        (blended / totals[:, :, :, None])
        .transpose(0, 2, 1, 3)
        .reshape(img_count * lat_count, heads_res * RES_HEAD)
        .astype(BF)
    )
    return jnp.dot(pooled, wo_res, preferred_element_type=F32)


def flow_kernel(dims, *refs):
    n_x, n, count, sub, owners, shared, first = dims
    (part_ref, lat_ref, gain_ref, img_ref, own_ref, text_ref, wq_ref, wk_ref, wv_ref, wo_ref) = refs[:10]
    out_ref, text, page_ref = refs[10:13]
    (wq, wkv, late, own_half, away_out, away_in, x_out, x_in, sq_half, sq_away_out, sq_away_in,
     sq_x_out, sq_x_in, query, keys, values, pages, lat_in, att, second, came, mixed_rows) = refs[13:35]
    (load_sem, text_sem, qc_send, qc_recv, qx_send, qx_recv, lat_send, lat_recv, pz_send, pz_recv,
     pg_send, pg_x, pg_core, side_sem, core_sem, block_sem, in_sem, back_sem, inward_sem,
     outward_sem, free_sem) = refs[35:]
    n_seq, half = 2 * n_x, n // 2
    total = count * n_seq
    keep = own_half.shape[0]
    rows_all, rows_half = n_seq * sub, n_x * sub
    seq_me, me = lax.axis_index("seq"), lax.axis_index("tensor")
    core, x_me = seq_me % 2, seq_me // 2
    partner = 2 * x_me + 1 - core
    own = core * n_x + x_me
    side = me // half
    depth = me * (1 - side) + (n - 1 - me) * side
    inner, outer = me + 1 - 2 * side, me - 1 + 2 * side
    lag = 2 + 4 * (half - 1 - depth)
    feat, qwidth = wq.shape
    width = wo_ref.shape[1]
    heads = qwidth // HEAD
    scale = 1.0 / math.sqrt(HEAD)
    lat_rows = part_ref.shape[0]
    vis = part_ref.shape[1]
    part_rows = lat_rows // owners
    stride = n // owners
    wo = wkv if shared else late
    part = att if shared else second

    def remote(src, dst, sent, got, **where):
        return pltpu.make_async_remote_copy(
            src_ref=src, dst_ref=dst, send_sem=sent, recv_sem=got,
            device_id=where, device_id_type=pl.DeviceIdType.MESH,
        )

    def other_x(j):
        return (x_me + j) % n_x

    def other_z(j):
        return (me + j) % n

    def load_text(c):
        rows = pl.ds(pl.multiple_of(c * rows_all, rows_all), rows_all)
        return pltpu.make_async_copy(text_ref.at[rows], text.at[rows], text_sem.at[c])

    load_q = pltpu.make_async_copy(wq_ref, wq, load_sem.at[0])
    load_k = pltpu.make_async_copy(wk_ref, wkv.at[pl.ds(0, vis)], load_sem.at[1])
    load_v = pltpu.make_async_copy(wv_ref, wkv.at[pl.ds(vis, vis)], load_sem.at[2])
    load_o = pltpu.make_async_copy(wo_ref, wo.at[pl.ds(0, qwidth)], load_sem.at[3])

    def lat_piece(j):
        rows = pl.ds(j * part_rows, part_rows)
        return remote(
            part_ref.at[rows], lat_in.at[me], lat_send.at[j], lat_recv.at[me], tensor=j * stride
        )

    def page_rows(j):
        return pl.ds(pl.multiple_of(j * part_rows, part_rows), part_rows)

    def page_piece(j, z, k):
        ref = pages.at[seq_me, page_rows(j)]
        return remote(ref, ref, pz_send.at[k], pz_recv.at[j], tensor=z)

    def page_core(x, j, k):
        ref = pages.at[2 * x + core, page_rows(k)]
        return remote(ref, ref, pg_send.at[j, k], pg_core.at[x, k], seq=partner)

    def page_from_core(x, k):
        ref = pages.at[2 * x + 1 - core, page_rows(k)]
        return remote(ref, ref, pg_send.at[0, k], pg_core.at[x, k], seq=partner)

    def page_x(j, k):
        ref = pages.at[seq_me, page_rows(k)]
        return remote(
            ref, ref, pg_send.at[n_x + j - 1, k], pg_x.at[x_me, k], seq=2 * other_x(j) + core
        )

    def page_from_x(j, k):
        x = other_x(j)
        ref = pages.at[2 * x + core, page_rows(k)]
        return remote(ref, ref, pg_send.at[n_x + j - 1, k], pg_x.at[x, k], seq=2 * x + core)

    def away(c, which):
        src, dst = (away_out, away_in) if which == 0 else (sq_away_out, sq_away_in)
        return remote(
            src.at[c % RING], dst.at[c], qc_send.at[which, c % RING], qc_recv.at[which, c], seq=partner
        )

    def aside(c, j, which):
        src, dst = (x_out, x_in) if which == 0 else (sq_x_out, sq_x_in)
        return remote(
            src.at[c % RING, j - 1], dst.at[c, j - 1], qx_send.at[which, c % RING, j - 1],
            qx_recv.at[which, c, j - 1], seq=2 * other_x(j) + core,
        )

    def to_core(c, x, j):
        ref = att.at[c * n_seq + core * n_x + x]
        return remote(ref, ref, block_sem.at[c, j], core_sem.at[c, x], seq=partner)

    def from_core(c, x):
        ref = att.at[c * n_seq + (1 - core) * n_x + x]
        return remote(ref, ref, block_sem.at[c, 0], core_sem.at[c, x], seq=partner)

    def to_x(c, j):
        ref = att.at[c * n_seq + own]
        return remote(
            ref, ref, block_sem.at[c, n_x + j - 1], side_sem.at[c, x_me], seq=2 * other_x(j) + core
        )

    def from_x(c, j):
        x = other_x(j)
        ref = att.at[c * n_seq + core * n_x + x]
        return remote(ref, ref, block_sem.at[c, n_x + j - 1], side_sem.at[c, x], seq=2 * x + core)

    def rows_of(p):
        return pl.ds(pl.multiple_of(p * sub, sub), sub)

    def landing(p, early):
        if early:
            return came.at[p]
        return wq.at[pl.ds(pl.multiple_of((p - first) * sub, sub), sub)]

    def inward(p, early):
        return remote(part.at[p], landing(p, early), inward_sem.at[p], in_sem.at[p], tensor=inner)

    def across(p):
        return remote(
            part.at[p], out_ref.at[rows_of(p)], inward_sem.at[p], back_sem.at[p], tensor=inner
        )

    def outward(p):
        ref = out_ref.at[rows_of(p)]
        return remote(ref, ref, outward_sem.at[p], back_sem.at[p], tensor=outer)

    def half_rows(which):
        return pl.ds(pl.multiple_of(which * rows_half, rows_half), rows_half)

    def strip(x):
        return pl.ds(pl.multiple_of(x * sub, sub), sub)

    def project(c):
        slot = c % RING
        load_text(c).wait()

        @pl.when(c >= RING)
        def _():
            for which in (0, 1):
                away(c - RING, which).wait_send()

        rows = jnp.concatenate(
            [text[half_rows(2 * c + 1 - core)], text[half_rows(2 * c + core)]], axis=0
        ).astype(F32)
        squares = rows * rows
        sums = squares[:, :128]
        for g in range(1, feat // 128):
            sums = sums + squares[:, g * 128 : (g + 1) * 128]
        sq_away_out[slot] = sums[:rows_half]
        sq_half[c] = sums[rows_half:]
        scaled = (rows * gain_ref[...].astype(F32)).astype(BF)
        tile = math.gcd(qwidth, 1024)
        for t in range(0, qwidth, tile):
            value = jnp.dot(scaled, wq[:, t : t + tile], preferred_element_type=F32)
            away_out[slot, :, t : t + tile] = value[:rows_half].astype(BF)
            own_half[c % keep, :, t : t + tile] = value[rows_half:]
        for which in (0, 1):
            away(c, which).start()

    def scatter(c):
        slot = c % RING
        for which in (0, 1):
            away(c, which).wait_recv()

        @pl.when(c >= RING)
        def _():
            for j in range(1, n_x):
                for which in (0, 1):
                    aside(c - RING, j, which).wait_send()

        for j in range(1, n_x):
            rows = strip(other_x(j))
            x_out[slot, j - 1] = (own_half[c % keep, rows] + away_in[c, rows].astype(F32)).astype(BF)
            sq_x_out[slot, j - 1] = sq_half[c, rows] + sq_away_in[c, rows]
            for which in (0, 1):
                aside(c, j, which).start()

    def finish(c):
        rows = strip(x_me)
        value = own_half[c % keep, rows] + away_in[c, rows].astype(F32)
        square = sq_half[c, rows] + sq_away_in[c, rows]
        for j in range(1, n_x):
            for which in (0, 1):
                aside(c, j, which).wait_recv()
            value = value + x_in[c, j - 1].astype(F32)
            square = square + sq_x_in[c, j - 1]
        mean = jnp.sum(square, axis=1, keepdims=True) / (feat * n_seq)
        query[...] = (value * lax.rsqrt(mean + 1e-05)).astype(BF)

    def attend(c):
        img = img_ref[strip(c)]
        allowed = img == own_ref[...]
        visible = (img >= 0).astype(F32)
        cuts = [slice(h * HEAD, (h + 1) * HEAD) for h in range(heads)]
        logits = [
            lax.dot_general(
                query[:, cut], keys[:, cut], (((1,), (1,)), ((), ())), preferred_element_type=F32
            )
            for cut in cuts
        ]
        logits = [jnp.where(allowed, value * scale, -1e30) for value in logits]
        peaks = [jnp.max(value, axis=1, keepdims=True) for value in logits]
        probs = [jnp.exp(value - peak).astype(BF) for value, peak in zip(logits, peaks)]
        weights = [jnp.sum(p.astype(F32), axis=1, keepdims=True) for p in probs]
        mixed = [
            jnp.dot(p, values[:, cut], preferred_element_type=F32) for p, cut in zip(probs, cuts)
        ]
        for value, weight, cut in zip(mixed, weights, cuts):
            att[c * n_seq + own, :, cut] = (value / weight * visible).astype(BF)
        for j in range(1, n_x):
            to_x(c, j).start()
        to_core(c, x_me, 0).start()

    def product(c):
        tile = math.gcd(width, 1024)

        @pl.loop(0, width // tile)
        def _(t):
            cols = pl.ds(pl.multiple_of(t * tile, tile), tile)
            rows = att[pl.ds(c * n_seq, n_seq)].reshape(rows_all, qwidth)
            value = jnp.dot(rows, wo[:qwidth, cols], preferred_element_type=F32)
            mixed_rows[:, cols] = value.astype(BF)

        for j in range(n_x):
            to_core(c, x_me, j).wait_send()
        for j in range(1, n_x):
            to_x(c, j).wait_send()
        for b in range(n_seq):
            part[c * n_seq + b] = mixed_rows[b * sub : (b + 1) * sub]

    def gather(p):
        for early in (True, False)[: 1 + (first < total)]:
            @pl.when((p < first) == early)
            def _(early=early):
                @pl.when(depth > 0)
                def _():
                    inward(p, early).wait_recv()
                    part[p] = (part[p].astype(F32) + landing(p, early)[...].astype(F32)).astype(BF)

                @pl.when(depth < half - 1)
                def _():
                    if not early:
                        @pl.when(p == first)
                        def _():
                            pl.semaphore_wait(free_sem, 1)

                    inward(p, early).start()

        @pl.when(depth == half - 1)
        def _():
            across(p).start()

    def spread(p):
        outward(p).wait_recv()

        @pl.when(depth == half - 1)
        def _():
            rows = rows_of(p)
            out_ref[rows] = (part[p].astype(F32) + out_ref[rows].astype(F32)).astype(BF)

        @pl.when(depth > 0)
        def _():
            outward(p).start()

    def sum_latents():
        @pl.when(me % stride == 0)
        def _():
            j = me // stride
            rows = page_rows(j)
            value = part_ref[rows]
            for k in range(1, n):
                z = other_z(k)
                remote(
                    part_ref.at[rows], lat_in.at[z], lat_send.at[0], lat_recv.at[z], tensor=z
                ).wait_recv()
                value = value + lat_in[z]
            base = (j * part_rows) % lat_ref.shape[0]
            mine = lat_ref[pl.ds(pl.multiple_of(base, part_rows), part_rows)].astype(F32)
            pages[seq_me, rows] = (mine + value).astype(BF)
            for k in range(1, n):
                page_piece(j, other_z(k), k - 1).start()

    def share_page():
        for k in range(owners):
            j = (me // stride + k) % owners

            @pl.when(me != j * stride)
            def _(j=j):
                page_piece(j, j * stride, 0).wait_recv()

            for i in range(1, n_x):
                page_x(i, j).start()
            page_core(x_me, 0, j).start()
        page_ref[...] = pages[seq_me]

    def pass_pages():
        for k in range(owners):
            j = (me // stride + k) % owners
            for i in range(1, n_x):
                page_from_x(i, j).wait_recv()
                page_core(other_x(i), i, j).start()

    def keys_values():
        load_k.wait()
        load_v.wait()
        for x in range(n_x):
            for k in range(owners):
                page_from_core(x, k).wait_recv()
        rows = pages[...].reshape(n_seq * lat_rows, vis)
        tile = math.gcd(qwidth, 1024)
        for base, target in ((0, keys), (vis, values)):
            @pl.loop(0, qwidth // tile)
            def _(t, base=base, target=target):
                cols = pl.ds(pl.multiple_of(t * tile, tile), tile)
                target[:, cols] = jnp.dot(
                    rows, wkv[base : base + vis, cols], preferred_element_type=F32
                ).astype(BF)
        if shared:
            load_o.start()

    load_text(0).start()
    load_q.start()
    for c in range(1, count):
        load_text(c).start()
    load_k.start()
    load_v.start()
    if not shared:
        load_o.start()

    barrier = pltpu.get_barrier_semaphore()

    def greet(**where):
        pl.semaphore_signal(barrier, inc=1, device_id=where, device_id_type=pl.DeviceIdType.MESH)

    greet(seq=partner)
    for j in range(1, n_x):
        greet(seq=2 * other_x(j) + core)
    for j in range(1, n):
        greet(tensor=other_z(j))
    pl.semaphore_wait(barrier, 1 + (n_x - 1) + (n - 1))

    for j in range(owners):
        @pl.when(me != j * stride)
        def _(j=j):
            lat_piece(j).start()

    load_q.wait()

    @pl.loop(0, count + LEAD + 1)
    def _(s):
        pl.when(s == SUM_STEP)(sum_latents)
        pl.when(s == PAGE_STEP)(share_page)
        pl.when(s == PASS_STEP)(pass_pages)

        @pl.when(s < count)
        def _():
            project(s)

            if first < total:
                @pl.when(jnp.logical_and(s == count - 1, depth > 0))
                def _():
                    pl.semaphore_signal(
                        free_sem, inc=1, device_id={"tensor": outer},
                        device_id_type=pl.DeviceIdType.MESH,
                    )

        later = jnp.maximum(s - LATER, 0)

        @pl.when(jnp.logical_or(s == EARLY, jnp.logical_and(later >= 1, later < count)))
        def _():
            scatter(later)

        c = s - LEAD - 1

        @pl.when(c >= 0)
        def _():
            for j in range(1, n_x):
                from_x(c, j).wait_recv()
                to_core(c, other_x(j), j).start()

        pl.when(s == LEAD)(keys_values)

        @pl.when(jnp.logical_and(s >= LEAD, s < LEAD + count))
        def _():
            finish(s - LEAD)
            attend(s - LEAD)

        pl.when(c == 0)(load_o.wait)

        @pl.when(c >= 0)
        def _():
            for x in range(n_x):
                from_core(c, x).wait_recv()
            product(c)

            @pl.loop(0, n_seq)
            def _(b):
                p = c * n_seq + b
                gather(p)

                @pl.when(jnp.logical_and(depth > 0, p >= lag))
                def _():
                    spread(p - lag)

    @pl.loop(0, total)
    def _(p):
        @pl.when(jnp.logical_or(depth == 0, p >= total - lag))
        def _():
            spread(p)

    @pl.loop(0, total)
    def _(p):
        across(p).wait_send()

        @pl.when(depth > 0)
        def _():
            outward(p).wait_send()

    for c in range(max(count - RING, 0), count):
        for which in (0, 1):
            away(c, which).wait_send()
            for j in range(1, n_x):
                aside(c, j, which).wait_send()
    for k in range(owners):
        for j in range(n_x):
            page_core(x_me, j, k).wait_send()
        for j in range(1, n_x):
            page_x(j, k).wait_send()
    for j in range(owners):
        @pl.when(me != j * stride)
        def _(j=j):
            lat_piece(j).wait_send()

    @pl.when(me % stride == 0)
    def _():
        for k in range(1, n):
            page_piece(me // stride, other_z(k), k - 1).wait_send()


def flow(partial_value, latents, gain, img, owner, text, wq, wk, wv, wo, n_x, n):
    n_seq = 2 * n_x
    tokens, feat = text.shape
    qwidth, width = wo.shape
    lat_rows, vis = partial_value.shape
    sub = math.gcd(tokens // n_seq, SUB)
    count = tokens // (n_seq * sub)
    pieces = count * n_seq
    owners = math.gcd(n, lat_rows // 16)
    shared = qwidth == width and qwidth <= 2 * vis
    first = min(pieces, n_seq) if shared and pieces * sub <= feat else pieces
    dma = pltpu.SemaphoreType.DMA
    vmem, anywhere = pl.BlockSpec(memory_space=pltpu.VMEM), pl.BlockSpec(memory_space=pltpu.HBM)
    others = max(n_x - 1, 1)
    half_rows = n_x * sub
    stay = [pltpu.with_memory_space_constraint(v, pltpu.HBM) for v in (text, wq, wk, wv, wo)]
    scratch = [
        ((feat, qwidth), BF),
        ((2 * vis, qwidth), BF),
        ((16, 128) if shared else (qwidth, width), BF),
        ((min(count, LEAD + 2), half_rows, qwidth), F32),
        ((RING, half_rows, qwidth), BF),
        ((count, half_rows, qwidth), BF),
        ((RING, others, sub, qwidth), BF),
        ((count, others, sub, qwidth), BF),
        ((count, half_rows, 128), F32),
        ((RING, half_rows, 128), F32),
        ((count, half_rows, 128), F32),
        ((RING, others, sub, 128), F32),
        ((count, others, sub, 128), F32),
        ((sub, qwidth), BF),
        ((n_seq * lat_rows, qwidth), BF),
        ((n_seq * lat_rows, qwidth), BF),
        ((n_seq, lat_rows, vis), BF),
        ((n, lat_rows // owners, vis), F32),
        ((pieces, sub, qwidth), BF),
        ((1, 16, 128) if shared else (pieces, sub, width), BF),
        ((first, sub, width), BF),
        ((n_seq * sub, width), BF),
    ]
    return pl.pallas_call(
        functools.partial(flow_kernel, (n_x, n, count, sub, owners, shared, first)),
        out_shape=(
            jax.ShapeDtypeStruct((tokens, width), BF),
            jax.ShapeDtypeStruct((tokens, feat), BF),
            jax.ShapeDtypeStruct((lat_rows, vis), BF),
        ),
        in_specs=[vmem] * 5 + [anywhere] * 5,
        out_specs=(vmem, vmem, vmem),
        scratch_shapes=[pltpu.VMEM(shape, kind) for shape, kind in scratch]
        + [
            dma((4,)),
            dma((count,)),
            dma((2, RING)),
            dma((2, count)),
            dma((2, RING, others)),
            dma((2, count, others)),
            dma((owners,)),
            dma((n,)),
            dma((n,)),
            dma((owners,)),
            dma((2 * n_x, owners)),
            dma((n_x, owners)),
            dma((n_x, owners)),
            dma((count, n_x)),
            dma((count, n_x)),
            dma((count, 2 * n_x - 1)),
        ]
        + [dma((pieces,))] * 4
        + [pltpu.SemaphoreType.REGULAR],
        compiler_params=pltpu.CompilerParams(
            collective_id=0, has_side_effects=True, vmem_limit_bytes=41984 << 10
        ),
        name="flow",
    )(partial_value, latents, gain, img, owner, *stay)


def close_kernel(rows, slots, text_ref, gate_ref, branch_ref, out_ref, buf, sem):
    steps = text_ref.shape[0] // rows
    gate = jnp.tanh(gate_ref[...])

    def put(i):
        return pltpu.make_async_copy(
            buf.at[i % slots], out_ref.at[pl.ds(i * rows, rows)], sem.at[i % slots]
        )

    @pl.loop(0, steps)
    def _(i):
        @pl.when(i >= slots)
        def _():
            put(i - slots).wait()

        at = pl.ds(pl.multiple_of(i * rows, rows), rows)
        buf[i % slots] = text_ref[at].astype(F32) + gate * branch_ref[at].astype(F32)
        put(i).start()

    @pl.loop(max(steps - slots, 0), steps)
    def _(i):
        put(i).wait()


def close(text, gate, branch):
    tokens, width = text.shape
    rows = math.gcd(tokens, 64)
    whole = pl.BlockSpec(memory_space=pltpu.VMEM)
    return pl.pallas_call(
        functools.partial(close_kernel, rows, 4),
        out_shape=jax.ShapeDtypeStruct((tokens, width), F32),
        in_specs=[whole] * 3,
        out_specs=pl.BlockSpec(memory_space=pl.ANY),
        scratch_shapes=[pltpu.VMEM((4, rows, width), F32), pltpu.SemaphoreType.DMA((4,))],
        compiler_params=pltpu.CompilerParams(vmem_limit_bytes=4 << 20),
        name="close",
    )(text, gate, branch)


def make_shards(n_seq, n_tensor):
    n_x = n_seq // 2

    def shards(
        patches,
        latents,
        wq_res,
        wk_res,
        wv_res,
        wo_res,
        text,
        norm_gain,
        wq_x,
        wk_x,
        wv_x,
        wo_x,
        gate_x,
        text_image,
    ):
        seq_me = lax.axis_index("seq")
        block = (seq_me % 2) * n_x + seq_me // 2
        lat_count = latents.shape[0]
        tokens = text.shape[0]
        sub = math.gcd(tokens // n_seq, SUB)
        img = lax.dynamic_index_in_dim(
            text_image.reshape(-1, n_seq, sub), block, 1, keepdims=False
        ).reshape(-1, 1)
        partial_value = resample(patches, latents, wq_res, wk_res, wv_res, wo_res)
        owner = jnp.arange(n_seq * partial_value.shape[0], dtype=jnp.int32) // lat_count
        branch, text, page_latents = flow(
            partial_value, latents, norm_gain[None, :], img, owner[None, :], text,
            wq_x, wk_x, wv_x, wo_x, n_x, n_tensor,
        )
        return close(text, gate_x[None, :], branch), page_latents

    return shards


def solution(mesh):
    in_specs = (
        P(("groups", "seq"), None),
        P(),
        P(None, "tensor"),
        P(None, "tensor"),
        P(None, "tensor"),
        P("tensor", None),
        P("groups", "seq"),
        P("seq"),
        P("seq", "tensor"),
        P(None, "tensor"),
        P(None, "tensor"),
        P("tensor", "seq"),
        P("seq"),
        P("groups"),
    )
    out_specs = (P("groups", "seq"), P(("groups", "seq"), None))
    body = make_shards(mesh.shape["seq"], mesh.shape["tensor"])
    return jax.shard_map(body, mesh=mesh, in_specs=in_specs, out_specs=out_specs, check_vma=False)
```

```python
import functools
import math

import jax
import jax.numpy as jnp
from jax import lax
from jax.experimental import pallas as pl
from jax.experimental.pallas import tpu as pltpu
from jax.sharding import PartitionSpec as P

HEAD = 128
RES_HEAD = 96
PATCH_IMG = 257
SUB = 32
CUT = 2
TILES = 2
SOON = 2
LAG = 3
LEAD = 12
SUM_STEP, PAGE_STEP, PASS_STEP = 4, 8, 11
EARLY, AHEAD, LATER = 2, 2, 11
RING = 2
BF = jnp.bfloat16
F32 = jnp.float32


def resample(patches, latents, wq_res, wk_res, wv_res, wo_res):
    inv_res = 1.0 / math.sqrt(RES_HEAD)
    lat_count = latents.shape[0]
    img_count = patches.shape[0] // PATCH_IMG
    heads_res = wq_res.shape[1] // RES_HEAD
    queries = (
        jnp.dot(latents, wq_res, preferred_element_type=F32)
        .astype(BF)
        .reshape(lat_count, heads_res, RES_HEAD)
    )
    page_keys = (
        jnp.dot(patches, wk_res, preferred_element_type=F32)
        .astype(BF)
        .reshape(img_count, PATCH_IMG, heads_res, RES_HEAD)
    )
    page_values = (
        jnp.dot(patches, wv_res, preferred_element_type=F32)
        .astype(BF)
        .reshape(img_count, PATCH_IMG, heads_res, RES_HEAD)
    )
    scores = jnp.einsum("lhd,iphd->ihlp", queries, page_keys, preferred_element_type=F32) * inv_res
    summit = jnp.max(scores, axis=3, keepdims=True)
    weights = jnp.exp(scores - summit).astype(BF)
    totals = jnp.sum(weights, axis=3, dtype=F32)
    blended = jnp.einsum("ihlp,iphd->ihld", weights, page_values, preferred_element_type=F32)
    pooled = (
        (blended / totals[:, :, :, None])
        .transpose(0, 2, 1, 3)
        .reshape(img_count * lat_count, heads_res * RES_HEAD)
        .astype(BF)
    )
    return jnp.dot(pooled, wo_res, preferred_element_type=F32)


def flow_kernel(dims, *refs):
    n_x, n, count, sub, owners, shared, tight = dims
    (part_ref, lat_ref, gain_ref, img_ref, own_ref, text_ref, wq_ref, wk_ref, wv_ref, wo_ref) = refs[:10]
    out_ref, text, page_ref = refs[10:13]
    (wq, wkv, late, own_half, away_out, away_in, x_out, x_in, sq_half, sq_away_out, sq_away_in,
     sq_x_out, sq_x_in, query, keys, values, pages, lat_in, att, second, came, mixed_rows) = refs[13:35]
    (load_sem, text_sem, qc_send, qc_recv, qx_send, qx_recv, lat_send, lat_recv, pz_send, pz_recv,
     pg_send, pg_x, pg_core, side_sem, core_sem, block_sem, in_sem, back_sem, inward_sem,
     outward_sem, free_sem) = refs[35:]
    n_seq, half = 2 * n_x, n // 2
    cut = CUT if sub % (16 * CUT) == 0 else 1
    size, per = sub // cut, n_seq * cut
    total = count * per
    keep = own_half.shape[0]
    rows_all, rows_half = n_seq * sub, n_x * sub
    seq_me, me = lax.axis_index("seq"), lax.axis_index("tensor")
    core, x_me = seq_me % 2, seq_me // 2
    partner = 2 * x_me + 1 - core
    own = core * n_x + x_me
    side = me // half
    depth = me * (1 - side) + (n - 1 - me) * side
    inner, outer = me + 1 - 2 * side, me - 1 + 2 * side
    lag = LAG + 5 * (half - 1 - depth)
    feat, qwidth = wq.shape
    width = wo_ref.shape[1]
    heads = qwidth // HEAD
    scale = 1.0 / math.sqrt(HEAD)
    lat_rows = part_ref.shape[0]
    vis = part_ref.shape[1]
    part_rows = lat_rows // owners
    stride = n // owners
    wo = wkv if shared else late
    part = att if shared else second

    def remote(src, dst, sent, got, **where):
        return pltpu.make_async_remote_copy(
            src_ref=src, dst_ref=dst, send_sem=sent, recv_sem=got,
            device_id=where, device_id_type=pl.DeviceIdType.MESH,
        )

    def other_x(j):
        return (x_me + j) % n_x

    def other_z(j):
        return (me + j) % n

    def load_text(c):
        rows = pl.ds(pl.multiple_of(c * rows_all, rows_all), rows_all)
        return pltpu.make_async_copy(text_ref.at[rows], text.at[rows], text_sem.at[c])

    load_q = pltpu.make_async_copy(wq_ref, wq, load_sem.at[0])
    load_k = pltpu.make_async_copy(wk_ref, wkv.at[pl.ds(0, vis)], load_sem.at[1])
    load_v = pltpu.make_async_copy(wv_ref, wkv.at[pl.ds(vis, vis)], load_sem.at[2])
    load_o = pltpu.make_async_copy(wo_ref, wo.at[pl.ds(0, qwidth)], load_sem.at[3])

    def lat_piece(j):
        rows = pl.ds(j * part_rows, part_rows)
        return remote(
            part_ref.at[rows], lat_in.at[me], lat_send.at[j], lat_recv.at[me], tensor=j * stride
        )

    def page_rows(j):
        return pl.ds(pl.multiple_of(j * part_rows, part_rows), part_rows)

    def page_piece(j, z, k):
        ref = pages.at[seq_me, page_rows(j)]
        return remote(ref, ref, pz_send.at[k], pz_recv.at[j], tensor=z)

    def page_core(x, j, k):
        ref = pages.at[2 * x + core, page_rows(k)]
        return remote(ref, ref, pg_send.at[j, k], pg_core.at[x, k], seq=partner)

    def page_from_core(x, k):
        ref = pages.at[2 * x + 1 - core, page_rows(k)]
        return remote(ref, ref, pg_send.at[0, k], pg_core.at[x, k], seq=partner)

    def page_x(j, k):
        ref = pages.at[seq_me, page_rows(k)]
        return remote(
            ref, ref, pg_send.at[n_x + j - 1, k], pg_x.at[x_me, k], seq=2 * other_x(j) + core
        )

    def page_from_x(j, k):
        x = other_x(j)
        ref = pages.at[2 * x + core, page_rows(k)]
        return remote(ref, ref, pg_send.at[n_x + j - 1, k], pg_x.at[x, k], seq=2 * x + core)

    def away(c, which):
        src, dst = (away_out, away_in) if which == 0 else (sq_away_out, sq_away_in)
        return remote(
            src.at[c % RING], dst.at[c], qc_send.at[which, c % RING], qc_recv.at[which, c], seq=partner
        )

    def aside(c, j, which):
        src, dst = (x_out, x_in) if which == 0 else (sq_x_out, sq_x_in)
        return remote(
            src.at[c % RING, j - 1], dst.at[c, j - 1], qx_send.at[which, c % RING, j - 1],
            qx_recv.at[which, c, j - 1], seq=2 * other_x(j) + core,
        )

    def to_core(c, x, j):
        ref = att.at[c * n_seq + core * n_x + x]
        return remote(ref, ref, block_sem.at[c, j], core_sem.at[c, x], seq=partner)

    def from_core(c, x):
        ref = att.at[c * n_seq + (1 - core) * n_x + x]
        return remote(ref, ref, block_sem.at[c, 0], core_sem.at[c, x], seq=partner)

    def to_x(c, j):
        ref = att.at[c * n_seq + own]
        return remote(
            ref, ref, block_sem.at[c, n_x + j - 1], side_sem.at[c, x_me], seq=2 * other_x(j) + core
        )

    def from_x(c, j):
        x = other_x(j)
        ref = att.at[c * n_seq + core * n_x + x]
        return remote(ref, ref, block_sem.at[c, n_x + j - 1], side_sem.at[c, x], seq=2 * x + core)

    def rows_of(p):
        return pl.ds(pl.multiple_of(p * size, size), size)

    def piece(p):
        return part.at[p // cut, pl.ds(pl.multiple_of((p % cut) * size, size), size)]

    def landing(p):
        return (wq if tight else came).at[rows_of(p)]

    def inward(p):
        return remote(piece(p), landing(p), inward_sem.at[p], in_sem.at[p], tensor=inner)

    def across(p):
        return remote(
            piece(p), out_ref.at[rows_of(p)], inward_sem.at[p], back_sem.at[p], tensor=inner
        )

    def outward(p):
        ref = out_ref.at[rows_of(p)]
        return remote(ref, ref, outward_sem.at[p], back_sem.at[p], tensor=outer)

    def half_rows(which):
        return pl.ds(pl.multiple_of(which * rows_half, rows_half), rows_half)

    def strip(x):
        return pl.ds(pl.multiple_of(x * sub, sub), sub)

    def project(c):
        slot = c % RING
        load_text(c).wait()

        @pl.when(c >= RING)
        def _():
            for which in (0, 1):
                away(c - RING, which).wait_send()

        rows = jnp.concatenate(
            [text[half_rows(2 * c + 1 - core)], text[half_rows(2 * c + core)]], axis=0
        ).astype(F32)
        squares = rows * rows
        sums = squares[:, :128]
        for g in range(1, feat // 128):
            sums = sums + squares[:, g * 128 : (g + 1) * 128]
        sq_away_out[slot] = sums[:rows_half]
        sq_half[c] = sums[rows_half:]
        scaled = (rows * gain_ref[...].astype(F32)).astype(BF)
        tile = math.gcd(qwidth, 1024)
        for t in range(0, qwidth, tile):
            value = jnp.dot(scaled, wq[:, t : t + tile], preferred_element_type=F32)
            away_out[slot, :, t : t + tile] = value[:rows_half].astype(BF)
            own_half[c % keep, :, t : t + tile] = value[rows_half:]
        for which in (0, 1):
            away(c, which).start()

    def scatter(c):
        slot = c % RING
        for which in (0, 1):
            away(c, which).wait_recv()

        @pl.when(c >= RING)
        def _():
            for j in range(1, n_x):
                for which in (0, 1):
                    aside(c - RING, j, which).wait_send()

        for j in range(1, n_x):
            rows = strip(other_x(j))
            x_out[slot, j - 1] = (own_half[c % keep, rows] + away_in[c, rows].astype(F32)).astype(BF)
            sq_x_out[slot, j - 1] = sq_half[c, rows] + sq_away_in[c, rows]
            for which in (0, 1):
                aside(c, j, which).start()

    def finish(c):
        rows = strip(x_me)
        value = own_half[c % keep, rows] + away_in[c, rows].astype(F32)
        square = sq_half[c, rows] + sq_away_in[c, rows]
        for j in range(1, n_x):
            for which in (0, 1):
                aside(c, j, which).wait_recv()
            value = value + x_in[c, j - 1].astype(F32)
            square = square + sq_x_in[c, j - 1]
        mean = jnp.sum(square, axis=1, keepdims=True) / (feat * n_seq)
        query[...] = (value * lax.rsqrt(mean + 1e-05)).astype(BF)

    def attend(c):
        img = img_ref[strip(c)]
        allowed = img == own_ref[...]
        visible = (img >= 0).astype(F32)
        cuts = [slice(h * HEAD, (h + 1) * HEAD) for h in range(heads)]
        logits = [
            lax.dot_general(
                query[:, cut], keys[:, cut], (((1,), (1,)), ((), ())), preferred_element_type=F32
            )
            for cut in cuts
        ]
        logits = [jnp.where(allowed, value * scale, -1e30) for value in logits]
        peaks = [jnp.max(value, axis=1, keepdims=True) for value in logits]
        probs = [jnp.exp(value - peak).astype(BF) for value, peak in zip(logits, peaks)]
        weights = [jnp.sum(p.astype(F32), axis=1, keepdims=True) for p in probs]
        mixed = [
            jnp.dot(p, values[:, cut], preferred_element_type=F32) for p, cut in zip(probs, cuts)
        ]
        for value, weight, cut in zip(mixed, weights, cuts):
            att[c * n_seq + own, :, cut] = (value / weight * visible).astype(BF)
        for j in range(1, n_x):
            to_x(c, j).start()
        to_core(c, x_me, 0).start()

    def product(c, t):
        tile = width // TILES
        cols = slice(t * tile, (t + 1) * tile)
        rows = att[pl.ds(c * n_seq, n_seq)].reshape(rows_all, qwidth)
        value = jnp.dot(rows, wo[:qwidth, cols], preferred_element_type=F32)
        mixed_rows[:, cols] = value.astype(BF)

    def replace(c):
        for j in range(n_x):
            to_core(c, x_me, j).wait_send()
        for j in range(1, n_x):
            to_x(c, j).wait_send()
        for b in range(n_seq):
            part[c * n_seq + b] = mixed_rows[b * sub : (b + 1) * sub]

    def gather(p):
        @pl.when(depth > 0)
        def _():
            inward(p).wait_recv()
            piece(p)[...] = (piece(p)[...].astype(F32) + landing(p)[...].astype(F32)).astype(BF)

        @pl.when(depth < half - 1)
        def _():
            if tight:
                @pl.when(p == 0)
                def _():
                    pl.semaphore_wait(free_sem, 1)

            inward(p).start()

        @pl.when(depth == half - 1)
        def _():
            across(p).start()

    def spread(p):
        outward(p).wait_recv()

        @pl.when(depth == half - 1)
        def _():
            rows = rows_of(p)
            out_ref[rows] = (piece(p)[...].astype(F32) + out_ref[rows].astype(F32)).astype(BF)

        @pl.when(depth > 0)
        def _():
            outward(p).start()

    def sum_latents():
        @pl.when(me % stride == 0)
        def _():
            j = me // stride
            rows = page_rows(j)
            value = part_ref[rows]
            for k in range(1, n):
                z = other_z(k)
                remote(
                    part_ref.at[rows], lat_in.at[z], lat_send.at[0], lat_recv.at[z], tensor=z
                ).wait_recv()
                value = value + lat_in[z]
            base = (j * part_rows) % lat_ref.shape[0]
            mine = lat_ref[pl.ds(pl.multiple_of(base, part_rows), part_rows)].astype(F32)
            pages[seq_me, rows] = (mine + value).astype(BF)
            for k in range(1, n):
                page_piece(j, other_z(k), k - 1).start()

    def share_page():
        for k in range(owners):
            j = (me // stride + k) % owners

            @pl.when(me != j * stride)
            def _(j=j):
                page_piece(j, j * stride, 0).wait_recv()

            for i in range(1, n_x):
                page_x(i, j).start()
            page_core(x_me, 0, j).start()
        page_ref[...] = pages[seq_me]

    def pass_pages():
        for k in range(owners):
            j = (me // stride + k) % owners
            for i in range(1, n_x):
                page_from_x(i, j).wait_recv()
                page_core(other_x(i), i, j).start()

    def keys_values():
        load_k.wait()
        load_v.wait()
        for x in range(n_x):
            for k in range(owners):
                page_from_core(x, k).wait_recv()
        rows = pages[...].reshape(n_seq * lat_rows, vis)
        tile = math.gcd(qwidth, 1024)
        for base, target in ((0, keys), (vis, values)):
            @pl.loop(0, qwidth // tile)
            def _(t, base=base, target=target):
                cols = pl.ds(pl.multiple_of(t * tile, tile), tile)
                target[:, cols] = jnp.dot(
                    rows, wkv[base : base + vis, cols], preferred_element_type=F32
                ).astype(BF)
        if shared:
            load_o.start()

    load_text(0).start()
    load_q.start()
    for c in range(1, min(SOON, count)):
        load_text(c).start()
    barrier = pltpu.get_barrier_semaphore()

    def greet(**where):
        pl.semaphore_signal(barrier, inc=1, device_id=where, device_id_type=pl.DeviceIdType.MESH)

    greet(seq=partner)
    for j in range(1, n_x):
        greet(seq=2 * other_x(j) + core)
    for j in range(1, n):
        greet(tensor=other_z(j))
    pl.semaphore_wait(barrier, 1 + (n_x - 1) + (n - 1))

    for j in range(owners):
        @pl.when(me != j * stride)
        def _(j=j):
            lat_piece(j).start()

    load_q.wait()
    for c in range(SOON, count):
        load_text(c).start()
    load_k.start()
    load_v.start()
    if not shared:
        load_o.start()

    @pl.loop(0, count + LEAD + 2)
    def _(s):
        pl.when(s == SUM_STEP)(sum_latents)
        pl.when(s == PAGE_STEP)(share_page)
        pl.when(s == PASS_STEP)(pass_pages)

        @pl.when(s < count)
        def _():
            project(s)

            if tight:
                @pl.when(jnp.logical_and(s == count - 1, depth > 0))
                def _():
                    pl.semaphore_signal(
                        free_sem, inc=1, device_id={"tensor": outer},
                        device_id_type=pl.DeviceIdType.MESH,
                    )

        @pl.when(jnp.logical_and(s >= EARLY, s < EARLY + min(AHEAD, count)))
        def _():
            scatter(s - EARLY)

        c = s - LEAD - 1
        ready = jnp.logical_and(c >= 0, c < count)

        def pieces(low, high):
            @pl.when(c >= 1)
            def _():
                @pl.loop(low, high)
                def _(b):
                    p = (c - 1) * per + b
                    gather(p)

                    @pl.when(jnp.logical_and(depth > 0, p >= lag))
                    def _():
                        spread(p - lag)

        pieces(0, per // 2)

        @pl.when(ready)
        def _():
            for j in range(1, n_x):
                from_x(c, j).wait_recv()
                to_core(c, other_x(j), j).start()

        pl.when(s == LEAD)(keys_values)

        @pl.when(jnp.logical_and(s >= LEAD, s < LEAD + count))
        def _():
            finish(s - LEAD)
            attend(s - LEAD)

        @pl.when(jnp.logical_and(s >= LATER + AHEAD, s < LATER + count))
        def _():
            scatter(s - LATER)

        pl.when(c == 0)(load_o.wait)
        pieces(per // 2, 3 * per // 4)

        @pl.when(ready)
        def _():
            for x in range(n_x):
                from_core(c, x).wait_recv()
            product(c, 0)

        pieces(3 * per // 4, per)

        @pl.when(ready)
        def _():
            for t in range(1, TILES):
                product(c, t)
            replace(c)

    @pl.loop(0, total)
    def _(p):
        @pl.when(jnp.logical_or(depth == 0, p >= total - lag))
        def _():
            spread(p)

    @pl.loop(0, total)
    def _(p):
        across(p).wait_send()

        @pl.when(depth > 0)
        def _():
            outward(p).wait_send()

    for c in range(max(count - RING, 0), count):
        for which in (0, 1):
            away(c, which).wait_send()
            for j in range(1, n_x):
                aside(c, j, which).wait_send()
    for k in range(owners):
        for j in range(n_x):
            page_core(x_me, j, k).wait_send()
        for j in range(1, n_x):
            page_x(j, k).wait_send()
    for j in range(owners):
        @pl.when(me != j * stride)
        def _(j=j):
            lat_piece(j).wait_send()

    @pl.when(me % stride == 0)
    def _():
        for k in range(1, n):
            page_piece(me // stride, other_z(k), k - 1).wait_send()


def flow(partial_value, latents, gain, img, owner, text, wq, wk, wv, wo, n_x, n):
    n_seq = 2 * n_x
    tokens, feat = text.shape
    qwidth, width = wo.shape
    lat_rows, vis = partial_value.shape
    sub = math.gcd(tokens // n_seq, SUB)
    count = tokens // (n_seq * sub)
    blocks = count * n_seq
    pieces = blocks * (CUT if sub % (16 * CUT) == 0 else 1)
    owners = math.gcd(n, lat_rows // 16)
    shared = qwidth == width and qwidth <= 2 * vis
    tight = qwidth == width and tokens <= feat
    dma = pltpu.SemaphoreType.DMA
    vmem, anywhere = pl.BlockSpec(memory_space=pltpu.VMEM), pl.BlockSpec(memory_space=pltpu.HBM)
    others = max(n_x - 1, 1)
    half_rows = n_x * sub
    stay = [pltpu.with_memory_space_constraint(v, pltpu.HBM) for v in (text, wq, wk, wv, wo)]
    scratch = [
        ((feat, qwidth), BF),
        ((2 * vis, qwidth), BF),
        ((16, 128) if shared else (qwidth, width), BF),
        ((min(count, LEAD + 2), half_rows, qwidth), F32),
        ((RING, half_rows, qwidth), BF),
        ((count, half_rows, qwidth), BF),
        ((RING, others, sub, qwidth), BF),
        ((count, others, sub, qwidth), BF),
        ((count, half_rows, 128), F32),
        ((RING, half_rows, 128), F32),
        ((count, half_rows, 128), F32),
        ((RING, others, sub, 128), F32),
        ((count, others, sub, 128), F32),
        ((sub, qwidth), BF),
        ((n_seq * lat_rows, qwidth), BF),
        ((n_seq * lat_rows, qwidth), BF),
        ((n_seq, lat_rows, vis), BF),
        ((n, lat_rows // owners, vis), F32),
        ((blocks, sub, qwidth), BF),
        ((1, 16, 128) if shared else (blocks, sub, width), BF),
        ((16, 128) if tight else (tokens, width), BF),
        ((n_seq * sub, width), BF),
    ]
    return pl.pallas_call(
        functools.partial(flow_kernel, (n_x, n, count, sub, owners, shared, tight)),
        out_shape=(
            jax.ShapeDtypeStruct((tokens, width), BF),
            jax.ShapeDtypeStruct((tokens, feat), BF),
            jax.ShapeDtypeStruct((lat_rows, vis), BF),
        ),
        in_specs=[vmem] * 5 + [anywhere] * 5,
        out_specs=(vmem, vmem, vmem),
        scratch_shapes=[pltpu.VMEM(shape, kind) for shape, kind in scratch]
        + [
            dma((4,)),
            dma((count,)),
            dma((2, RING)),
            dma((2, count)),
            dma((2, RING, others)),
            dma((2, count, others)),
            dma((owners,)),
            dma((n,)),
            dma((n,)),
            dma((owners,)),
            dma((2 * n_x, owners)),
            dma((n_x, owners)),
            dma((n_x, owners)),
            dma((count, n_x)),
            dma((count, n_x)),
            dma((count, 2 * n_x - 1)),
        ]
        + [dma((pieces,))] * 4
        + [pltpu.SemaphoreType.REGULAR],
        compiler_params=pltpu.CompilerParams(
            collective_id=0, has_side_effects=True, vmem_limit_bytes=41984 << 10
        ),
        name="flow",
    )(partial_value, latents, gain, img, owner, *stay)


def close_kernel(rows, slots, text_ref, gate_ref, branch_ref, page_ref, out_ref, page_out, buf, sem, page_sem):
    steps = text_ref.shape[0] // rows
    gate = jnp.tanh(gate_ref[...])
    page = pltpu.make_async_copy(page_ref, page_out, page_sem)

    def put(i):
        return pltpu.make_async_copy(
            buf.at[i % slots], out_ref.at[pl.ds(i * rows, rows)], sem.at[i % slots]
        )

    page.start()

    @pl.loop(0, steps)
    def _(i):
        @pl.when(i >= slots)
        def _():
            put(i - slots).wait()

        at = pl.ds(pl.multiple_of(i * rows, rows), rows)
        buf[i % slots] = text_ref[at].astype(F32) + gate * branch_ref[at].astype(F32)
        put(i).start()

    @pl.loop(max(steps - slots, 0), steps)
    def _(i):
        put(i).wait()

    page.wait()


def close(text, gate, branch, page):
    tokens, width = text.shape
    rows = math.gcd(tokens, 64)
    slots = 8
    whole, anywhere = pl.BlockSpec(memory_space=pltpu.VMEM), pl.BlockSpec(memory_space=pl.ANY)
    return pl.pallas_call(
        functools.partial(close_kernel, rows, slots),
        out_shape=(
            jax.ShapeDtypeStruct((tokens, width), F32),
            jax.ShapeDtypeStruct(page.shape, page.dtype),
        ),
        in_specs=[whole] * 4,
        out_specs=(anywhere, anywhere),
        scratch_shapes=[
            pltpu.VMEM((slots, rows, width), F32),
            pltpu.SemaphoreType.DMA((slots,)),
            pltpu.SemaphoreType.DMA,
        ],
        compiler_params=pltpu.CompilerParams(vmem_limit_bytes=8 << 20),
        name="close",
    )(text, gate, branch, page)


def make_shards(n_seq, n_tensor):
    n_x = n_seq // 2

    def shards(
        patches,
        latents,
        wq_res,
        wk_res,
        wv_res,
        wo_res,
        text,
        norm_gain,
        wq_x,
        wk_x,
        wv_x,
        wo_x,
        gate_x,
        text_image,
    ):
        seq_me = lax.axis_index("seq")
        block = (seq_me % 2) * n_x + seq_me // 2
        lat_count = latents.shape[0]
        tokens = text.shape[0]
        sub = math.gcd(tokens // n_seq, SUB)
        img = lax.dynamic_index_in_dim(
            text_image.reshape(-1, n_seq, sub), block, 1, keepdims=False
        ).reshape(-1, 1)
        partial_value = resample(patches, latents, wq_res, wk_res, wv_res, wo_res)
        owner = jnp.arange(n_seq * partial_value.shape[0], dtype=jnp.int32) // lat_count
        branch, text, page_latents = flow(
            partial_value, latents, norm_gain[None, :], img, owner[None, :], text,
            wq_x, wk_x, wv_x, wo_x, n_x, n_tensor,
        )
        return close(text, gate_x[None, :], branch, page_latents)

    return shards


def solution(mesh):
    in_specs = (
        P(("groups", "seq"), None),
        P(),
        P(None, "tensor"),
        P(None, "tensor"),
        P(None, "tensor"),
        P("tensor", None),
        P("groups", "seq"),
        P("seq"),
        P("seq", "tensor"),
        P(None, "tensor"),
        P(None, "tensor"),
        P("tensor", "seq"),
        P("seq"),
        P("groups"),
    )
    out_specs = (P("groups", "seq"), P(("groups", "seq"), None))
    body = make_shards(mesh.shape["seq"], mesh.shape["tensor"])
    return jax.shard_map(body, mesh=mesh, in_specs=in_specs, out_specs=out_specs, check_vma=False)
```

```python
import functools
import math

import jax
import jax.numpy as jnp
from jax import lax
from jax.experimental import pallas as pl
from jax.experimental.pallas import tpu as pltpu
from jax.sharding import PartitionSpec as P

HEAD = 128
RES_HEAD = 96
PATCH_IMG = 257
SUB = 32
CUT = 2
TILES = 2
SOON = 2
LAG = 3
LEAD = 12
SUM_STEP, PAGE_STEP, PASS_STEP = 4, 7, 10
EARLY, AHEAD, LATER = 2, 2, 11
RING = 2
BF = jnp.bfloat16
F32 = jnp.float32


def flow_kernel(dims, *refs):
    n_x, n, count, sub, owners, shared, tight, roomy, windowed = dims
    (patch_hbm, lat_hbm, gain_hbm, img_hbm, wqr_hbm, wkr_hbm, wvr_hbm, wor_hbm,
     text_ref, wq_ref, wk_ref, wv_ref, wo_ref) = refs[:13]
    out_ref, text, page_ref = refs[13:16]
    (part_sum, part_ref, lat_ref, lat_own, gain_ref, img_ref, patch_ref, wqr, wkr, wvr, wor, wq, wkv, late, own_half, away_in, x_out, x_in, sq_half, sq_away_out, sq_away_in,
     sq_x_out, sq_x_in, query, keys, values, pages, lat_in, att, second, came, mixed_rows) = refs[16:48]
    (load_sem, res_sem, text_sem, qc_send, qc_recv, qx_send, qx_recv, lat_send, lat_recv, pz_send, pz_recv,
     pg_send, pg_x, pg_core, side_sem, core_sem, block_sem, in_sem, back_sem, inward_sem,
     outward_sem, free_sem) = refs[48:]
    n_seq, half = 2 * n_x, n // 2
    cut = CUT if sub % (16 * CUT) == 0 else 1
    size, per = sub // cut, n_seq * cut
    total = count * per
    keep = own_half.shape[0]
    rows_all, rows_half = n_seq * sub, n_x * sub
    seq_me, me = lax.axis_index("seq"), lax.axis_index("tensor")
    core, x_me = seq_me % 2, seq_me // 2
    partner = 2 * x_me + 1 - core
    own = core * n_x + x_me
    side = me // half
    depth = me * (1 - side) + (n - 1 - me) * side
    inner, outer = me + 1 - 2 * side, me - 1 + 2 * side
    lag = LAG + 5 * (half - 1 - depth)
    feat, qwidth = wq.shape
    width = wo_ref.shape[1]
    heads = qwidth // HEAD
    scale = 1.0 / math.sqrt(HEAD)
    lat_rows = part_ref.shape[0]
    vis = part_ref.shape[1]
    part_rows = lat_rows // owners
    stride = n // owners
    wo = wkv if shared else late
    if roomy:
        at = count * rows_all
        mixed_rows = wq.at[pl.ds(at, rows_all)]
        keys = wq.at[pl.ds(at + rows_all, n_seq * lat_rows)]
        query = wq.at[pl.ds(at + rows_all + n_seq * lat_rows, sub)]
    part = att if shared else second

    def remote(src, dst, sent, got, **where):
        return pltpu.make_async_remote_copy(
            src_ref=src, dst_ref=dst, send_sem=sent, recv_sem=got,
            device_id=where, device_id_type=pl.DeviceIdType.MESH,
        )

    def other_x(j):
        return (x_me + j) % n_x

    def other_z(j):
        return (me + j) % n

    def load_text(c):
        rows = pl.ds(pl.multiple_of(c * rows_all, rows_all), rows_all)
        return pltpu.make_async_copy(text_ref.at[rows], text.at[rows], text_sem.at[c])

    load_q = pltpu.make_async_copy(wq_ref, wq, load_sem.at[0])
    load_k = pltpu.make_async_copy(wk_ref, wkv.at[pl.ds(0, vis)], load_sem.at[1])
    load_v = pltpu.make_async_copy(wv_ref, wkv.at[pl.ds(vis, vis)], load_sem.at[2])
    load_o = pltpu.make_async_copy(wo_ref, wo.at[pl.ds(0, qwidth)], load_sem.at[3])

    res = wqr_hbm.shape[1]
    lat_count = lat_hbm.shape[0]
    if windowed:
        wqr, wkr, wvr = (wkv.at[pl.ds(0, vis), pl.ds(k * res, res)] for k in range(3))
        wor = wkv.at[pl.ds(vis, res), pl.ds(0, vis)]
        lat_ref = wkv.at[pl.ds(vis + res, lat_count), pl.ds(0, vis)]
    lat_from = (me // stride * part_rows) % lat_count
    load_own = pltpu.make_async_copy(
        lat_hbm.at[pl.ds(pl.multiple_of(lat_from, part_rows), part_rows)], lat_own, res_sem.at[8]
    )
    load_res = [
        pltpu.make_async_copy(src, dst, res_sem.at[k])
        for k, (src, dst) in enumerate((
            (lat_hbm, lat_ref), (wqr_hbm, wqr), (patch_hbm, patch_ref), (wkr_hbm, wkr),
            (wvr_hbm, wvr), (wor_hbm, wor), (gain_hbm, gain_ref), (img_hbm, img_ref),
        ))
    ]

    def resample():
        images = patch_ref.shape[0] // PATCH_IMG
        whole = PATCH_IMG // 128 * 128
        count_res = res // RES_HEAD
        inv_res = 1.0 / math.sqrt(RES_HEAD)
        load_res[0].wait()
        load_res[1].wait()
        lat_q = jnp.dot(lat_ref[...], wqr[...], preferred_element_type=F32).astype(BF).astype(F32)
        column = lax.broadcasted_iota(jnp.int32, (1, res), 1)
        inside = [
            jnp.logical_and(column >= h * RES_HEAD, column < (h + 1) * RES_HEAD)
            for h in range(count_res)
        ]
        stacked = jnp.concatenate([jnp.where(m, lat_q, 0.0) for m in inside], axis=0)
        packed = stacked.astype(BF)
        for k in range(2, 6):
            load_res[k].wait()
        for i in range(images):
            base = i * PATCH_IMG
            spans = [(base, whole)] + [(base + r, 1) for r in range(whole, PATCH_IMG)]

            def both(w):
                return [
                    jnp.dot(patch_ref[at : at + rows], w[...], preferred_element_type=F32).astype(BF)
                    for at, rows in spans
                ]

            page_k, page_v = both(wkr), both(wvr)
            scores = lax.dot_general(
                packed, page_k[0], (((1,), (1,)), ((), ())), preferred_element_type=F32
            ) * inv_res
            extra = [
                jnp.sum(stacked * row.astype(F32), axis=1, keepdims=True) * inv_res
                for row in page_k[1:]
            ]
            summit = jnp.max(scores, axis=1, keepdims=True)
            for more in extra:
                summit = jnp.maximum(summit, more)
            weights = jnp.exp(scores - summit).astype(BF)
            sums = jnp.sum(weights.astype(F32), axis=1, keepdims=True)
            blended = jnp.dot(weights, page_v[0], preferred_element_type=F32)
            for more, row in zip(extra, page_v[1:]):
                weight = jnp.exp(more - summit).astype(BF).astype(F32)
                sums = sums + weight
                blended = blended + weight * row.astype(F32)
            blended = blended / sums
            pooled = jnp.zeros((lat_count, res), F32)
            for h, m in enumerate(inside):
                pooled = jnp.where(m, blended[h * lat_count : (h + 1) * lat_count], pooled)
            value = jnp.dot(pooled.astype(BF), wor[...], preferred_element_type=F32)
            part_sum[i * lat_count : (i + 1) * lat_count] = value
            part_ref[i * lat_count : (i + 1) * lat_count] = value.astype(BF)

    def lat_piece(j):
        rows = pl.ds(j * part_rows, part_rows)
        return remote(
            part_ref.at[rows], lat_in.at[me], lat_send.at[j], lat_recv.at[me], tensor=j * stride
        )

    def page_rows(j):
        return pl.ds(pl.multiple_of(j * part_rows, part_rows), part_rows)

    def page_piece(j, z, k):
        ref = pages.at[seq_me, page_rows(j)]
        return remote(ref, ref, pz_send.at[k], pz_recv.at[j], tensor=z)

    def page_core(x, j, k):
        ref = pages.at[2 * x + core, page_rows(k)]
        return remote(ref, ref, pg_send.at[j, k], pg_core.at[x, k], seq=partner)

    def page_from_core(x, k):
        ref = pages.at[2 * x + 1 - core, page_rows(k)]
        return remote(ref, ref, pg_send.at[0, k], pg_core.at[x, k], seq=partner)

    def page_x(j, k):
        ref = pages.at[seq_me, page_rows(k)]
        return remote(
            ref, ref, pg_send.at[n_x + j - 1, k], pg_x.at[x_me, k], seq=2 * other_x(j) + core
        )

    def page_from_x(j, k):
        x = other_x(j)
        ref = pages.at[2 * x + core, page_rows(k)]
        return remote(ref, ref, pg_send.at[n_x + j - 1, k], pg_x.at[x, k], seq=2 * x + core)

    def outgoing(c):
        return (count - 1) * n_seq + (c % RING) * n_x

    def away(c, which):
        if which == 0:
            src, dst = att.at[pl.ds(outgoing(c), n_x)], away_in
        else:
            src, dst = sq_away_out.at[c % RING], sq_away_in
        return remote(
            src, dst.at[c], qc_send.at[which, c % RING], qc_recv.at[which, c], seq=partner
        )

    def aside(c, j, which):
        src, dst = (x_out, x_in) if which == 0 else (sq_x_out, sq_x_in)
        return remote(
            src.at[c % RING, j - 1], dst.at[c, j - 1], qx_send.at[which, c % RING, j - 1],
            qx_recv.at[which, c, j - 1], seq=2 * other_x(j) + core,
        )

    def to_core(c, x, j):
        ref = att.at[c * n_seq + core * n_x + x]
        return remote(ref, ref, block_sem.at[c, j], core_sem.at[c, x], seq=partner)

    def from_core(c, x):
        ref = att.at[c * n_seq + (1 - core) * n_x + x]
        return remote(ref, ref, block_sem.at[c, 0], core_sem.at[c, x], seq=partner)

    def to_x(c, j):
        ref = att.at[c * n_seq + own]
        return remote(
            ref, ref, block_sem.at[c, n_x + j - 1], side_sem.at[c, x_me], seq=2 * other_x(j) + core
        )

    def from_x(c, j):
        x = other_x(j)
        ref = att.at[c * n_seq + core * n_x + x]
        return remote(ref, ref, block_sem.at[c, n_x + j - 1], side_sem.at[c, x], seq=2 * x + core)

    def rows_of(p):
        return pl.ds(pl.multiple_of(p * size, size), size)

    def piece(p):
        return part.at[p // cut, pl.ds(pl.multiple_of((p % cut) * size, size), size)]

    def landing(p):
        return (wq if tight else came).at[rows_of(p)]

    def inward(p):
        return remote(piece(p), landing(p), inward_sem.at[p], in_sem.at[p], tensor=inner)

    def across(p):
        return remote(
            piece(p), out_ref.at[rows_of(p)], inward_sem.at[p], back_sem.at[p], tensor=inner
        )

    def outward(p):
        ref = out_ref.at[rows_of(p)]
        return remote(ref, ref, outward_sem.at[p], back_sem.at[p], tensor=outer)

    def half_rows(which):
        return pl.ds(pl.multiple_of(which * rows_half, rows_half), rows_half)

    def strip(x):
        return pl.ds(pl.multiple_of(x * sub, sub), sub)

    def project(c):
        slot = c % RING
        load_text(c).wait()

        @pl.when(c >= RING)
        def _():
            for which in (0, 1):
                away(c - RING, which).wait_send()

        rows = jnp.concatenate(
            [text[half_rows(2 * c + 1 - core)], text[half_rows(2 * c + core)]], axis=0
        ).astype(F32)
        squares = rows * rows
        groups = [slice(g * 128, (g + 1) * 128) for g in range(feat // 128)]
        sums = squares[:, groups[0]]
        for group in groups[1:]:
            sums = sums + squares[:, group]
        sq_away_out[slot] = sums[:rows_half]
        sq_half[c] = sums[rows_half:]
        gain = gain_ref[...].astype(F32)
        scaled = jnp.concatenate(
            [(rows[:, group] * gain[g : g + 1]).astype(BF) for g, group in enumerate(groups)], axis=1
        )
        tile = math.gcd(qwidth, 1024)
        for t in range(0, qwidth, tile):
            value = jnp.dot(scaled, wq[:, t : t + tile], preferred_element_type=F32)
            for x in range(n_x):
                att[outgoing(c) + x, :, t : t + tile] = value[x * sub : (x + 1) * sub].astype(BF)
            own_half[c % keep, :, t : t + tile] = value[rows_half:]
        for which in (0, 1):
            away(c, which).start()

    def scatter(c):
        slot = c % RING
        for which in (0, 1):
            away(c, which).wait_recv()

        @pl.when(c >= RING)
        def _():
            for j in range(1, n_x):
                for which in (0, 1):
                    aside(c - RING, j, which).wait_send()

        for j in range(1, n_x):
            rows = strip(other_x(j))
            x_out[slot, j - 1] = (own_half[c % keep, rows] + away_in[c, other_x(j)].astype(F32)).astype(BF)
            sq_x_out[slot, j - 1] = sq_half[c, rows] + sq_away_in[c, rows]
            for which in (0, 1):
                aside(c, j, which).start()

    def finish(c):
        rows = strip(x_me)
        value = own_half[c % keep, rows] + away_in[c, x_me].astype(F32)
        square = sq_half[c, rows] + sq_away_in[c, rows]
        for j in range(1, n_x):
            for which in (0, 1):
                aside(c, j, which).wait_recv()
            value = value + x_in[c, j - 1].astype(F32)
            square = square + sq_x_in[c, j - 1]
        mean = jnp.sum(square, axis=1, keepdims=True) / (feat * n_seq)
        query[...] = (value * lax.rsqrt(mean + 1e-05)).astype(BF)

    def attend(c):
        line = jnp.broadcast_to(img_ref[pl.ds(c, 1)], (sub, rows_all)).astype(F32)
        lane = lax.broadcasted_iota(jnp.int32, (sub, rows_all), 1)
        token = lax.broadcasted_iota(jnp.int32, (sub, rows_all), 0) + own * sub
        img = jnp.sum(jnp.where(lane == token, line, 0.0), axis=1, keepdims=True)
        slot = lax.broadcasted_iota(jnp.int32, (1, n_seq * lat_rows), 1)
        owner = lax.div(slot, jnp.int32(lat_count)).astype(F32)
        allowed = img == owner
        visible = (img >= 0).astype(F32)
        cuts = [slice(h * HEAD, (h + 1) * HEAD) for h in range(heads)]
        logits = [
            lax.dot_general(
                query[:, cut], keys[:, cut], (((1,), (1,)), ((), ())), preferred_element_type=F32
            )
            for cut in cuts
        ]
        logits = [jnp.where(allowed, value * scale, -1e30) for value in logits]
        peaks = [jnp.max(value, axis=1, keepdims=True) for value in logits]
        probs = [jnp.exp(value - peak).astype(BF) for value, peak in zip(logits, peaks)]
        weights = [jnp.sum(p.astype(F32), axis=1, keepdims=True) for p in probs]
        mixed = [
            jnp.dot(p, values[:, cut], preferred_element_type=F32) for p, cut in zip(probs, cuts)
        ]
        for value, weight, cut in zip(mixed, weights, cuts):
            att[c * n_seq + own, :, cut] = (value / weight * visible).astype(BF)
        for j in range(1, n_x):
            to_x(c, j).start()
        to_core(c, x_me, 0).start()

    def product(c, t):
        tile = width // TILES
        cols = slice(t * tile, (t + 1) * tile)
        rows = att[pl.ds(c * n_seq, n_seq)].reshape(rows_all, qwidth)
        value = jnp.dot(rows, wo[:qwidth, cols], preferred_element_type=F32)
        mixed_rows[:, cols] = value.astype(BF)

    def replace(c):
        for j in range(n_x):
            to_core(c, x_me, j).wait_send()
        for j in range(1, n_x):
            to_x(c, j).wait_send()
        for b in range(n_seq):
            part[c * n_seq + b] = mixed_rows[b * sub : (b + 1) * sub]

    def gather(p):
        @pl.when(depth > 0)
        def _():
            inward(p).wait_recv()
            piece(p)[...] = (piece(p)[...].astype(F32) + landing(p)[...].astype(F32)).astype(BF)

        @pl.when(depth < half - 1)
        def _():
            if tight:
                @pl.when(p == 0)
                def _():
                    pl.semaphore_wait(free_sem, 1)

            inward(p).start()

        @pl.when(depth == half - 1)
        def _():
            across(p).start()

    def spread(p):
        outward(p).wait_recv()

        @pl.when(depth == half - 1)
        def _():
            rows = rows_of(p)
            out_ref[rows] = (piece(p)[...].astype(F32) + out_ref[rows].astype(F32)).astype(BF)

        @pl.when(depth > 0)
        def _():
            outward(p).start()

    def sum_latents():
        @pl.when(me % stride == 0)
        def _():
            j = me // stride
            rows = page_rows(j)
            value = part_sum[rows]
            for k in range(1, n):
                z = other_z(k)
                remote(
                    part_ref.at[rows], lat_in.at[z], lat_send.at[0], lat_recv.at[z], tensor=z
                ).wait_recv()
                value = value + lat_in[z].astype(F32)
            pages[seq_me, rows] = (lat_own[...].astype(F32) + value).astype(BF)
            for k in range(1, n):
                page_piece(j, other_z(k), k - 1).start()

    def share_page():
        for k in range(owners):
            j = (me // stride + k) % owners

            @pl.when(me != j * stride)
            def _(j=j):
                page_piece(j, j * stride, 0).wait_recv()

            for i in range(1, n_x):
                page_x(i, j).start()
            page_core(x_me, 0, j).start()
        page_ref[...] = pages[seq_me]

    def pass_pages():
        for k in range(owners):
            j = (me // stride + k) % owners
            for i in range(1, n_x):
                page_from_x(i, j).wait_recv()
                page_core(other_x(i), i, j).start()

    def keys_values():
        for c in range(max(count - RING, 0), count):
            for which in (0, 1):
                away(c, which).wait_send()
        load_k.wait()
        load_v.wait()
        for x in range(n_x):
            for k in range(owners):
                page_from_core(x, k).wait_recv()
        rows = pages[...].reshape(n_seq * lat_rows, vis)
        tile = math.gcd(qwidth, 1024)
        for base, target in ((0, keys), (vis, values)):
            for t in range(0, qwidth, tile):
                target[:, t : t + tile] = jnp.dot(
                    rows, wkv[base : base + vis, t : t + tile], preferred_element_type=F32
                ).astype(BF)
        if shared:
            load_o.start()

    for load in (*load_res, load_own):
        load.start()

    barrier = pltpu.get_barrier_semaphore()

    def greet(**where):
        pl.semaphore_signal(barrier, inc=1, device_id=where, device_id_type=pl.DeviceIdType.MESH)

    greet(seq=partner)
    for j in range(1, n_x):
        greet(seq=2 * other_x(j) + core)
    for j in range(1, n):
        greet(tensor=other_z(j))
    for load in (load_res[6], load_res[7], load_own):
        load.wait()
    load_text(0).start()
    load_q.start()
    for c in range(1, min(SOON, count)):
        load_text(c).start()
    resample()
    pl.semaphore_wait(barrier, 1 + (n_x - 1) + (n - 1))

    for j in range(owners):
        @pl.when(me != j * stride)
        def _(j=j):
            lat_piece(j).start()

    load_q.wait()
    for c in range(SOON, count):
        load_text(c).start()
    load_k.start()
    load_v.start()
    if not shared:
        load_o.start()

    @pl.loop(0, count + LEAD + 2)
    def _(s):
        pl.when(s == SUM_STEP)(sum_latents)
        pl.when(s == PAGE_STEP)(share_page)
        pl.when(s == PASS_STEP)(pass_pages)

        @pl.when(s < count)
        def _():
            project(s)

            if tight:
                @pl.when(jnp.logical_and(s == count - 1, depth > 0))
                def _():
                    pl.semaphore_signal(
                        free_sem, inc=1, device_id={"tensor": outer},
                        device_id_type=pl.DeviceIdType.MESH,
                    )

        @pl.when(jnp.logical_and(s >= EARLY, s < EARLY + min(AHEAD, count)))
        def _():
            scatter(s - EARLY)

        c = s - LEAD - 1
        ready = jnp.logical_and(c >= 0, c < count)

        def pieces(low, high):
            @pl.when(c >= 1)
            def _():
                @pl.loop(low, high)
                def _(b):
                    p = (c - 1) * per + b
                    gather(p)

                    @pl.when(jnp.logical_and(depth > 0, p >= lag))
                    def _():
                        spread(p - lag)

        pieces(0, per // 2)

        @pl.when(ready)
        def _():
            for j in range(1, n_x):
                from_x(c, j).wait_recv()
                to_core(c, other_x(j), j).start()

        pl.when(s == LEAD)(keys_values)

        @pl.when(jnp.logical_and(s >= LEAD, s < LEAD + count))
        def _():
            finish(s - LEAD)
            attend(s - LEAD)

        @pl.when(jnp.logical_and(s >= LATER + AHEAD, s < LATER + count))
        def _():
            scatter(s - LATER)

        pl.when(c == 0)(load_o.wait)
        pieces(per // 2, 3 * per // 4)

        @pl.when(ready)
        def _():
            for x in range(n_x):
                from_core(c, x).wait_recv()
            product(c, 0)

        pieces(3 * per // 4, per)

        @pl.when(ready)
        def _():
            for t in range(1, TILES):
                product(c, t)
            replace(c)

    @pl.loop(0, total)
    def _(p):
        @pl.when(jnp.logical_or(depth == 0, p >= total - lag))
        def _():
            spread(p)

    @pl.loop(0, total)
    def _(p):
        across(p).wait_send()

        @pl.when(depth > 0)
        def _():
            outward(p).wait_send()

    for c in range(max(count - RING, 0), count):
        for which in (0, 1):
            for j in range(1, n_x):
                aside(c, j, which).wait_send()
    for k in range(owners):
        for j in range(n_x):
            page_core(x_me, j, k).wait_send()
        for j in range(1, n_x):
            page_x(j, k).wait_send()
    for j in range(owners):
        @pl.when(me != j * stride)
        def _(j=j):
            lat_piece(j).wait_send()

    @pl.when(me % stride == 0)
    def _():
        for k in range(1, n):
            page_piece(me // stride, other_z(k), k - 1).wait_send()


def flow(patches, latents, gain, text_image, wq_res, wk_res, wv_res, wo_res, text, wq, wk, wv, wo, n_x, n):
    n_seq = 2 * n_x
    tokens, feat = text.shape
    qwidth, width = wo.shape
    vis = patches.shape[1]
    lat_rows = patches.shape[0] // PATCH_IMG * latents.shape[0]
    sub = math.gcd(tokens // n_seq, SUB)
    count = tokens // (n_seq * sub)
    blocks = count * n_seq
    pieces = blocks * (CUT if sub % (16 * CUT) == 0 else 1)
    owners = math.gcd(n, lat_rows // 16)
    shared = qwidth == width and qwidth <= 2 * vis
    tight = qwidth == width and tokens <= feat
    roomy = tight and tokens + n_seq * (sub + lat_rows) + sub <= feat
    dma = pltpu.SemaphoreType.DMA
    vmem, anywhere = pl.BlockSpec(memory_space=pltpu.VMEM), pl.BlockSpec(memory_space=pltpu.HBM)
    others = max(n_x - 1, 1)
    half_rows = n_x * sub
    gain, img = gain.reshape(-1, 128), text_image.reshape(count, -1)
    res = wo_res.shape[0]
    windowed = (
        res % 128 == 0 and 3 * res <= qwidth and vis <= qwidth and res + latents.shape[0] <= vis
    )
    stay = [
        pltpu.with_memory_space_constraint(value, pltpu.HBM)
        for value in (
            patches, latents, gain, img, wq_res, wk_res, wv_res, wo_res, text, wq, wk, wv, wo
        )
    ]
    scratch = [
        ((lat_rows, vis), F32),
        ((lat_rows, vis), BF),
        ((16, 128) if windowed else latents.shape, BF),
        ((lat_rows // owners, vis), BF),
        (gain.shape, BF),
        (img.shape, jnp.int32),
        (patches.shape, BF),
        *(
            ((16, 128) if windowed else value.shape, BF)
            for value in (wq_res, wk_res, wv_res, wo_res)
        ),
        ((feat, qwidth), BF),
        ((2 * vis, qwidth), BF),
        ((16, 128) if shared else (qwidth, width), BF),
        ((min(count, LEAD + 2), half_rows, qwidth), F32),
        ((count, n_x, sub, qwidth), BF),
        ((RING, others, sub, qwidth), BF),
        ((count, others, sub, qwidth), BF),
        ((count, half_rows, 128), F32),
        ((RING, half_rows, 128), F32),
        ((count, half_rows, 128), F32),
        ((RING, others, sub, 128), F32),
        ((count, others, sub, 128), F32),
        ((16, 128) if roomy else (sub, qwidth), BF),
        ((16, 128) if roomy else (n_seq * lat_rows, qwidth), BF),
        ((n_seq * lat_rows, qwidth), BF),
        ((n_seq, lat_rows, vis), BF),
        ((n, lat_rows // owners, vis), BF),
        ((blocks, sub, qwidth), BF),
        ((1, 16, 128) if shared else (blocks, sub, width), BF),
        ((16, 128) if tight else (tokens, width), BF),
        ((16, 128) if roomy else (n_seq * sub, width), BF),
    ]
    return pl.pallas_call(
        functools.partial(flow_kernel, (n_x, n, count, sub, owners, shared, tight, roomy, windowed)),
        out_shape=(
            jax.ShapeDtypeStruct((tokens, width), BF),
            jax.ShapeDtypeStruct((tokens, feat), BF),
            jax.ShapeDtypeStruct((lat_rows, vis), BF),
        ),
        in_specs=[anywhere] * len(stay),
        out_specs=(vmem, vmem, vmem),
        scratch_shapes=[pltpu.VMEM(shape, kind) for shape, kind in scratch]
        + [
            dma((4,)),
            dma((9,)),
            dma((count,)),
            dma((2, RING)),
            dma((2, count)),
            dma((2, RING, others)),
            dma((2, count, others)),
            dma((owners,)),
            dma((n,)),
            dma((n,)),
            dma((owners,)),
            dma((2 * n_x, owners)),
            dma((n_x, owners)),
            dma((n_x, owners)),
            dma((count, n_x)),
            dma((count, n_x)),
            dma((count, 2 * n_x - 1)),
        ]
        + [dma((pieces,))] * 4
        + [pltpu.SemaphoreType.REGULAR],
        compiler_params=pltpu.CompilerParams(
            collective_id=0, has_side_effects=True, vmem_limit_bytes=41984 << 10
        ),
        name="flow",
    )(*stay)


def close_kernel(rows, slots, text_ref, gate_ref, branch_ref, page_ref, out_ref, page_out, buf, sem, page_sem):
    steps = text_ref.shape[0] // rows
    gate = jnp.tanh(gate_ref[...])
    page = pltpu.make_async_copy(page_ref, page_out, page_sem)

    def put(i):
        return pltpu.make_async_copy(
            buf.at[i % slots], out_ref.at[pl.ds(i * rows, rows)], sem.at[i % slots]
        )

    page.start()

    @pl.loop(0, steps)
    def _(i):
        @pl.when(i >= slots)
        def _():
            put(i - slots).wait()

        at = pl.ds(pl.multiple_of(i * rows, rows), rows)
        buf[i % slots] = text_ref[at].astype(F32) + gate * branch_ref[at].astype(F32)
        put(i).start()

    @pl.loop(max(steps - slots, 0), steps)
    def _(i):
        put(i).wait()

    page.wait()


def close(text, gate, branch, page):
    tokens, width = text.shape
    rows = math.gcd(tokens, 64)
    slots = 8
    whole, anywhere = pl.BlockSpec(memory_space=pltpu.VMEM), pl.BlockSpec(memory_space=pl.ANY)
    return pl.pallas_call(
        functools.partial(close_kernel, rows, slots),
        out_shape=(
            jax.ShapeDtypeStruct((tokens, width), F32),
            jax.ShapeDtypeStruct(page.shape, page.dtype),
        ),
        in_specs=[whole] * 4,
        out_specs=(anywhere, anywhere),
        scratch_shapes=[
            pltpu.VMEM((slots, rows, width), F32),
            pltpu.SemaphoreType.DMA((slots,)),
            pltpu.SemaphoreType.DMA,
        ],
        compiler_params=pltpu.CompilerParams(vmem_limit_bytes=8 << 20),
        name="close",
    )(text, gate, branch, page)


def make_shards(n_seq, n_tensor):
    n_x = n_seq // 2

    def shards(
        patches,
        latents,
        wq_res,
        wk_res,
        wv_res,
        wo_res,
        text,
        norm_gain,
        wq_x,
        wk_x,
        wv_x,
        wo_x,
        gate_x,
        text_image,
    ):
        branch, text, page_latents = flow(
            patches, latents, norm_gain, text_image, wq_res, wk_res, wv_res, wo_res, text,
            wq_x, wk_x, wv_x, wo_x, n_x, n_tensor,
        )
        return close(text, gate_x[None, :], branch, page_latents)

    return shards


def solution(mesh):
    in_specs = (
        P(("groups", "seq"), None),
        P(),
        P(None, "tensor"),
        P(None, "tensor"),
        P(None, "tensor"),
        P("tensor", None),
        P("groups", "seq"),
        P("seq"),
        P("seq", "tensor"),
        P(None, "tensor"),
        P(None, "tensor"),
        P("tensor", "seq"),
        P("seq"),
        P("groups"),
    )
    out_specs = (P("groups", "seq"), P(("groups", "seq"), None))
    body = make_shards(mesh.shape["seq"], mesh.shape["tensor"])
    return jax.shard_map(body, mesh=mesh, in_specs=in_specs, out_specs=out_specs, check_vma=False)
```

```python
import functools
import math

import jax
import jax.numpy as jnp
from jax import lax
from jax.experimental import pallas as pl
from jax.experimental.pallas import tpu as pltpu
from jax.sharding import PartitionSpec as P

HEAD = 128
RES_HEAD = 96
PATCH_IMG = 257
SUB = 32
CUT = 2
TILES = 2
SOON = 2
LAG, SHORT = 4, 2
LEAD = 10
SUM_STEP, PAGE_STEP, PASS_STEP = 3, 6, 9
EARLY, AHEAD, LATER = 1, 2, 9
RING = 2
BF = jnp.bfloat16
F32 = jnp.float32


def flow_kernel(dims, *refs):
    n_x, n, count, sub, owners, shared, tight, roomy, windowed = dims
    (patch_hbm, lat_hbm, gain_hbm, img_hbm, wqr_hbm, wkr_hbm, wvr_hbm, wor_hbm,
     text_ref, wq_ref, wk_ref, wv_ref, wo_ref) = refs[:13]
    out_ref, text, page_ref = refs[13:16]
    (part_sum, part_ref, lat_ref, lat_own, gain_ref, img_ref, patch_ref, wqr, wkr, wvr, wor, wq, wkv, late, own_half, away_in, x_out, x_in, sq_half, sq_away_out, sq_away_in,
     sq_x_out, sq_x_in, query, keys, values, pages, lat_in, att, second, came, mixed_rows) = refs[16:48]
    (load_sem, res_sem, text_sem, qc_send, qc_recv, qx_send, qx_recv, lat_send, lat_recv, pz_send, pz_recv,
     pg_send, pg_x, pg_core, side_sem, core_sem, block_sem, in_sem, back_sem, inward_sem,
     outward_sem, free_sem) = refs[48:]
    n_seq, half = 2 * n_x, n // 2
    cut = CUT if sub % (16 * CUT) == 0 else 1
    size, per = sub // cut, n_seq * cut
    total = count * per
    keep = own_half.shape[0]
    rows_all, rows_half = n_seq * sub, n_x * sub
    seq_me, me = lax.axis_index("seq"), lax.axis_index("tensor")
    core, x_me = seq_me % 2, seq_me // 2
    partner = 2 * x_me + 1 - core
    own = core * n_x + x_me
    side = me // half
    depth = me * (1 - side) + (n - 1 - me) * side
    inner, outer = me + 1 - 2 * side, me - 1 + 2 * side
    lag = LAG + 5 * (half - 1 - depth)
    feat, qwidth = wq.shape
    width = wo_ref.shape[1]
    heads = qwidth // HEAD
    scale = 1.0 / math.sqrt(HEAD)
    lat_rows = part_ref.shape[0]
    vis = part_ref.shape[1]
    part_rows = lat_rows // owners
    stride = n // owners
    wo = wkv if shared else late
    if roomy:
        keys = wkv.at[pl.ds(qwidth, n_seq * lat_rows)]
        mixed_rows = wkv.at[pl.ds(qwidth + n_seq * lat_rows, rows_all)]
        query = wkv.at[pl.ds(qwidth + n_seq * lat_rows + rows_all, sub)]
    part = att if shared else second

    def remote(src, dst, sent, got, **where):
        return pltpu.make_async_remote_copy(
            src_ref=src, dst_ref=dst, send_sem=sent, recv_sem=got,
            device_id=where, device_id_type=pl.DeviceIdType.MESH,
        )

    def other_x(j):
        return (x_me + j) % n_x

    def other_z(j):
        return (me + j) % n

    def load_text(c):
        rows = pl.ds(pl.multiple_of(c * rows_all, rows_all), rows_all)
        return pltpu.make_async_copy(text_ref.at[rows], text.at[rows], text_sem.at[c])

    load_q = pltpu.make_async_copy(wq_ref, wq, load_sem.at[0])
    load_k = pltpu.make_async_copy(wk_ref, wkv.at[pl.ds(0, vis)], load_sem.at[1])
    load_v = pltpu.make_async_copy(wv_ref, wkv.at[pl.ds(vis, vis)], load_sem.at[2])
    load_o = pltpu.make_async_copy(wo_ref, wo.at[pl.ds(0, qwidth)], load_sem.at[3])

    res = wqr_hbm.shape[1]
    lat_count = lat_hbm.shape[0]
    if windowed:
        wqr, wkr, wvr = (wkv.at[pl.ds(0, vis), pl.ds(k * res, res)] for k in range(3))
        wor = wkv.at[pl.ds(vis, res), pl.ds(0, vis)]
        lat_ref = wkv.at[pl.ds(vis + res, lat_count), pl.ds(0, vis)]
    lat_from = (me // stride * part_rows) % lat_count
    load_own = pltpu.make_async_copy(
        lat_hbm.at[pl.ds(pl.multiple_of(lat_from, part_rows), part_rows)], lat_own, res_sem.at[8]
    )
    load_res = [
        pltpu.make_async_copy(src, dst, res_sem.at[k])
        for k, (src, dst) in enumerate((
            (lat_hbm, lat_ref), (wqr_hbm, wqr), (patch_hbm, patch_ref), (wkr_hbm, wkr),
            (wvr_hbm, wvr), (wor_hbm, wor), (gain_hbm, gain_ref), (img_hbm, img_ref),
        ))
    ]

    def resample():
        images = patch_ref.shape[0] // PATCH_IMG
        whole = PATCH_IMG // 128 * 128
        count_res = res // RES_HEAD
        inv_res = 1.0 / math.sqrt(RES_HEAD)
        load_res[0].wait()
        load_res[1].wait()
        lat_q = jnp.dot(lat_ref[...], wqr[...], preferred_element_type=F32).astype(BF).astype(F32)
        column = lax.broadcasted_iota(jnp.int32, (1, res), 1)
        inside = [
            jnp.logical_and(column >= h * RES_HEAD, column < (h + 1) * RES_HEAD)
            for h in range(count_res)
        ]
        stacked = jnp.concatenate([jnp.where(m, lat_q, 0.0) for m in inside], axis=0)
        packed = stacked.astype(BF)
        for k in range(2, 6):
            load_res[k].wait()
        for i in range(images):
            base = i * PATCH_IMG
            spans = [(base, whole)] + [(base + r, 1) for r in range(whole, PATCH_IMG)]

            def both(w):
                return [
                    jnp.dot(patch_ref[at : at + rows], w[...], preferred_element_type=F32).astype(BF)
                    for at, rows in spans
                ]

            page_k, page_v = both(wkr), both(wvr)
            scores = lax.dot_general(
                packed, page_k[0], (((1,), (1,)), ((), ())), preferred_element_type=F32
            ) * inv_res
            extra = [
                jnp.sum(stacked * row.astype(F32), axis=1, keepdims=True) * inv_res
                for row in page_k[1:]
            ]
            summit = jnp.max(scores, axis=1, keepdims=True)
            for more in extra:
                summit = jnp.maximum(summit, more)
            weights = jnp.exp(scores - summit).astype(BF)
            sums = jnp.sum(weights.astype(F32), axis=1, keepdims=True)
            blended = jnp.dot(weights, page_v[0], preferred_element_type=F32)
            for more, row in zip(extra, page_v[1:]):
                weight = jnp.exp(more - summit).astype(BF).astype(F32)
                sums = sums + weight
                blended = blended + weight * row.astype(F32)
            blended = blended / sums
            pooled = jnp.zeros((lat_count, res), F32)
            for h, m in enumerate(inside):
                pooled = jnp.where(m, blended[h * lat_count : (h + 1) * lat_count], pooled)
            value = jnp.dot(pooled.astype(BF), wor[...], preferred_element_type=F32)
            part_sum[i * lat_count : (i + 1) * lat_count] = value
            part_ref[i * lat_count : (i + 1) * lat_count] = value.astype(BF)

    def lat_piece(j):
        rows = pl.ds(j * part_rows, part_rows)
        return remote(
            part_ref.at[rows], lat_in.at[me], lat_send.at[j], lat_recv.at[me], tensor=j * stride
        )

    def page_rows(j):
        return pl.ds(pl.multiple_of(j * part_rows, part_rows), part_rows)

    def page_piece(j, z, k):
        ref = pages.at[seq_me, page_rows(j)]
        return remote(ref, ref, pz_send.at[k], pz_recv.at[j], tensor=z)

    def page_core(x, j, k):
        ref = pages.at[2 * x + core, page_rows(k)]
        return remote(ref, ref, pg_send.at[j, k], pg_core.at[x, k], seq=partner)

    def page_from_core(x, k):
        ref = pages.at[2 * x + 1 - core, page_rows(k)]
        return remote(ref, ref, pg_send.at[0, k], pg_core.at[x, k], seq=partner)

    def page_x(j, k):
        ref = pages.at[seq_me, page_rows(k)]
        return remote(
            ref, ref, pg_send.at[n_x + j - 1, k], pg_x.at[x_me, k], seq=2 * other_x(j) + core
        )

    def page_from_x(j, k):
        x = other_x(j)
        ref = pages.at[2 * x + core, page_rows(k)]
        return remote(ref, ref, pg_send.at[n_x + j - 1, k], pg_x.at[x, k], seq=2 * x + core)

    def outgoing(c):
        return (count - 1) * n_seq + (c % RING) * n_x

    def away(c, which):
        if which == 0:
            src, dst = att.at[pl.ds(outgoing(c), n_x)], away_in
        else:
            src, dst = sq_away_out.at[c % RING], sq_away_in
        return remote(
            src, dst.at[c], qc_send.at[which, c % RING], qc_recv.at[which, c], seq=partner
        )

    def aside(c, j, which):
        src, dst = (x_out, x_in) if which == 0 else (sq_x_out, sq_x_in)
        return remote(
            src.at[c % RING, j - 1], dst.at[c, j - 1], qx_send.at[which, c % RING, j - 1],
            qx_recv.at[which, c, j - 1], seq=2 * other_x(j) + core,
        )

    def to_core(c, x, j):
        ref = att.at[c * n_seq + core * n_x + x]
        return remote(ref, ref, block_sem.at[c, j], core_sem.at[c, x], seq=partner)

    def from_core(c, x):
        ref = att.at[c * n_seq + (1 - core) * n_x + x]
        return remote(ref, ref, block_sem.at[c, 0], core_sem.at[c, x], seq=partner)

    def to_x(c, j):
        ref = att.at[c * n_seq + own]
        return remote(
            ref, ref, block_sem.at[c, n_x + j - 1], side_sem.at[c, x_me], seq=2 * other_x(j) + core
        )

    def from_x(c, j):
        x = other_x(j)
        ref = att.at[c * n_seq + core * n_x + x]
        return remote(ref, ref, block_sem.at[c, n_x + j - 1], side_sem.at[c, x], seq=2 * x + core)

    def rows_of(p):
        return pl.ds(pl.multiple_of(p * size, size), size)

    def piece(p):
        return part.at[p // cut, pl.ds(pl.multiple_of((p % cut) * size, size), size)]

    def landing(p):
        return (wq if tight else came).at[rows_of(p)]

    def inward(p):
        return remote(piece(p), landing(p), inward_sem.at[p], in_sem.at[p], tensor=inner)

    def across(p):
        return remote(
            piece(p), out_ref.at[rows_of(p)], inward_sem.at[p], back_sem.at[p], tensor=inner
        )

    def outward(p):
        ref = out_ref.at[rows_of(p)]
        return remote(ref, ref, outward_sem.at[p], back_sem.at[p], tensor=outer)

    def half_rows(which):
        return pl.ds(pl.multiple_of(which * rows_half, rows_half), rows_half)

    def strip(x):
        return pl.ds(pl.multiple_of(x * sub, sub), sub)

    def project(c):
        slot = c % RING
        load_text(c).wait()

        @pl.when(c >= RING)
        def _():
            for which in (0, 1):
                away(c - RING, which).wait_send()

        rows = jnp.concatenate(
            [text[half_rows(2 * c + 1 - core)], text[half_rows(2 * c + core)]], axis=0
        ).astype(F32)
        squares = rows * rows
        groups = [slice(g * 128, (g + 1) * 128) for g in range(feat // 128)]
        sums = squares[:, groups[0]]
        for group in groups[1:]:
            sums = sums + squares[:, group]
        sq_away_out[slot] = sums[:rows_half]
        sq_half[c] = sums[rows_half:]
        gain = gain_ref[...].astype(F32)
        scaled = jnp.concatenate(
            [(rows[:, group] * gain[g : g + 1]).astype(BF) for g, group in enumerate(groups)], axis=1
        )
        tile = math.gcd(qwidth, 1024)
        for t in range(0, qwidth, tile):
            value = jnp.dot(scaled, wq[:, t : t + tile], preferred_element_type=F32)
            for x in range(n_x):
                att[outgoing(c) + x, :, t : t + tile] = value[x * sub : (x + 1) * sub].astype(BF)
            own_half[c % keep, :, t : t + tile] = value[rows_half:]
        for which in (0, 1):
            away(c, which).start()

    def scatter(c):
        slot = c % RING
        for which in (0, 1):
            away(c, which).wait_recv()

        @pl.when(c >= RING)
        def _():
            for j in range(1, n_x):
                for which in (0, 1):
                    aside(c - RING, j, which).wait_send()

        for j in range(1, n_x):
            rows = strip(other_x(j))
            x_out[slot, j - 1] = (own_half[c % keep, rows] + away_in[c, other_x(j)].astype(F32)).astype(BF)
            sq_x_out[slot, j - 1] = sq_half[c, rows] + sq_away_in[c, rows]
            for which in (0, 1):
                aside(c, j, which).start()

    def finish(c):
        rows = strip(x_me)
        value = own_half[c % keep, rows] + away_in[c, x_me].astype(F32)
        square = sq_half[c, rows] + sq_away_in[c, rows]
        for j in range(1, n_x):
            for which in (0, 1):
                aside(c, j, which).wait_recv()
            value = value + x_in[c, j - 1].astype(F32)
            square = square + sq_x_in[c, j - 1]
        mean = jnp.sum(square, axis=1, keepdims=True) / (feat * n_seq)
        query[...] = (value * lax.rsqrt(mean + 1e-05)).astype(BF)

    def attend(c):
        line = jnp.broadcast_to(img_ref[pl.ds(c, 1)], (sub, rows_all)).astype(F32)
        lane = lax.broadcasted_iota(jnp.int32, (sub, rows_all), 1)
        token = lax.broadcasted_iota(jnp.int32, (sub, rows_all), 0) + own * sub
        img = jnp.sum(jnp.where(lane == token, line, 0.0), axis=1, keepdims=True)
        slot = lax.broadcasted_iota(jnp.int32, (1, n_seq * lat_rows), 1)
        owner = lax.div(slot, jnp.int32(lat_count)).astype(F32)
        allowed = img == owner
        visible = (img >= 0).astype(F32)
        cuts = [slice(h * HEAD, (h + 1) * HEAD) for h in range(heads)]
        logits = [
            lax.dot_general(
                query[:, cut], keys[:, cut], (((1,), (1,)), ((), ())), preferred_element_type=F32
            )
            for cut in cuts
        ]
        logits = [jnp.where(allowed, value * scale, -1e30) for value in logits]
        peaks = [jnp.max(value, axis=1, keepdims=True) for value in logits]
        probs = [jnp.exp(value - peak).astype(BF) for value, peak in zip(logits, peaks)]
        weights = [jnp.sum(p.astype(F32), axis=1, keepdims=True) for p in probs]
        mixed = [
            jnp.dot(p, values[:, cut], preferred_element_type=F32) for p, cut in zip(probs, cuts)
        ]
        for value, weight, cut in zip(mixed, weights, cuts):
            att[c * n_seq + own, :, cut] = (value / weight * visible).astype(BF)
        for j in range(1, n_x):
            to_x(c, j).start()
        to_core(c, x_me, 0).start()

    def product(c, t):
        tile = width // TILES
        cols = slice(t * tile, (t + 1) * tile)
        rows = att[pl.ds(c * n_seq, n_seq)].reshape(rows_all, qwidth)
        value = jnp.dot(rows, wo[:qwidth, cols], preferred_element_type=F32)
        mixed_rows[:, cols] = value.astype(BF)

    def replace(c):
        for j in range(n_x):
            to_core(c, x_me, j).wait_send()
        for j in range(1, n_x):
            to_x(c, j).wait_send()
        for b in range(n_seq):
            part[c * n_seq + b] = mixed_rows[b * sub : (b + 1) * sub]

    def gather(p):
        @pl.when(depth > 0)
        def _():
            inward(p).wait_recv()
            piece(p)[...] = (piece(p)[...].astype(F32) + landing(p)[...].astype(F32)).astype(BF)

        @pl.when(depth < half - 1)
        def _():
            if tight:
                @pl.when(p == 0)
                def _():
                    pl.semaphore_wait(free_sem, 1)

            inward(p).start()

        @pl.when(depth == half - 1)
        def _():
            across(p).start()

    def spread(p):
        outward(p).wait_recv()

        @pl.when(depth == half - 1)
        def _():
            rows = rows_of(p)
            out_ref[rows] = (piece(p)[...].astype(F32) + out_ref[rows].astype(F32)).astype(BF)

        @pl.when(depth > 0)
        def _():
            outward(p).start()

    def sum_latents():
        @pl.when(me % stride == 0)
        def _():
            j = me // stride
            rows = page_rows(j)
            value = part_sum[rows]
            for k in range(1, n):
                z = other_z(k)
                remote(
                    part_ref.at[rows], lat_in.at[z], lat_send.at[0], lat_recv.at[z], tensor=z
                ).wait_recv()
                value = value + lat_in[z].astype(F32)
            pages[seq_me, rows] = (lat_own[...].astype(F32) + value).astype(BF)
            for k in range(1, n):
                page_piece(j, other_z(k), k - 1).start()

    def share_page():
        for k in range(owners):
            j = (me // stride + k) % owners

            @pl.when(me != j * stride)
            def _(j=j):
                page_piece(j, j * stride, 0).wait_recv()

            for i in range(1, n_x):
                page_x(i, j).start()
            page_core(x_me, 0, j).start()
        page_ref[...] = pages[seq_me]

    def pass_pages():
        for k in range(owners):
            j = (me // stride + k) % owners
            for i in range(1, n_x):
                page_from_x(i, j).wait_recv()
                page_core(other_x(i), i, j).start()

    def keys_values():
        load_k.wait()
        load_v.wait()
        for x in range(n_x):
            for k in range(owners):
                page_from_core(x, k).wait_recv()
        rows = pages[...].reshape(n_seq * lat_rows, vis)
        tile = math.gcd(qwidth, 1024)
        for base, target in ((vis, values), (0, keys)):
            for t in range(0, qwidth, tile):
                target[:, t : t + tile] = jnp.dot(
                    rows, wkv[base : base + vis, t : t + tile], preferred_element_type=F32
                ).astype(BF)
        if shared:
            load_o.start()

    for load in (*load_res, load_own):
        load.start()

    barrier = pltpu.get_barrier_semaphore()

    def greet(**where):
        pl.semaphore_signal(barrier, inc=1, device_id=where, device_id_type=pl.DeviceIdType.MESH)

    greet(seq=partner)
    for j in range(1, n_x):
        greet(seq=2 * other_x(j) + core)
    for j in range(1, n):
        greet(tensor=other_z(j))
    for load in (load_res[6], load_res[7], load_own):
        load.wait()
    load_text(0).start()
    load_q.start()
    for c in range(1, min(SOON, count)):
        load_text(c).start()
    resample()
    pl.semaphore_wait(barrier, 1 + (n_x - 1) + (n - 1))

    for j in range(owners):
        @pl.when(me != j * stride)
        def _(j=j):
            lat_piece(j).start()

    load_q.wait()
    for c in range(SOON, count):
        load_text(c).start()
    load_k.start()
    load_v.start()
    if not shared:
        load_o.start()

    @pl.loop(0, count + LEAD + 2)
    def _(s):
        pl.when(s == SUM_STEP)(sum_latents)
        pl.when(s == PAGE_STEP)(share_page)
        pl.when(s == PASS_STEP)(pass_pages)

        @pl.when(s < min(count, LEAD))
        def _():
            project(s)

        @pl.when(jnp.logical_and(s >= EARLY, s < EARLY + min(AHEAD, count)))
        def _():
            scatter(s - EARLY)

        c = s - LEAD - 1
        ready = jnp.logical_and(c >= 0, c < count)

        def pieces(low, high):
            @pl.when(c >= 1)
            def _():
                @pl.loop(low, high)
                def _(b):
                    p = (c - 1) * per + b
                    gather(p)

                    @pl.when(
                        jnp.logical_and(depth > 0, jnp.logical_and(p < per, p >= lag - SHORT))
                    )
                    def _():
                        spread(p - lag + SHORT)

                    @pl.when(
                        jnp.logical_and(depth > 0, jnp.logical_and(p >= per + SHORT, p >= lag))
                    )
                    def _():
                        spread(p - lag)

        pieces(0, per // 2)

        @pl.when(ready)
        def _():
            for j in range(1, n_x):
                from_x(c, j).wait_recv()
                to_core(c, other_x(j), j).start()

        pl.when(s == LEAD)(keys_values)

        @pl.when(jnp.logical_and(s >= LEAD, s < LEAD + count))
        def _():
            finish(s - LEAD)
            attend(s - LEAD)

        @pl.when(jnp.logical_and(s >= LATER + AHEAD, s < LATER + count))
        def _():
            scatter(s - LATER)

        @pl.when(s == LEAD)
        def _():
            @pl.loop(LEAD, count)
            def _(later):
                project(later)

            for last in range(max(count - RING, 0), count):
                for which in (0, 1):
                    away(last, which).wait_send()
            if tight:
                @pl.when(depth > 0)
                def _():
                    pl.semaphore_signal(
                        free_sem, inc=1, device_id={"tensor": outer},
                        device_id_type=pl.DeviceIdType.MESH,
                    )

        pl.when(c == 0)(load_o.wait)
        pieces(per // 2, 3 * per // 4)

        @pl.when(ready)
        def _():
            for x in range(n_x):
                from_core(c, x).wait_recv()
            product(c, 0)

        pieces(3 * per // 4, per)

        @pl.when(ready)
        def _():
            for t in range(1, TILES):
                product(c, t)
            replace(c)

    @pl.loop(0, total)
    def _(p):
        @pl.when(jnp.logical_or(depth == 0, p >= total - lag))
        def _():
            spread(p)

    @pl.loop(0, total)
    def _(p):
        across(p).wait_send()

        @pl.when(depth > 0)
        def _():
            outward(p).wait_send()

    for c in range(max(count - RING, 0), count):
        for which in (0, 1):
            for j in range(1, n_x):
                aside(c, j, which).wait_send()
    for k in range(owners):
        for j in range(n_x):
            page_core(x_me, j, k).wait_send()
        for j in range(1, n_x):
            page_x(j, k).wait_send()
    for j in range(owners):
        @pl.when(me != j * stride)
        def _(j=j):
            lat_piece(j).wait_send()

    @pl.when(me % stride == 0)
    def _():
        for k in range(1, n):
            page_piece(me // stride, other_z(k), k - 1).wait_send()


def flow(patches, latents, gain, text_image, wq_res, wk_res, wv_res, wo_res, text, wq, wk, wv, wo, n_x, n):
    n_seq = 2 * n_x
    tokens, feat = text.shape
    qwidth, width = wo.shape
    vis = patches.shape[1]
    lat_rows = patches.shape[0] // PATCH_IMG * latents.shape[0]
    sub = math.gcd(tokens // n_seq, SUB)
    count = tokens // (n_seq * sub)
    blocks = count * n_seq
    pieces = blocks * (CUT if sub % (16 * CUT) == 0 else 1)
    owners = math.gcd(n, lat_rows // 16)
    shared = qwidth == width and qwidth <= 2 * vis
    tight = qwidth == width and tokens <= feat
    roomy = shared and vis <= qwidth and qwidth + n_seq * (sub + lat_rows) + sub <= 2 * vis
    dma = pltpu.SemaphoreType.DMA
    vmem, anywhere = pl.BlockSpec(memory_space=pltpu.VMEM), pl.BlockSpec(memory_space=pltpu.HBM)
    others = max(n_x - 1, 1)
    half_rows = n_x * sub
    gain, img = gain.reshape(-1, 128), text_image.reshape(count, -1)
    res = wo_res.shape[0]
    windowed = (
        res % 128 == 0 and 3 * res <= qwidth and vis <= qwidth and res + latents.shape[0] <= vis
    )
    stay = [
        pltpu.with_memory_space_constraint(value, pltpu.HBM)
        for value in (
            patches, latents, gain, img, wq_res, wk_res, wv_res, wo_res, text, wq, wk, wv, wo
        )
    ]
    scratch = [
        ((lat_rows, vis), F32),
        ((lat_rows, vis), BF),
        ((16, 128) if windowed else latents.shape, BF),
        ((lat_rows // owners, vis), BF),
        (gain.shape, BF),
        (img.shape, jnp.int32),
        (patches.shape, BF),
        *(
            ((16, 128) if windowed else value.shape, BF)
            for value in (wq_res, wk_res, wv_res, wo_res)
        ),
        ((feat, qwidth), BF),
        ((2 * vis, qwidth), BF),
        ((16, 128) if shared else (qwidth, width), BF),
        ((min(count, LEAD + 2), half_rows, qwidth), F32),
        ((count, n_x, sub, qwidth), BF),
        ((RING, others, sub, qwidth), BF),
        ((count, others, sub, qwidth), BF),
        ((count, half_rows, 128), F32),
        ((RING, half_rows, 128), F32),
        ((count, half_rows, 128), F32),
        ((RING, others, sub, 128), F32),
        ((count, others, sub, 128), F32),
        ((16, 128) if roomy else (sub, qwidth), BF),
        ((16, 128) if roomy else (n_seq * lat_rows, qwidth), BF),
        ((n_seq * lat_rows, qwidth), BF),
        ((n_seq, lat_rows, vis), BF),
        ((n, lat_rows // owners, vis), BF),
        ((blocks, sub, qwidth), BF),
        ((1, 16, 128) if shared else (blocks, sub, width), BF),
        ((16, 128) if tight else (tokens, width), BF),
        ((16, 128) if roomy else (n_seq * sub, width), BF),
    ]
    return pl.pallas_call(
        functools.partial(flow_kernel, (n_x, n, count, sub, owners, shared, tight, roomy, windowed)),
        out_shape=(
            jax.ShapeDtypeStruct((tokens, width), BF),
            jax.ShapeDtypeStruct((tokens, feat), BF),
            jax.ShapeDtypeStruct((lat_rows, vis), BF),
        ),
        in_specs=[anywhere] * len(stay),
        out_specs=(vmem, vmem, vmem),
        scratch_shapes=[pltpu.VMEM(shape, kind) for shape, kind in scratch]
        + [
            dma((4,)),
            dma((9,)),
            dma((count,)),
            dma((2, RING)),
            dma((2, count)),
            dma((2, RING, others)),
            dma((2, count, others)),
            dma((owners,)),
            dma((n,)),
            dma((n,)),
            dma((owners,)),
            dma((2 * n_x, owners)),
            dma((n_x, owners)),
            dma((n_x, owners)),
            dma((count, n_x)),
            dma((count, n_x)),
            dma((count, 2 * n_x - 1)),
        ]
        + [dma((pieces,))] * 4
        + [pltpu.SemaphoreType.REGULAR],
        compiler_params=pltpu.CompilerParams(
            collective_id=0, has_side_effects=True, vmem_limit_bytes=41984 << 10
        ),
        name="flow",
    )(*stay)


def close_kernel(rows, slots, text_ref, gate_ref, branch_ref, page_ref, out_ref, page_out, buf, sem, page_sem):
    steps = text_ref.shape[0] // rows
    gate = jnp.tanh(gate_ref[...])
    page = pltpu.make_async_copy(page_ref, page_out, page_sem)

    def put(i):
        return pltpu.make_async_copy(
            buf.at[i % slots], out_ref.at[pl.ds(i * rows, rows)], sem.at[i % slots]
        )

    page.start()

    @pl.loop(0, steps)
    def _(i):
        @pl.when(i >= slots)
        def _():
            put(i - slots).wait()

        at = pl.ds(pl.multiple_of(i * rows, rows), rows)
        buf[i % slots] = text_ref[at].astype(F32) + gate * branch_ref[at].astype(F32)
        put(i).start()

    @pl.loop(max(steps - slots, 0), steps)
    def _(i):
        put(i).wait()

    page.wait()


def close(text, gate, branch, page):
    tokens, width = text.shape
    rows = math.gcd(tokens, 64)
    slots = 8
    whole, anywhere = pl.BlockSpec(memory_space=pltpu.VMEM), pl.BlockSpec(memory_space=pl.ANY)
    return pl.pallas_call(
        functools.partial(close_kernel, rows, slots),
        out_shape=(
            jax.ShapeDtypeStruct((tokens, width), F32),
            jax.ShapeDtypeStruct(page.shape, page.dtype),
        ),
        in_specs=[whole] * 4,
        out_specs=(anywhere, anywhere),
        scratch_shapes=[
            pltpu.VMEM((slots, rows, width), F32),
            pltpu.SemaphoreType.DMA((slots,)),
            pltpu.SemaphoreType.DMA,
        ],
        compiler_params=pltpu.CompilerParams(vmem_limit_bytes=8 << 20),
        name="close",
    )(text, gate, branch, page)


def make_shards(n_seq, n_tensor):
    n_x = n_seq // 2

    def shards(
        patches,
        latents,
        wq_res,
        wk_res,
        wv_res,
        wo_res,
        text,
        norm_gain,
        wq_x,
        wk_x,
        wv_x,
        wo_x,
        gate_x,
        text_image,
    ):
        branch, text, page_latents = flow(
            patches, latents, norm_gain, text_image, wq_res, wk_res, wv_res, wo_res, text,
            wq_x, wk_x, wv_x, wo_x, n_x, n_tensor,
        )
        return close(text, gate_x[None, :], branch, page_latents)

    return shards


def solution(mesh):
    in_specs = (
        P(("groups", "seq"), None),
        P(),
        P(None, "tensor"),
        P(None, "tensor"),
        P(None, "tensor"),
        P("tensor", None),
        P("groups", "seq"),
        P("seq"),
        P("seq", "tensor"),
        P(None, "tensor"),
        P(None, "tensor"),
        P("tensor", "seq"),
        P("seq"),
        P("groups"),
    )
    out_specs = (P("groups", "seq"), P(("groups", "seq"), None))
    body = make_shards(mesh.shape["seq"], mesh.shape["tensor"])
    return jax.shard_map(body, mesh=mesh, in_specs=in_specs, out_specs=out_specs, check_vma=False)
```

```python
import functools
import math

import jax
import jax.numpy as jnp
from jax import lax
from jax.experimental import pallas as pl
from jax.experimental.pallas import tpu as pltpu
from jax.sharding import PartitionSpec as P

HEAD = 128
RES_HEAD = 96
PATCH_IMG = 257
SUB = 32
CUT = 2
TILES = 2
SOON = 2
LAG, SHORT = 4, 2
LEAD = 10
SUM_STEP, PAGE_STEP, PASS_STEP = 3, 6, 9
EARLY, AHEAD, LATER = 1, 2, 9
RING = 2
BF = jnp.bfloat16
F32 = jnp.float32


def flow_kernel(dims, *refs):
    n_x, n, count, sub, owners, shared, tight, roomy, windowed = dims
    (patch_hbm, lat_hbm, gain_hbm, img_hbm, wqr_hbm, wkr_hbm, wvr_hbm, wor_hbm,
     text_ref, wq_ref, wk_ref, wv_ref, wo_ref) = refs[:13]
    out_ref, text, page_ref = refs[13:16]
    (part_sum, part_ref, lat_ref, lat_own, gain_ref, img_ref, patch_ref, wqr, wkr, wvr, wor, wq, wkv, late, own_half, away_in, x_out, x_in, sq_half, sq_away_out, sq_away_in,
     sq_x_out, sq_x_in, query, keys, values, pages, lat_in, att, second, came, mixed_rows) = refs[16:48]
    (load_sem, res_sem, text_sem, qc_send, qc_recv, qx_send, qx_recv, lat_send, lat_recv, pz_send, pz_recv,
     pg_send, pg_x, pg_core, side_sem, core_sem, block_sem, in_sem, back_sem, inward_sem,
     outward_sem, free_sem) = refs[48:]
    n_seq, half = 2 * n_x, n // 2
    cut = CUT if sub % (16 * CUT) == 0 else 1
    size, per = sub // cut, n_seq * cut
    total = count * per
    keep = own_half.shape[0]
    rows_all, rows_half = n_seq * sub, n_x * sub
    seq_me, me = lax.axis_index("seq"), lax.axis_index("tensor")
    core, x_me = seq_me % 2, seq_me // 2
    partner = 2 * x_me + 1 - core
    own = core * n_x + x_me
    side = me // half
    depth = me * (1 - side) + (n - 1 - me) * side
    inner, outer = me + 1 - 2 * side, me - 1 + 2 * side
    lag = LAG + 5 * (half - 1 - depth)
    feat, qwidth = wq.shape
    width = wo_ref.shape[1]
    heads = qwidth // HEAD
    scale = 1.0 / math.sqrt(HEAD)
    lat_rows = part_ref.shape[0]
    vis = part_ref.shape[1]
    part_rows = lat_rows // owners
    stride = n // owners
    wo = wkv if shared else late
    if roomy:
        keys = wkv.at[pl.ds(qwidth, n_seq * lat_rows)]
        mixed_rows = wkv.at[pl.ds(qwidth + n_seq * lat_rows, rows_all)]
        query = wkv.at[pl.ds(qwidth + n_seq * lat_rows + rows_all, sub)]
    part = att if shared else second

    def remote(src, dst, sent, got, **where):
        return pltpu.make_async_remote_copy(
            src_ref=src, dst_ref=dst, send_sem=sent, recv_sem=got,
            device_id=where, device_id_type=pl.DeviceIdType.MESH,
        )

    def other_x(j):
        return (x_me + j) % n_x

    def other_z(j):
        return (me + j) % n

    def load_text(c):
        rows = pl.ds(pl.multiple_of(c * rows_all, rows_all), rows_all)
        return pltpu.make_async_copy(text_ref.at[rows], text.at[rows], text_sem.at[c])

    load_q = pltpu.make_async_copy(wq_ref, wq, load_sem.at[0])
    load_k = pltpu.make_async_copy(wk_ref, wkv.at[pl.ds(0, vis)], load_sem.at[1])
    load_v = pltpu.make_async_copy(wv_ref, wkv.at[pl.ds(vis, vis)], load_sem.at[2])
    load_o = pltpu.make_async_copy(wo_ref, wo.at[pl.ds(0, qwidth)], load_sem.at[3])

    res = wqr_hbm.shape[1]
    lat_count = lat_hbm.shape[0]
    if windowed:
        wqr, wkr, wvr = (wkv.at[pl.ds(0, vis), pl.ds(k * res, res)] for k in range(3))
        wor = wkv.at[pl.ds(vis, res), pl.ds(0, vis)]
        lat_ref = wkv.at[pl.ds(vis + res, lat_count), pl.ds(0, vis)]
    lat_from = (me // stride * part_rows) % lat_count
    load_own = pltpu.make_async_copy(
        lat_hbm.at[pl.ds(pl.multiple_of(lat_from, part_rows), part_rows)], lat_own, res_sem.at[8]
    )
    load_res = [
        pltpu.make_async_copy(src, dst, res_sem.at[k])
        for k, (src, dst) in enumerate((
            (lat_hbm, lat_ref), (wqr_hbm, wqr), (patch_hbm, patch_ref), (wkr_hbm, wkr),
            (wvr_hbm, wvr), (wor_hbm, wor), (gain_hbm, gain_ref), (img_hbm, img_ref),
        ))
    ]

    def resample():
        images = patch_ref.shape[0] // PATCH_IMG
        whole = PATCH_IMG // 128 * 128
        count_res = res // RES_HEAD
        inv_res = 1.0 / math.sqrt(RES_HEAD)
        load_res[0].wait()
        load_res[1].wait()
        lat_q = jnp.dot(lat_ref[...], wqr[...], preferred_element_type=F32).astype(BF).astype(F32)
        column = lax.broadcasted_iota(jnp.int32, (1, res), 1)
        inside = [
            jnp.logical_and(column >= h * RES_HEAD, column < (h + 1) * RES_HEAD)
            for h in range(count_res)
        ]
        stacked = jnp.concatenate([jnp.where(m, lat_q, 0.0) for m in inside], axis=0)
        packed = stacked.astype(BF)
        for k in range(2, 6):
            load_res[k].wait()
        for i in range(images):
            base = i * PATCH_IMG
            spans = [(base, whole)] + [(base + r, 1) for r in range(whole, PATCH_IMG)]

            def both(w):
                return [
                    jnp.dot(patch_ref[at : at + rows], w[...], preferred_element_type=F32).astype(BF)
                    for at, rows in spans
                ]

            page_k, page_v = both(wkr), both(wvr)
            scores = lax.dot_general(
                packed, page_k[0], (((1,), (1,)), ((), ())), preferred_element_type=F32
            ) * inv_res
            extra = [
                jnp.sum(stacked * row.astype(F32), axis=1, keepdims=True) * inv_res
                for row in page_k[1:]
            ]
            summit = jnp.max(scores, axis=1, keepdims=True)
            for more in extra:
                summit = jnp.maximum(summit, more)
            weights = jnp.exp(scores - summit).astype(BF)
            sums = jnp.sum(weights.astype(F32), axis=1, keepdims=True)
            blended = jnp.dot(weights, page_v[0], preferred_element_type=F32)
            for more, row in zip(extra, page_v[1:]):
                weight = jnp.exp(more - summit).astype(BF).astype(F32)
                sums = sums + weight
                blended = blended + weight * row.astype(F32)
            blended = blended / sums
            pooled = jnp.zeros((lat_count, res), F32)
            for h, m in enumerate(inside):
                pooled = jnp.where(m, blended[h * lat_count : (h + 1) * lat_count], pooled)
            value = jnp.dot(pooled.astype(BF), wor[...], preferred_element_type=F32)
            part_sum[i * lat_count : (i + 1) * lat_count] = value
            part_ref[i * lat_count : (i + 1) * lat_count] = value.astype(BF)

    def lat_piece(j):
        rows = pl.ds(j * part_rows, part_rows)
        return remote(
            part_ref.at[rows], lat_in.at[me], lat_send.at[j], lat_recv.at[me], tensor=j * stride
        )

    def page_rows(j):
        return pl.ds(pl.multiple_of(j * part_rows, part_rows), part_rows)

    def page_piece(j, z, k):
        ref = pages.at[seq_me, page_rows(j)]
        return remote(ref, ref, pz_send.at[k], pz_recv.at[j], tensor=z)

    def page_core(x, j, k):
        ref = pages.at[2 * x + core, page_rows(k)]
        return remote(ref, ref, pg_send.at[j, k], pg_core.at[x, k], seq=partner)

    def page_from_core(x, k):
        ref = pages.at[2 * x + 1 - core, page_rows(k)]
        return remote(ref, ref, pg_send.at[0, k], pg_core.at[x, k], seq=partner)

    def page_x(j, k):
        ref = pages.at[seq_me, page_rows(k)]
        return remote(
            ref, ref, pg_send.at[n_x + j - 1, k], pg_x.at[x_me, k], seq=2 * other_x(j) + core
        )

    def page_from_x(j, k):
        x = other_x(j)
        ref = pages.at[2 * x + core, page_rows(k)]
        return remote(ref, ref, pg_send.at[n_x + j - 1, k], pg_x.at[x, k], seq=2 * x + core)

    def outgoing(c):
        return (count - 1) * n_seq + (c % RING) * n_x

    def away(c, which):
        if which == 0:
            src, dst = att.at[pl.ds(outgoing(c), n_x)], away_in
        else:
            src, dst = sq_away_out.at[c % RING], sq_away_in
        return remote(
            src, dst.at[c], qc_send.at[which, c % RING], qc_recv.at[which, c], seq=partner
        )

    def aside(c, j, which):
        src, dst = (x_out, x_in) if which == 0 else (sq_x_out, sq_x_in)
        return remote(
            src.at[c % RING, j - 1], dst.at[c, j - 1], qx_send.at[which, c % RING, j - 1],
            qx_recv.at[which, c, j - 1], seq=2 * other_x(j) + core,
        )

    def to_core(c, x, j):
        ref = att.at[c * n_seq + core * n_x + x]
        return remote(ref, ref, block_sem.at[c, j], core_sem.at[c, x], seq=partner)

    def from_core(c, x):
        ref = att.at[c * n_seq + (1 - core) * n_x + x]
        return remote(ref, ref, block_sem.at[c, 0], core_sem.at[c, x], seq=partner)

    def to_x(c, j):
        ref = att.at[c * n_seq + own]
        return remote(
            ref, ref, block_sem.at[c, n_x + j - 1], side_sem.at[c, x_me], seq=2 * other_x(j) + core
        )

    def from_x(c, j):
        x = other_x(j)
        ref = att.at[c * n_seq + core * n_x + x]
        return remote(ref, ref, block_sem.at[c, n_x + j - 1], side_sem.at[c, x], seq=2 * x + core)

    def block_at(c, q):
        return c * n_seq + (q % 2) * n_x + (x_me + q // 2) % n_x

    def spot(p):
        block = p // cut
        return block_at(block // n_seq, block % n_seq)

    def rows_of(p):
        return pl.ds(pl.multiple_of(spot(p) * sub + (p % cut) * size, size), size)

    def piece(p):
        return part.at[spot(p), pl.ds(pl.multiple_of((p % cut) * size, size), size)]

    def landing(p):
        return (wq if tight else came).at[rows_of(p)]

    def inward(p):
        return remote(piece(p), landing(p), inward_sem.at[p], in_sem.at[p], tensor=inner)

    def across(p):
        return remote(
            piece(p), out_ref.at[rows_of(p)], inward_sem.at[p], back_sem.at[p], tensor=inner
        )

    def outward(p):
        ref = out_ref.at[rows_of(p)]
        return remote(ref, ref, outward_sem.at[p], back_sem.at[p], tensor=outer)

    def half_rows(which):
        return pl.ds(pl.multiple_of(which * rows_half, rows_half), rows_half)

    def strip(x):
        return pl.ds(pl.multiple_of(x * sub, sub), sub)

    def project(c):
        slot = c % RING
        load_text(c).wait()

        @pl.when(c >= RING)
        def _():
            for which in (0, 1):
                away(c - RING, which).wait_send()

        rows = jnp.concatenate(
            [text[half_rows(2 * c + 1 - core)], text[half_rows(2 * c + core)]], axis=0
        ).astype(F32)
        squares = rows * rows
        groups = [slice(g * 128, (g + 1) * 128) for g in range(feat // 128)]
        sums = squares[:, groups[0]]
        for group in groups[1:]:
            sums = sums + squares[:, group]
        sq_away_out[slot] = sums[:rows_half]
        sq_half[c] = sums[rows_half:]
        gain = gain_ref[...].astype(F32)
        scaled = jnp.concatenate(
            [(rows[:, group] * gain[g : g + 1]).astype(BF) for g, group in enumerate(groups)], axis=1
        )
        tile = math.gcd(qwidth, 1024)
        for t in range(0, qwidth, tile):
            value = jnp.dot(scaled, wq[:, t : t + tile], preferred_element_type=F32)
            for x in range(n_x):
                att[outgoing(c) + x, :, t : t + tile] = value[x * sub : (x + 1) * sub].astype(BF)
            own_half[c % keep, :, t : t + tile] = value[rows_half:]
        for which in (0, 1):
            away(c, which).start()

    def scatter(c):
        slot = c % RING
        for which in (0, 1):
            away(c, which).wait_recv()

        @pl.when(c >= RING)
        def _():
            for j in range(1, n_x):
                for which in (0, 1):
                    aside(c - RING, j, which).wait_send()

        for j in range(1, n_x):
            rows = strip(other_x(j))
            x_out[slot, j - 1] = (own_half[c % keep, rows] + away_in[c, other_x(j)].astype(F32)).astype(BF)
            sq_x_out[slot, j - 1] = sq_half[c, rows] + sq_away_in[c, rows]
            for which in (0, 1):
                aside(c, j, which).start()

    def finish(c):
        rows = strip(x_me)
        value = own_half[c % keep, rows] + away_in[c, x_me].astype(F32)
        square = sq_half[c, rows] + sq_away_in[c, rows]
        for j in range(1, n_x):
            for which in (0, 1):
                aside(c, j, which).wait_recv()
            value = value + x_in[c, j - 1].astype(F32)
            square = square + sq_x_in[c, j - 1]
        mean = jnp.sum(square, axis=1, keepdims=True) / (feat * n_seq)
        query[...] = (value * lax.rsqrt(mean + 1e-05)).astype(BF)

    def attend(c):
        line = jnp.broadcast_to(img_ref[pl.ds(c, 1)], (sub, rows_all)).astype(F32)
        lane = lax.broadcasted_iota(jnp.int32, (sub, rows_all), 1)
        token = lax.broadcasted_iota(jnp.int32, (sub, rows_all), 0) + own * sub
        img = jnp.sum(jnp.where(lane == token, line, 0.0), axis=1, keepdims=True)
        slot = lax.broadcasted_iota(jnp.int32, (1, n_seq * lat_rows), 1)
        owner = lax.div(slot, jnp.int32(lat_count)).astype(F32)
        allowed = img == owner
        visible = (img >= 0).astype(F32)
        cuts = [slice(h * HEAD, (h + 1) * HEAD) for h in range(heads)]
        logits = [
            lax.dot_general(
                query[:, cut], keys[:, cut], (((1,), (1,)), ((), ())), preferred_element_type=F32
            )
            for cut in cuts
        ]
        logits = [jnp.where(allowed, value * scale, -1e30) for value in logits]
        peaks = [jnp.max(value, axis=1, keepdims=True) for value in logits]
        probs = [jnp.exp(value - peak).astype(BF) for value, peak in zip(logits, peaks)]
        weights = [jnp.sum(p.astype(F32), axis=1, keepdims=True) for p in probs]
        mixed = [
            jnp.dot(p, values[:, cut], preferred_element_type=F32) for p, cut in zip(probs, cuts)
        ]
        for value, weight, cut in zip(mixed, weights, cuts):
            att[c * n_seq + own, :, cut] = (value / weight * visible).astype(BF)
        for j in range(1, n_x):
            to_x(c, j).start()
        to_core(c, x_me, 0).start()

    def product(c, t, low, high):
        tile = width // TILES
        cols = slice(t * tile, (t + 1) * tile)
        rows = jnp.concatenate([att[block_at(c, q)] for q in range(low, high)], axis=0)
        value = jnp.dot(rows, wo[:qwidth, cols], preferred_element_type=F32)
        mixed_rows[low * sub : high * sub, cols] = value.astype(BF)

    def replace(c, low, high):
        if low == 0:
            to_core(c, x_me, 0).wait_send()
            for j in range(1, n_x):
                to_x(c, j).wait_send()
        if high == n_seq:
            for j in range(1, n_x):
                to_core(c, x_me, j).wait_send()
        for q in range(low, high):
            part[block_at(c, q)] = mixed_rows[q * sub : (q + 1) * sub]

    def gather(p):
        @pl.when(depth > 0)
        def _():
            inward(p).wait_recv()
            piece(p)[...] = (piece(p)[...].astype(F32) + landing(p)[...].astype(F32)).astype(BF)

        @pl.when(depth < half - 1)
        def _():
            if tight:
                @pl.when(p == 0)
                def _():
                    pl.semaphore_wait(free_sem, 1)

            inward(p).start()

        @pl.when(depth == half - 1)
        def _():
            across(p).start()

    def spread(p):
        outward(p).wait_recv()

        @pl.when(depth == half - 1)
        def _():
            rows = rows_of(p)
            out_ref[rows] = (piece(p)[...].astype(F32) + out_ref[rows].astype(F32)).astype(BF)

        @pl.when(depth > 0)
        def _():
            outward(p).start()

    def sum_latents():
        @pl.when(me % stride == 0)
        def _():
            j = me // stride
            rows = page_rows(j)
            value = part_sum[rows]
            for k in range(1, n):
                z = other_z(k)
                remote(
                    part_ref.at[rows], lat_in.at[z], lat_send.at[0], lat_recv.at[z], tensor=z
                ).wait_recv()
                value = value + lat_in[z].astype(F32)
            pages[seq_me, rows] = (lat_own[...].astype(F32) + value).astype(BF)
            for k in range(1, n):
                page_piece(j, other_z(k), k - 1).start()

    def share_page():
        for k in range(owners):
            j = (me // stride + k) % owners

            @pl.when(me != j * stride)
            def _(j=j):
                page_piece(j, j * stride, 0).wait_recv()

            for i in range(1, n_x):
                page_x(i, j).start()
            page_core(x_me, 0, j).start()
        page_ref[...] = pages[seq_me]

    def pass_pages():
        for k in range(owners):
            j = (me // stride + k) % owners
            for i in range(1, n_x):
                page_from_x(i, j).wait_recv()
                page_core(other_x(i), i, j).start()

    def keys_values():
        load_k.wait()
        load_v.wait()
        for x in range(n_x):
            for k in range(owners):
                page_from_core(x, k).wait_recv()
        rows = pages[...].reshape(n_seq * lat_rows, vis)
        tile = math.gcd(qwidth, 1024)
        for base, target in ((vis, values), (0, keys)):
            for t in range(0, qwidth, tile):
                target[:, t : t + tile] = jnp.dot(
                    rows, wkv[base : base + vis, t : t + tile], preferred_element_type=F32
                ).astype(BF)
        if shared:
            load_o.start()

    for load in (*load_res, load_own):
        load.start()

    barrier = pltpu.get_barrier_semaphore()

    def greet(**where):
        pl.semaphore_signal(barrier, inc=1, device_id=where, device_id_type=pl.DeviceIdType.MESH)

    greet(seq=partner)
    for j in range(1, n_x):
        greet(seq=2 * other_x(j) + core)
    for j in range(1, n):
        greet(tensor=other_z(j))
    for load in (load_res[6], load_res[7], load_own):
        load.wait()
    load_text(0).start()
    load_q.start()
    for c in range(1, min(SOON, count)):
        load_text(c).start()
    resample()
    pl.semaphore_wait(barrier, 1 + (n_x - 1) + (n - 1))

    for j in range(owners):
        @pl.when(me != j * stride)
        def _(j=j):
            lat_piece(j).start()

    load_q.wait()
    for c in range(SOON, count):
        load_text(c).start()
    load_k.start()
    load_v.start()
    if not shared:
        load_o.start()

    @pl.loop(0, count + LEAD + 2)
    def _(s):
        pl.when(s == SUM_STEP)(sum_latents)
        pl.when(s == PAGE_STEP)(share_page)
        pl.when(s == PASS_STEP)(pass_pages)

        @pl.when(s < min(count, LEAD))
        def _():
            project(s)

        @pl.when(jnp.logical_and(s >= EARLY, s < EARLY + min(AHEAD, count)))
        def _():
            scatter(s - EARLY)

        c = s - LEAD - 1
        ready = jnp.logical_and(c >= 0, c < count)

        def pieces(low, high):
            @pl.when(c >= 1)
            def _():
                @pl.loop(low, high)
                def _(b):
                    p = (c - 1) * per + b

                    @pl.when(jnp.logical_or(depth > 0, p >= 2 * cut))
                    def _():
                        gather(p)

                    @pl.when(
                        jnp.logical_and(depth > 0, jnp.logical_and(p < per, p >= lag - SHORT))
                    )
                    def _():
                        spread(p - lag + SHORT)

                    @pl.when(
                        jnp.logical_and(depth > 0, jnp.logical_and(p >= per + SHORT, p >= lag))
                    )
                    def _():
                        spread(p - lag)

        pieces(0, per // 2)

        @pl.when(ready)
        def _():
            for j in range(1, n_x):
                from_x(c, j).wait_recv()
                to_core(c, other_x(j), j).start()

        pl.when(s == LEAD)(keys_values)

        @pl.when(jnp.logical_and(s >= LEAD, s < LEAD + count))
        def _():
            finish(s - LEAD)
            attend(s - LEAD)

        @pl.when(jnp.logical_and(s >= LATER + AHEAD, s < LATER + count))
        def _():
            scatter(s - LATER)

        @pl.when(s == LEAD)
        def _():
            @pl.loop(LEAD, count)
            def _(later):
                project(later)

            for last in range(max(count - RING, 0), count):
                for which in (0, 1):
                    away(last, which).wait_send()
            if tight:
                @pl.when(depth > 0)
                def _():
                    pl.semaphore_signal(
                        free_sem, inc=1, device_id={"tensor": outer},
                        device_id_type=pl.DeviceIdType.MESH,
                    )

        @pl.when(s == LEAD)
        def _():
            load_o.wait()
            from_core(0, x_me).wait_recv()
            for t in range(TILES):
                product(0, t, 0, 2)
            replace(0, 0, 2)

            @pl.when(depth == 0)
            def _():
                @pl.loop(0, 2 * cut)
                def _(p):
                    gather(p)

        pieces(per // 2, 3 * per // 4)

        @pl.when(ready)
        def _():
            for j in range(1, n_x):
                from_core(c, other_x(j)).wait_recv()

            @pl.when(c >= 1)
            def _():
                from_core(c, x_me).wait_recv()
                product(c, 0, 0, n_seq)

            @pl.when(c == 0)
            def _():
                product(0, 0, 2, n_seq)

        pieces(3 * per // 4, per)

        @pl.when(ready)
        def _():
            @pl.when(c >= 1)
            def _():
                for t in range(1, TILES):
                    product(c, t, 0, n_seq)
                replace(c, 0, n_seq)

            @pl.when(c == 0)
            def _():
                for t in range(1, TILES):
                    product(0, t, 2, n_seq)
                replace(0, 2, n_seq)

    @pl.loop(0, total)
    def _(p):
        @pl.when(jnp.logical_or(depth == 0, p >= total - lag))
        def _():
            spread(p)

    @pl.loop(0, total)
    def _(p):
        across(p).wait_send()

        @pl.when(depth > 0)
        def _():
            outward(p).wait_send()

    for c in range(max(count - RING, 0), count):
        for which in (0, 1):
            for j in range(1, n_x):
                aside(c, j, which).wait_send()
    for k in range(owners):
        for j in range(n_x):
            page_core(x_me, j, k).wait_send()
        for j in range(1, n_x):
            page_x(j, k).wait_send()
    for j in range(owners):
        @pl.when(me != j * stride)
        def _(j=j):
            lat_piece(j).wait_send()

    @pl.when(me % stride == 0)
    def _():
        for k in range(1, n):
            page_piece(me // stride, other_z(k), k - 1).wait_send()


def flow(patches, latents, gain, text_image, wq_res, wk_res, wv_res, wo_res, text, wq, wk, wv, wo, n_x, n):
    n_seq = 2 * n_x
    tokens, feat = text.shape
    qwidth, width = wo.shape
    vis = patches.shape[1]
    lat_rows = patches.shape[0] // PATCH_IMG * latents.shape[0]
    sub = math.gcd(tokens // n_seq, SUB)
    count = tokens // (n_seq * sub)
    blocks = count * n_seq
    pieces = blocks * (CUT if sub % (16 * CUT) == 0 else 1)
    owners = math.gcd(n, lat_rows // 16)
    shared = qwidth == width and qwidth <= 2 * vis
    tight = qwidth == width and tokens <= feat
    roomy = shared and vis <= qwidth and qwidth + n_seq * (sub + lat_rows) + sub <= 2 * vis
    dma = pltpu.SemaphoreType.DMA
    vmem, anywhere = pl.BlockSpec(memory_space=pltpu.VMEM), pl.BlockSpec(memory_space=pltpu.HBM)
    others = max(n_x - 1, 1)
    half_rows = n_x * sub
    gain, img = gain.reshape(-1, 128), text_image.reshape(count, -1)
    res = wo_res.shape[0]
    windowed = (
        res % 128 == 0 and 3 * res <= qwidth and vis <= qwidth and res + latents.shape[0] <= vis
    )
    stay = [
        pltpu.with_memory_space_constraint(value, pltpu.HBM)
        for value in (
            patches, latents, gain, img, wq_res, wk_res, wv_res, wo_res, text, wq, wk, wv, wo
        )
    ]
    scratch = [
        ((lat_rows, vis), F32),
        ((lat_rows, vis), BF),
        ((16, 128) if windowed else latents.shape, BF),
        ((lat_rows // owners, vis), BF),
        (gain.shape, BF),
        (img.shape, jnp.int32),
        (patches.shape, BF),
        *(
            ((16, 128) if windowed else value.shape, BF)
            for value in (wq_res, wk_res, wv_res, wo_res)
        ),
        ((feat, qwidth), BF),
        ((2 * vis, qwidth), BF),
        ((16, 128) if shared else (qwidth, width), BF),
        ((min(count, LEAD + 2), half_rows, qwidth), F32),
        ((count, n_x, sub, qwidth), BF),
        ((RING, others, sub, qwidth), BF),
        ((count, others, sub, qwidth), BF),
        ((count, half_rows, 128), F32),
        ((RING, half_rows, 128), F32),
        ((count, half_rows, 128), F32),
        ((RING, others, sub, 128), F32),
        ((count, others, sub, 128), F32),
        ((16, 128) if roomy else (sub, qwidth), BF),
        ((16, 128) if roomy else (n_seq * lat_rows, qwidth), BF),
        ((n_seq * lat_rows, qwidth), BF),
        ((n_seq, lat_rows, vis), BF),
        ((n, lat_rows // owners, vis), BF),
        ((blocks, sub, qwidth), BF),
        ((1, 16, 128) if shared else (blocks, sub, width), BF),
        ((16, 128) if tight else (tokens, width), BF),
        ((16, 128) if roomy else (n_seq * sub, width), BF),
    ]
    return pl.pallas_call(
        functools.partial(flow_kernel, (n_x, n, count, sub, owners, shared, tight, roomy, windowed)),
        out_shape=(
            jax.ShapeDtypeStruct((tokens, width), BF),
            jax.ShapeDtypeStruct((tokens, feat), BF),
            jax.ShapeDtypeStruct((lat_rows, vis), BF),
        ),
        in_specs=[anywhere] * len(stay),
        out_specs=(vmem, vmem, vmem),
        scratch_shapes=[pltpu.VMEM(shape, kind) for shape, kind in scratch]
        + [
            dma((4,)),
            dma((9,)),
            dma((count,)),
            dma((2, RING)),
            dma((2, count)),
            dma((2, RING, others)),
            dma((2, count, others)),
            dma((owners,)),
            dma((n,)),
            dma((n,)),
            dma((owners,)),
            dma((2 * n_x, owners)),
            dma((n_x, owners)),
            dma((n_x, owners)),
            dma((count, n_x)),
            dma((count, n_x)),
            dma((count, 2 * n_x - 1)),
        ]
        + [dma((pieces,))] * 4
        + [pltpu.SemaphoreType.REGULAR],
        compiler_params=pltpu.CompilerParams(
            collective_id=0, has_side_effects=True, vmem_limit_bytes=41984 << 10
        ),
        name="flow",
    )(*stay)


def close_kernel(rows, slots, text_ref, gate_ref, branch_ref, page_ref, out_ref, page_out, buf, sem, page_sem):
    steps = text_ref.shape[0] // rows
    gate = jnp.tanh(gate_ref[...])
    page = pltpu.make_async_copy(page_ref, page_out, page_sem)

    def put(i):
        return pltpu.make_async_copy(
            buf.at[i % slots], out_ref.at[pl.ds(i * rows, rows)], sem.at[i % slots]
        )

    page.start()

    @pl.loop(0, steps)
    def _(i):
        @pl.when(i >= slots)
        def _():
            put(i - slots).wait()

        at = pl.ds(pl.multiple_of(i * rows, rows), rows)
        buf[i % slots] = text_ref[at].astype(F32) + gate * branch_ref[at].astype(F32)
        put(i).start()

    @pl.loop(max(steps - slots, 0), steps)
    def _(i):
        put(i).wait()

    page.wait()


def close(text, gate, branch, page):
    tokens, width = text.shape
    rows = math.gcd(tokens, 64)
    slots = 8
    whole, anywhere = pl.BlockSpec(memory_space=pltpu.VMEM), pl.BlockSpec(memory_space=pl.ANY)
    return pl.pallas_call(
        functools.partial(close_kernel, rows, slots),
        out_shape=(
            jax.ShapeDtypeStruct((tokens, width), F32),
            jax.ShapeDtypeStruct(page.shape, page.dtype),
        ),
        in_specs=[whole] * 4,
        out_specs=(anywhere, anywhere),
        scratch_shapes=[
            pltpu.VMEM((slots, rows, width), F32),
            pltpu.SemaphoreType.DMA((slots,)),
            pltpu.SemaphoreType.DMA,
        ],
        compiler_params=pltpu.CompilerParams(vmem_limit_bytes=8 << 20),
        name="close",
    )(text, gate, branch, page)


def make_shards(n_seq, n_tensor):
    n_x = n_seq // 2

    def shards(
        patches,
        latents,
        wq_res,
        wk_res,
        wv_res,
        wo_res,
        text,
        norm_gain,
        wq_x,
        wk_x,
        wv_x,
        wo_x,
        gate_x,
        text_image,
    ):
        branch, text, page_latents = flow(
            patches, latents, norm_gain, text_image, wq_res, wk_res, wv_res, wo_res, text,
            wq_x, wk_x, wv_x, wo_x, n_x, n_tensor,
        )
        return close(text, gate_x[None, :], branch, page_latents)

    return shards


def solution(mesh):
    in_specs = (
        P(("groups", "seq"), None),
        P(),
        P(None, "tensor"),
        P(None, "tensor"),
        P(None, "tensor"),
        P("tensor", None),
        P("groups", "seq"),
        P("seq"),
        P("seq", "tensor"),
        P(None, "tensor"),
        P(None, "tensor"),
        P("tensor", "seq"),
        P("seq"),
        P("groups"),
    )
    out_specs = (P("groups", "seq"), P(("groups", "seq"), None))
    body = make_shards(mesh.shape["seq"], mesh.shape["tensor"])
    return jax.shard_map(body, mesh=mesh, in_specs=in_specs, out_specs=out_specs, check_vma=False)
```

```python
import functools
import math

import jax
import jax.numpy as jnp
from jax import lax
from jax.experimental import pallas as pl
from jax.experimental.pallas import tpu as pltpu
from jax.sharding import PartitionSpec as P

HEAD = 128
RES_HEAD = 96
PATCH_IMG = 257
SUB = 32
CUT = 2
TILES = 2
SOON = 2
LAG, SHORT = 4, 2
LEAD = 9
SUM_STEP, PAGE_STEP, PASS_STEP = 3, 6, 8
EARLY, AHEAD, LATER = 1, 2, 8
RING = 2
BF = jnp.bfloat16
F32 = jnp.float32


def flow_kernel(dims, *refs):
    n_x, n, count, sub, owners, shared, tight, roomy, windowed = dims
    (patch_hbm, lat_hbm, gain_hbm, img_hbm, wqr_hbm, wkr_hbm, wvr_hbm, wor_hbm,
     text_ref, wq_ref, wk_ref, wv_ref, wo_ref) = refs[:13]
    out_ref, text, page_ref = refs[13:16]
    (part_sum, part_ref, lat_ref, lat_own, gain_ref, img_ref, patch_ref, wqr, wkr, wvr, wor, wq, wkv, late, own_half, away_in, x_out, x_in, sq_half, sq_away_out, sq_away_in,
     sq_x_out, sq_x_in, query, keys, values, pages, lat_in, att, second, came, mixed_rows) = refs[16:48]
    (load_sem, res_sem, text_sem, qc_send, qc_recv, qx_send, qx_recv, lat_send, lat_recv, pz_send, pz_recv,
     pg_send, pg_x, pg_core, side_sem, core_sem, block_sem, in_sem, back_sem, inward_sem,
     outward_sem, free_sem) = refs[48:]
    n_seq, half = 2 * n_x, n // 2
    cut = CUT if sub % (16 * CUT) == 0 else 1
    size, per = sub // cut, n_seq * cut
    total = count * per
    keep = own_half.shape[0]
    rows_all, rows_half = n_seq * sub, n_x * sub
    seq_me, me = lax.axis_index("seq"), lax.axis_index("tensor")
    core, x_me = seq_me % 2, seq_me // 2
    partner = 2 * x_me + 1 - core
    own = core * n_x + x_me
    side = me // half
    depth = me * (1 - side) + (n - 1 - me) * side
    inner, outer = me + 1 - 2 * side, me - 1 + 2 * side
    lag = LAG + 5 * (half - 1 - depth)
    feat, qwidth = wq.shape
    width = wo_ref.shape[1]
    heads = qwidth // HEAD
    scale = 1.0 / math.sqrt(HEAD)
    lat_rows = part_ref.shape[0]
    vis = part_ref.shape[1]
    part_rows = lat_rows // owners
    stride = n // owners
    wo = wkv if shared else late
    if roomy:
        keys = wkv.at[pl.ds(qwidth, n_seq * lat_rows)]
        mixed_rows = wkv.at[pl.ds(qwidth + n_seq * lat_rows, rows_all)]
        query = wkv.at[pl.ds(qwidth + n_seq * lat_rows + rows_all, sub)]
    part = att if shared else second

    def remote(src, dst, sent, got, **where):
        return pltpu.make_async_remote_copy(
            src_ref=src, dst_ref=dst, send_sem=sent, recv_sem=got,
            device_id=where, device_id_type=pl.DeviceIdType.MESH,
        )

    def other_x(j):
        return (x_me + j) % n_x

    def other_z(j):
        return (me + j) % n

    def load_text(c):
        rows = pl.ds(pl.multiple_of(c * rows_all, rows_all), rows_all)
        return pltpu.make_async_copy(text_ref.at[rows], text.at[rows], text_sem.at[c])

    load_q = pltpu.make_async_copy(wq_ref, wq, load_sem.at[0])
    load_k = pltpu.make_async_copy(wk_ref, wkv.at[pl.ds(0, vis)], load_sem.at[1])
    load_v = pltpu.make_async_copy(wv_ref, wkv.at[pl.ds(vis, vis)], load_sem.at[2])
    load_o = pltpu.make_async_copy(wo_ref, wo.at[pl.ds(0, qwidth)], load_sem.at[3])

    res = wqr_hbm.shape[1]
    lat_count = lat_hbm.shape[0]
    if windowed:
        wqr, wkr, wvr = (wkv.at[pl.ds(0, vis), pl.ds(k * res, res)] for k in range(3))
        wor = wkv.at[pl.ds(vis, res), pl.ds(0, vis)]
        lat_ref = wkv.at[pl.ds(vis + res, lat_count), pl.ds(0, vis)]
    lat_from = (me // stride * part_rows) % lat_count
    load_own = pltpu.make_async_copy(
        lat_hbm.at[pl.ds(pl.multiple_of(lat_from, part_rows), part_rows)], lat_own, res_sem.at[8]
    )
    load_res = [
        pltpu.make_async_copy(src, dst, res_sem.at[k])
        for k, (src, dst) in enumerate((
            (lat_hbm, lat_ref), (wqr_hbm, wqr), (patch_hbm, patch_ref), (wkr_hbm, wkr),
            (wvr_hbm, wvr), (wor_hbm, wor), (gain_hbm, gain_ref), (img_hbm, img_ref),
        ))
    ]

    def resample():
        images = patch_ref.shape[0] // PATCH_IMG
        whole = PATCH_IMG // 128 * 128
        count_res = res // RES_HEAD
        inv_res = 1.0 / math.sqrt(RES_HEAD)
        load_res[0].wait()
        load_res[1].wait()
        lat_q = jnp.dot(lat_ref[...], wqr[...], preferred_element_type=F32).astype(BF).astype(F32)
        column = lax.broadcasted_iota(jnp.int32, (1, res), 1)
        inside = [
            jnp.logical_and(column >= h * RES_HEAD, column < (h + 1) * RES_HEAD)
            for h in range(count_res)
        ]
        stacked = jnp.concatenate([jnp.where(m, lat_q, 0.0) for m in inside], axis=0)
        packed = stacked.astype(BF)
        for k in range(2, 6):
            load_res[k].wait()
        for i in range(images):
            base = i * PATCH_IMG
            spans = [(base, whole)] + [(base + r, 1) for r in range(whole, PATCH_IMG)]

            def both(w):
                return [
                    jnp.dot(patch_ref[at : at + rows], w[...], preferred_element_type=F32).astype(BF)
                    for at, rows in spans
                ]

            page_k, page_v = both(wkr), both(wvr)
            scores = lax.dot_general(
                packed, page_k[0], (((1,), (1,)), ((), ())), preferred_element_type=F32
            ) * inv_res
            extra = [
                jnp.sum(stacked * row.astype(F32), axis=1, keepdims=True) * inv_res
                for row in page_k[1:]
            ]
            summit = jnp.max(scores, axis=1, keepdims=True)
            for more in extra:
                summit = jnp.maximum(summit, more)
            weights = jnp.exp(scores - summit).astype(BF)
            sums = jnp.sum(weights.astype(F32), axis=1, keepdims=True)
            blended = jnp.dot(weights, page_v[0], preferred_element_type=F32)
            for more, row in zip(extra, page_v[1:]):
                weight = jnp.exp(more - summit).astype(BF).astype(F32)
                sums = sums + weight
                blended = blended + weight * row.astype(F32)
            blended = blended / sums
            pooled = jnp.zeros((lat_count, res), F32)
            for h, m in enumerate(inside):
                pooled = jnp.where(m, blended[h * lat_count : (h + 1) * lat_count], pooled)
            value = jnp.dot(pooled.astype(BF), wor[...], preferred_element_type=F32)
            part_sum[i * lat_count : (i + 1) * lat_count] = value
            part_ref[i * lat_count : (i + 1) * lat_count] = value.astype(BF)

    def lat_piece(j):
        rows = pl.ds(j * part_rows, part_rows)
        return remote(
            part_ref.at[rows], lat_in.at[me], lat_send.at[j], lat_recv.at[me], tensor=j * stride
        )

    def page_rows(j):
        return pl.ds(pl.multiple_of(j * part_rows, part_rows), part_rows)

    def page_piece(j, z, k):
        ref = pages.at[seq_me, page_rows(j)]
        return remote(ref, ref, pz_send.at[k], pz_recv.at[j], tensor=z)

    def page_core(x, j, k):
        ref = pages.at[2 * x + core, page_rows(k)]
        return remote(ref, ref, pg_send.at[j, k], pg_core.at[x, k], seq=partner)

    def page_from_core(x, k):
        ref = pages.at[2 * x + 1 - core, page_rows(k)]
        return remote(ref, ref, pg_send.at[0, k], pg_core.at[x, k], seq=partner)

    def page_x(j, k):
        ref = pages.at[seq_me, page_rows(k)]
        return remote(
            ref, ref, pg_send.at[n_x + j - 1, k], pg_x.at[x_me, k], seq=2 * other_x(j) + core
        )

    def page_from_x(j, k):
        x = other_x(j)
        ref = pages.at[2 * x + core, page_rows(k)]
        return remote(ref, ref, pg_send.at[n_x + j - 1, k], pg_x.at[x, k], seq=2 * x + core)

    def outgoing(c):
        return (count - 1) * n_seq + (c % RING) * n_x

    def away(c, which):
        if which == 0:
            src, dst = att.at[pl.ds(outgoing(c), n_x)], away_in
        else:
            src, dst = sq_away_out.at[c % RING], sq_away_in
        return remote(
            src, dst.at[c], qc_send.at[which, c % RING], qc_recv.at[which, c], seq=partner
        )

    def aside(c, j, which):
        src, dst = (x_out, x_in) if which == 0 else (sq_x_out, sq_x_in)
        return remote(
            src.at[c % RING, j - 1], dst.at[c, j - 1], qx_send.at[which, c % RING, j - 1],
            qx_recv.at[which, c, j - 1], seq=2 * other_x(j) + core,
        )

    def to_core(c, x, j):
        ref = att.at[c * n_seq + core * n_x + x]
        return remote(ref, ref, block_sem.at[c, j], core_sem.at[c, x], seq=partner)

    def from_core(c, x):
        ref = att.at[c * n_seq + (1 - core) * n_x + x]
        return remote(ref, ref, block_sem.at[c, 0], core_sem.at[c, x], seq=partner)

    def to_x(c, j):
        ref = att.at[c * n_seq + own]
        return remote(
            ref, ref, block_sem.at[c, n_x + j - 1], side_sem.at[c, x_me], seq=2 * other_x(j) + core
        )

    def from_x(c, j):
        x = other_x(j)
        ref = att.at[c * n_seq + core * n_x + x]
        return remote(ref, ref, block_sem.at[c, n_x + j - 1], side_sem.at[c, x], seq=2 * x + core)

    def rows_of(p):
        return pl.ds(pl.multiple_of(p * size, size), size)

    def piece(p):
        return part.at[p // cut, pl.ds(pl.multiple_of((p % cut) * size, size), size)]

    def landing(p):
        return (wq if tight else came).at[rows_of(p)]

    def inward(p):
        return remote(piece(p), landing(p), inward_sem.at[p], in_sem.at[p], tensor=inner)

    def across(p):
        return remote(
            piece(p), out_ref.at[rows_of(p)], inward_sem.at[p], back_sem.at[p], tensor=inner
        )

    def outward(p):
        ref = out_ref.at[rows_of(p)]
        return remote(ref, ref, outward_sem.at[p], back_sem.at[p], tensor=outer)

    def half_rows(which):
        return pl.ds(pl.multiple_of(which * rows_half, rows_half), rows_half)

    def strip(x):
        return pl.ds(pl.multiple_of(x * sub, sub), sub)

    def project(c):
        slot = c % RING
        load_text(c).wait()

        @pl.when(c >= RING)
        def _():
            for which in (0, 1):
                away(c - RING, which).wait_send()

        rows = jnp.concatenate(
            [text[half_rows(2 * c + 1 - core)], text[half_rows(2 * c + core)]], axis=0
        ).astype(F32)
        squares = rows * rows
        groups = [slice(g * 128, (g + 1) * 128) for g in range(feat // 128)]
        sums = squares[:, groups[0]]
        for group in groups[1:]:
            sums = sums + squares[:, group]
        sq_away_out[slot] = sums[:rows_half]
        sq_half[c] = sums[rows_half:]
        gain = gain_ref[...].astype(F32)
        scaled = jnp.concatenate(
            [(rows[:, group] * gain[g : g + 1]).astype(BF) for g, group in enumerate(groups)], axis=1
        )
        tile = math.gcd(qwidth, 1024)
        for t in range(0, qwidth, tile):
            value = jnp.dot(scaled, wq[:, t : t + tile], preferred_element_type=F32)
            for x in range(n_x):
                att[outgoing(c) + x, :, t : t + tile] = value[x * sub : (x + 1) * sub].astype(BF)
            own_half[c % keep, :, t : t + tile] = value[rows_half:]
        for which in (0, 1):
            away(c, which).start()

    def scatter(c):
        slot = c % RING
        for which in (0, 1):
            away(c, which).wait_recv()

        @pl.when(c >= RING)
        def _():
            for j in range(1, n_x):
                for which in (0, 1):
                    aside(c - RING, j, which).wait_send()

        for j in range(1, n_x):
            rows = strip(other_x(j))
            x_out[slot, j - 1] = (own_half[c % keep, rows] + away_in[c, other_x(j)].astype(F32)).astype(BF)
            sq_x_out[slot, j - 1] = sq_half[c, rows] + sq_away_in[c, rows]
            for which in (0, 1):
                aside(c, j, which).start()

    def finish(c):
        rows = strip(x_me)
        value = own_half[c % keep, rows] + away_in[c, x_me].astype(F32)
        square = sq_half[c, rows] + sq_away_in[c, rows]
        for j in range(1, n_x):
            for which in (0, 1):
                aside(c, j, which).wait_recv()
            value = value + x_in[c, j - 1].astype(F32)
            square = square + sq_x_in[c, j - 1]
        mean = jnp.sum(square, axis=1, keepdims=True) / (feat * n_seq)
        query[...] = (value * lax.rsqrt(mean + 1e-05)).astype(BF)

    def attend(c):
        line = jnp.broadcast_to(img_ref[pl.ds(c, 1)], (sub, rows_all)).astype(F32)
        lane = lax.broadcasted_iota(jnp.int32, (sub, rows_all), 1)
        token = lax.broadcasted_iota(jnp.int32, (sub, rows_all), 0) + own * sub
        img = jnp.sum(jnp.where(lane == token, line, 0.0), axis=1, keepdims=True)
        slot = lax.broadcasted_iota(jnp.int32, (1, n_seq * lat_rows), 1)
        owner = lax.div(slot, jnp.int32(lat_count)).astype(F32)
        allowed = img == owner
        visible = (img >= 0).astype(F32)
        cuts = [slice(h * HEAD, (h + 1) * HEAD) for h in range(heads)]
        logits = [
            lax.dot_general(
                query[:, cut], keys[:, cut], (((1,), (1,)), ((), ())), preferred_element_type=F32
            )
            for cut in cuts
        ]
        logits = [jnp.where(allowed, value * scale, -1e30) for value in logits]
        peaks = [jnp.max(value, axis=1, keepdims=True) for value in logits]
        probs = [jnp.exp(value - peak).astype(BF) for value, peak in zip(logits, peaks)]
        weights = [jnp.sum(p.astype(F32), axis=1, keepdims=True) for p in probs]
        mixed = [
            jnp.dot(p, values[:, cut], preferred_element_type=F32) for p, cut in zip(probs, cuts)
        ]
        for value, weight, cut in zip(mixed, weights, cuts):
            att[c * n_seq + own, :, cut] = (value / weight * visible).astype(BF)
        for j in range(1, n_x):
            to_x(c, j).start()
        to_core(c, x_me, 0).start()

    def product(c, t):
        tile = width // TILES
        cols = slice(t * tile, (t + 1) * tile)
        rows = att[pl.ds(c * n_seq, n_seq)].reshape(rows_all, qwidth)
        value = jnp.dot(rows, wo[:qwidth, cols], preferred_element_type=F32)
        mixed_rows[:, cols] = value.astype(BF)

    def replace(c):
        for j in range(n_x):
            to_core(c, x_me, j).wait_send()
        for j in range(1, n_x):
            to_x(c, j).wait_send()
        for b in range(n_seq):
            part[c * n_seq + b] = mixed_rows[b * sub : (b + 1) * sub]

    def gather(p):
        @pl.when(depth > 0)
        def _():
            inward(p).wait_recv()
            piece(p)[...] = (piece(p)[...].astype(F32) + landing(p)[...].astype(F32)).astype(BF)

        @pl.when(depth < half - 1)
        def _():
            if tight:
                @pl.when(p == 0)
                def _():
                    pl.semaphore_wait(free_sem, 1)

            inward(p).start()

        @pl.when(depth == half - 1)
        def _():
            across(p).start()

    def spread(p):
        outward(p).wait_recv()

        @pl.when(depth == half - 1)
        def _():
            rows = rows_of(p)
            out_ref[rows] = (piece(p)[...].astype(F32) + out_ref[rows].astype(F32)).astype(BF)

        @pl.when(depth > 0)
        def _():
            outward(p).start()

    def sum_latents():
        @pl.when(me % stride == 0)
        def _():
            j = me // stride
            rows = page_rows(j)
            value = part_sum[rows]
            for k in range(1, n):
                z = other_z(k)
                remote(
                    part_ref.at[rows], lat_in.at[z], lat_send.at[0], lat_recv.at[z], tensor=z
                ).wait_recv()
                value = value + lat_in[z].astype(F32)
            pages[seq_me, rows] = (lat_own[...].astype(F32) + value).astype(BF)
            for k in range(1, n):
                page_piece(j, other_z(k), k - 1).start()

    def share_page():
        for k in range(owners):
            j = (me // stride + k) % owners

            @pl.when(me != j * stride)
            def _(j=j):
                page_piece(j, j * stride, 0).wait_recv()

            for i in range(1, n_x):
                page_x(i, j).start()
            page_core(x_me, 0, j).start()
        page_ref[...] = pages[seq_me]

    def pass_pages():
        for k in range(owners):
            j = (me // stride + k) % owners
            for i in range(1, n_x):
                page_from_x(i, j).wait_recv()
                page_core(other_x(i), i, j).start()

    def keys_values():
        load_k.wait()
        load_v.wait()
        for x in range(n_x):
            for k in range(owners):
                page_from_core(x, k).wait_recv()
        rows = pages[...].reshape(n_seq * lat_rows, vis)
        tile = math.gcd(qwidth, 1024)
        for base, target in ((vis, values), (0, keys)):
            for t in range(0, qwidth, tile):
                target[:, t : t + tile] = jnp.dot(
                    rows, wkv[base : base + vis, t : t + tile], preferred_element_type=F32
                ).astype(BF)
        if shared:
            load_o.start()

    for load in (*load_res, load_own):
        load.start()

    barrier = pltpu.get_barrier_semaphore()

    def greet(**where):
        pl.semaphore_signal(barrier, inc=1, device_id=where, device_id_type=pl.DeviceIdType.MESH)

    greet(seq=partner)
    for j in range(1, n_x):
        greet(seq=2 * other_x(j) + core)
    for j in range(1, n):
        greet(tensor=other_z(j))
    for load in (load_res[6], load_res[7], load_own):
        load.wait()
    load_text(0).start()
    load_q.start()
    for c in range(1, min(SOON, count)):
        load_text(c).start()
    resample()
    pl.semaphore_wait(barrier, 1 + (n_x - 1) + (n - 1))

    for j in range(owners):
        @pl.when(me != j * stride)
        def _(j=j):
            lat_piece(j).start()

    load_q.wait()
    for c in range(SOON, count):
        load_text(c).start()
    load_k.start()
    load_v.start()
    if not shared:
        load_o.start()

    @pl.loop(0, count + LEAD + 2)
    def _(s):
        pl.when(s == SUM_STEP)(sum_latents)
        pl.when(s == PAGE_STEP)(share_page)
        pl.when(s == PASS_STEP)(pass_pages)

        @pl.when(s < min(count, LEAD))
        def _():
            project(s)

        @pl.when(jnp.logical_and(s >= EARLY, s < EARLY + min(AHEAD, count)))
        def _():
            scatter(s - EARLY)

        c = s - LEAD - 1
        ready = jnp.logical_and(c >= 0, c < count)

        def pieces(low, high):
            @pl.when(c >= 1)
            def _():
                @pl.loop(low, high)
                def _(b):
                    p = (c - 1) * per + b
                    gather(p)

                    @pl.when(
                        jnp.logical_and(depth > 0, jnp.logical_and(p < per, p >= lag - SHORT))
                    )
                    def _():
                        spread(p - lag + SHORT)

                    @pl.when(
                        jnp.logical_and(depth > 0, jnp.logical_and(p >= per + SHORT, p >= lag))
                    )
                    def _():
                        spread(p - lag)

        pieces(0, per // 2)

        @pl.when(ready)
        def _():
            for j in range(1, n_x):
                from_x(c, j).wait_recv()
                to_core(c, other_x(j), j).start()

        pl.when(s == LEAD)(keys_values)

        @pl.when(jnp.logical_and(s >= LEAD, s < LEAD + count))
        def _():
            finish(s - LEAD)
            attend(s - LEAD)

        @pl.when(jnp.logical_and(s >= LATER + AHEAD, s < LATER + count))
        def _():
            scatter(s - LATER)

        @pl.when(s == LEAD)
        def _():
            @pl.loop(LEAD, count)
            def _(later):
                project(later)

            for last in range(max(count - RING, 0), count):
                for which in (0, 1):
                    away(last, which).wait_send()
            if tight:
                @pl.when(depth > 0)
                def _():
                    pl.semaphore_signal(
                        free_sem, inc=1, device_id={"tensor": outer},
                        device_id_type=pl.DeviceIdType.MESH,
                    )

        pl.when(c == 0)(load_o.wait)
        pieces(per // 2, 3 * per // 4)

        @pl.when(ready)
        def _():
            for x in range(n_x):
                from_core(c, x).wait_recv()
            product(c, 0)

        pieces(3 * per // 4, per)

        @pl.when(ready)
        def _():
            for t in range(1, TILES):
                product(c, t)
            replace(c)

    @pl.loop(0, total)
    def _(p):
        @pl.when(jnp.logical_or(depth == 0, p >= total - lag))
        def _():
            spread(p)

    @pl.loop(0, total)
    def _(p):
        across(p).wait_send()

        @pl.when(depth > 0)
        def _():
            outward(p).wait_send()

    for c in range(max(count - RING, 0), count):
        for which in (0, 1):
            for j in range(1, n_x):
                aside(c, j, which).wait_send()
    for k in range(owners):
        for j in range(n_x):
            page_core(x_me, j, k).wait_send()
        for j in range(1, n_x):
            page_x(j, k).wait_send()
    for j in range(owners):
        @pl.when(me != j * stride)
        def _(j=j):
            lat_piece(j).wait_send()

    @pl.when(me % stride == 0)
    def _():
        for k in range(1, n):
            page_piece(me // stride, other_z(k), k - 1).wait_send()


def flow(patches, latents, gain, text_image, wq_res, wk_res, wv_res, wo_res, text, wq, wk, wv, wo, n_x, n):
    n_seq = 2 * n_x
    tokens, feat = text.shape
    qwidth, width = wo.shape
    vis = patches.shape[1]
    lat_rows = patches.shape[0] // PATCH_IMG * latents.shape[0]
    sub = math.gcd(tokens // n_seq, SUB)
    count = tokens // (n_seq * sub)
    blocks = count * n_seq
    pieces = blocks * (CUT if sub % (16 * CUT) == 0 else 1)
    owners = math.gcd(n, lat_rows // 16)
    shared = qwidth == width and qwidth <= 2 * vis
    tight = qwidth == width and tokens <= feat
    roomy = shared and vis <= qwidth and qwidth + n_seq * (sub + lat_rows) + sub <= 2 * vis
    dma = pltpu.SemaphoreType.DMA
    vmem, anywhere = pl.BlockSpec(memory_space=pltpu.VMEM), pl.BlockSpec(memory_space=pltpu.HBM)
    others = max(n_x - 1, 1)
    half_rows = n_x * sub
    gain, img = gain.reshape(-1, 128), text_image.reshape(count, -1)
    res = wo_res.shape[0]
    windowed = (
        res % 128 == 0 and 3 * res <= qwidth and vis <= qwidth and res + latents.shape[0] <= vis
    )
    stay = [
        pltpu.with_memory_space_constraint(value, pltpu.HBM)
        for value in (
            patches, latents, gain, img, wq_res, wk_res, wv_res, wo_res, text, wq, wk, wv, wo
        )
    ]
    scratch = [
        ((lat_rows, vis), F32),
        ((lat_rows, vis), BF),
        ((16, 128) if windowed else latents.shape, BF),
        ((lat_rows // owners, vis), BF),
        (gain.shape, BF),
        (img.shape, jnp.int32),
        (patches.shape, BF),
        *(
            ((16, 128) if windowed else value.shape, BF)
            for value in (wq_res, wk_res, wv_res, wo_res)
        ),
        ((feat, qwidth), BF),
        ((2 * vis, qwidth), BF),
        ((16, 128) if shared else (qwidth, width), BF),
        ((min(count, LEAD + 2), half_rows, qwidth), F32),
        ((count, n_x, sub, qwidth), BF),
        ((RING, others, sub, qwidth), BF),
        ((count, others, sub, qwidth), BF),
        ((count, half_rows, 128), F32),
        ((RING, half_rows, 128), F32),
        ((count, half_rows, 128), F32),
        ((RING, others, sub, 128), F32),
        ((count, others, sub, 128), F32),
        ((16, 128) if roomy else (sub, qwidth), BF),
        ((16, 128) if roomy else (n_seq * lat_rows, qwidth), BF),
        ((n_seq * lat_rows, qwidth), BF),
        ((n_seq, lat_rows, vis), BF),
        ((n, lat_rows // owners, vis), BF),
        ((blocks, sub, qwidth), BF),
        ((1, 16, 128) if shared else (blocks, sub, width), BF),
        ((16, 128) if tight else (tokens, width), BF),
        ((16, 128) if roomy else (n_seq * sub, width), BF),
    ]
    return pl.pallas_call(
        functools.partial(flow_kernel, (n_x, n, count, sub, owners, shared, tight, roomy, windowed)),
        out_shape=(
            jax.ShapeDtypeStruct((tokens, width), BF),
            jax.ShapeDtypeStruct((tokens, feat), BF),
            jax.ShapeDtypeStruct((lat_rows, vis), BF),
        ),
        in_specs=[anywhere] * len(stay),
        out_specs=(vmem, vmem, vmem),
        scratch_shapes=[pltpu.VMEM(shape, kind) for shape, kind in scratch]
        + [
            dma((4,)),
            dma((9,)),
            dma((count,)),
            dma((2, RING)),
            dma((2, count)),
            dma((2, RING, others)),
            dma((2, count, others)),
            dma((owners,)),
            dma((n,)),
            dma((n,)),
            dma((owners,)),
            dma((2 * n_x, owners)),
            dma((n_x, owners)),
            dma((n_x, owners)),
            dma((count, n_x)),
            dma((count, n_x)),
            dma((count, 2 * n_x - 1)),
        ]
        + [dma((pieces,))] * 4
        + [pltpu.SemaphoreType.REGULAR],
        compiler_params=pltpu.CompilerParams(
            collective_id=0, has_side_effects=True, vmem_limit_bytes=41984 << 10
        ),
        name="flow",
    )(*stay)


def close_kernel(rows, slots, text_ref, gate_ref, branch_ref, page_ref, out_ref, page_out, buf, sem, page_sem):
    steps = text_ref.shape[0] // rows
    gate = jnp.tanh(gate_ref[...])
    page = pltpu.make_async_copy(page_ref, page_out, page_sem)

    def put(i):
        return pltpu.make_async_copy(
            buf.at[i % slots], out_ref.at[pl.ds(i * rows, rows)], sem.at[i % slots]
        )

    page.start()

    @pl.loop(0, steps)
    def _(i):
        @pl.when(i >= slots)
        def _():
            put(i - slots).wait()

        at = pl.ds(pl.multiple_of(i * rows, rows), rows)
        buf[i % slots] = text_ref[at].astype(F32) + gate * branch_ref[at].astype(F32)
        put(i).start()

    @pl.loop(max(steps - slots, 0), steps)
    def _(i):
        put(i).wait()

    page.wait()


def close(text, gate, branch, page):
    tokens, width = text.shape
    rows = math.gcd(tokens, 64)
    slots = 8
    whole, anywhere = pl.BlockSpec(memory_space=pltpu.VMEM), pl.BlockSpec(memory_space=pl.ANY)
    return pl.pallas_call(
        functools.partial(close_kernel, rows, slots),
        out_shape=(
            jax.ShapeDtypeStruct((tokens, width), F32),
            jax.ShapeDtypeStruct(page.shape, page.dtype),
        ),
        in_specs=[whole] * 4,
        out_specs=(anywhere, anywhere),
        scratch_shapes=[
            pltpu.VMEM((slots, rows, width), F32),
            pltpu.SemaphoreType.DMA((slots,)),
            pltpu.SemaphoreType.DMA,
        ],
        compiler_params=pltpu.CompilerParams(vmem_limit_bytes=8 << 20),
        name="close",
    )(text, gate, branch, page)


def make_shards(n_seq, n_tensor):
    n_x = n_seq // 2

    def shards(
        patches,
        latents,
        wq_res,
        wk_res,
        wv_res,
        wo_res,
        text,
        norm_gain,
        wq_x,
        wk_x,
        wv_x,
        wo_x,
        gate_x,
        text_image,
    ):
        branch, text, page_latents = flow(
            patches, latents, norm_gain, text_image, wq_res, wk_res, wv_res, wo_res, text,
            wq_x, wk_x, wv_x, wo_x, n_x, n_tensor,
        )
        return close(text, gate_x[None, :], branch, page_latents)

    return shards


def solution(mesh):
    in_specs = (
        P(("groups", "seq"), None),
        P(),
        P(None, "tensor"),
        P(None, "tensor"),
        P(None, "tensor"),
        P("tensor", None),
        P("groups", "seq"),
        P("seq"),
        P("seq", "tensor"),
        P(None, "tensor"),
        P(None, "tensor"),
        P("tensor", "seq"),
        P("seq"),
        P("groups"),
    )
    out_specs = (P("groups", "seq"), P(("groups", "seq"), None))
    body = make_shards(mesh.shape["seq"], mesh.shape["tensor"])
    return jax.shard_map(body, mesh=mesh, in_specs=in_specs, out_specs=out_specs, check_vma=False)
```
